32 devices in a mesh: seq: 8 (over z, x), head: 4 (over y, core).
Axes of the slice: x: 2, y: 2, z: 4, core: 2. Of those that a mesh axis runs over, the one named last changes fastest.
Arguments:
- token_ids: int32 [8192], P('seq'), may hold values from 0 to 255
- embedding: bfloat16 [256, 1024], replicated, may hold values from -6 to 6
- fine_norm: float32 [1024], replicated, may hold values from 0.1 to 1.9
- fine_query: bfloat16 [1024, 1024], P(None, 'head'), may hold values from -2 to 2
- fine_key: bfloat16 [1024, 1024], P(None, 'head'), may hold values from -2 to 2
- fine_value: bfloat16 [1024, 1024], P(None, 'head'), may hold values from -0.1875 to 0.1875
- fine_output: bfloat16 [1024, 1024], P('head'), may hold values from -0.1875 to 0.1875
- shorten_weight: bfloat16 [4, 1024, 1024], P(None, 'head'), may hold values from -0.09375 to 0.09375
- coarse_norm: float32 [1024], replicated, may hold values from 0.1 to 1.9
- coarse_query: bfloat16 [1024, 1024], P(None, 'head'), may hold values from -2 to 2
- coarse_key: bfloat16 [1024, 1024], P(None, 'head'), may hold values from -2 to 2
- coarse_value: bfloat16 [1024, 1024], P(None, 'head'), may hold values from -0.1875 to 0.1875
- coarse_output: bfloat16 [1024, 1024], P('head'), may hold values from -0.1875 to 0.1875
- ffn_norm: float32 [1024], replicated, may hold values from 0.1 to 1.9
- ffn_up: bfloat16 [1024, 4096], P(None, 'head'), may hold values from -0.1875 to 0.1875
- ffn_down: bfloat16 [4096, 1024], P('head'), may hold values from -0.09375 to 0.09375
- upsample_weight: bfloat16 [1024, 4, 1024], P(None, None, 'head'), may hold values from -0.1875 to 0.1875
Outputs:
- block_output: bfloat16 [8192, 1024], P('seq', 'head')
The draws below stay inside these ranges and needn't reach their ends.
All inputs are finite; a program needn't handle non-finite values.
Results may differ from the reference program's by a relative error of at most 0.0102.
Values may be sent and summed in bfloat16 or wider, within the bound.
A program may use at most 128 MiB of HBM per device.

```python
import math
import jax
import jax.numpy as jnp
from jax import lax

D = 1024
HEADS = 16
HEAD_DIM = 64
FF = 4096
VOCAB = 256
SHORTEN = 4
WINDOW = 1024
TOKENS = 8192
COARSE = 2048


def draw_token_ids(key, part):
    region = 512
    region_count = TOKENS // region
    subkeys = jax.random.split(key, 5)
    centers = jax.random.randint(subkeys[0], (region_count,), 0, 256)
    spreads = jax.random.randint(subkeys[1], (region_count,), 2, 48)
    raw_noise = jax.random.randint(subkeys[2], (TOKENS,), 0, 65536)
    center_rows = jnp.repeat(centers, region)
    spread_rows = jnp.repeat(spreads, region)
    levels = jnp.clip(center_rows + raw_noise % (2 * spread_rows + 1) - spread_rows, 0, 255)
    lowest = jax.random.randint(subkeys[3], (), 0, TOKENS)
    stride = jax.random.randint(subkeys[4], (), 1, TOKENS)
    highest = (lowest + stride) % TOKENS
    levels = levels.at[lowest].set(0).at[highest].set(255)
    return levels.astype(jnp.int32)


def drawn_pair(key, which):
    base_key = jax.random.fold_in(key, which)
    first_key, second_key = jax.random.split(base_key, 2)
    columns = HEADS * HEAD_DIM
    querying = jax.random.normal(first_key, (D, columns), jnp.float32) * D ** (-0.5)
    keying = jax.random.normal(second_key, (D, columns), jnp.float32) * D ** (-0.5)
    return (jnp.clip(querying, -2.0, 2.0), jnp.clip(keying, -2.0, 2.0))


def draw_fine_query(key, part):
    return drawn_pair(key, 11)[0].astype(jnp.bfloat16)


def draw_fine_key(key, part):
    return drawn_pair(key, 11)[1].astype(jnp.bfloat16)


def draw_coarse_query(key, part):
    return drawn_pair(key, 23)[0].astype(jnp.bfloat16)


def draw_coarse_key(key, part):
    return drawn_pair(key, 23)[1].astype(jnp.bfloat16)


def shard_levels(own_key, shape, cuts, smallest, largest):
    def one(axis_at, parts):
        draws = jax.random.uniform(jax.random.fold_in(jax.random.fold_in(own_key, 6), axis_at), (parts,), jnp.float32, smallest / len(cuts), largest / len(cuts))
        return jnp.repeat(jnp.exp(draws), shape[axis_at] // parts).reshape((-1,) + (1,) * (len(shape) - axis_at - 1))

    level = one(*cuts[0])
    for cut in cuts[1:]:
        level = level * one(*cut)
    return level


def gaussian(key, extent, scale, bound, pieces=(), kind=jnp.bfloat16):
    values = scale * jax.random.normal(key, extent, jnp.float32)
    if pieces:
        values = values * shard_levels(key, extent, pieces, -0.22, 0.18)
    return jnp.clip(values, -bound, bound).astype(kind)


def setup_inputs(seed: int = 0) -> dict:
    seeds = jax.random.split(jax.random.key(seed), 18)
    return {
        "token_ids": draw_token_ids(jax.random.fold_in(seeds[17], 71), 0),
        "embedding": gaussian(seeds[1], (VOCAB, D), 1.0, 6.0),
        "fine_norm": jnp.clip(1.0 + 0.18 * jax.random.normal(seeds[2], (D,), jnp.float32), 0.1, 1.9),
        "fine_query": draw_fine_query(jax.random.fold_in(seeds[17], 71), 0),
        "fine_key": draw_fine_key(jax.random.fold_in(seeds[17], 71), 0),
        "fine_value": gaussian(seeds[5], (D, HEADS * HEAD_DIM), D ** -0.5, 0.1875, ((1, 4),)),
        "fine_output": gaussian(seeds[6], (HEADS * HEAD_DIM, D), (HEADS * HEAD_DIM) ** -0.5, 0.1875, ((0, 4),)),
        "shorten_weight": gaussian(seeds[7], (SHORTEN, D, D), (SHORTEN * D) ** -0.5, 0.09375, ((1, 4),)),
        "coarse_norm": jnp.clip(1.0 + 0.18 * jax.random.normal(seeds[8], (D,), jnp.float32), 0.1, 1.9),
        "coarse_query": draw_coarse_query(jax.random.fold_in(seeds[17], 71), 0),
        "coarse_key": draw_coarse_key(jax.random.fold_in(seeds[17], 71), 0),
        "coarse_value": gaussian(seeds[11], (D, HEADS * HEAD_DIM), D ** -0.5, 0.1875, ((1, 4),)),
        "coarse_output": gaussian(seeds[12], (HEADS * HEAD_DIM, D), (HEADS * HEAD_DIM) ** -0.5, 0.1875, ((0, 4),)),
        "ffn_norm": jnp.clip(1.0 + 0.18 * jax.random.normal(seeds[13], (D,), jnp.float32), 0.1, 1.9),
        "ffn_up": gaussian(seeds[14], (D, FF), D ** -0.5, 0.1875, ((1, 4),)),
        "ffn_down": gaussian(seeds[15], (FF, D), FF ** -0.5, 0.09375, ((0, 4),)),
        "upsample_weight": gaussian(seeds[16], (D, SHORTEN, D), D ** -0.5, 0.1875, ((2, 4),)),
    }


epsilon = 1e-06
masked_low = -1e+30

def rms_scale(values, gain):
    data = values.astype(jnp.float32)
    power = lax.optimization_barrier(jnp.mean(data * data, axis=-1, keepdims=True))
    return (data * lax.rsqrt(power + epsilon) * gain).astype(jnp.bfloat16)

def project(left, right):
    return jnp.dot(left, right, preferred_element_type=jnp.float32)

def rotate(values, positions):
    rows = values.shape[0]
    halfway = HEAD_DIM // 2
    pairs = values.reshape(rows, -1, 2, halfway)
    column_index = jnp.arange(halfway, dtype=jnp.int32)
    periods = 2 ** (4 + column_index * 14 // halfway)
    cycle = (positions[:, None] % periods[None, :]).astype(jnp.float32)
    angle = cycle * (2.0 * math.pi / periods.astype(jnp.float32))[None, :]
    cosine = jnp.cos(angle)[:, None, :]
    sine_part = jnp.sin(angle)[:, None, :]
    lower = pairs[:, :, 0]
    upper = pairs[:, :, 1]
    turned = jnp.stack([lower * cosine - upper * sine_part, upper * cosine + lower * sine_part], axis=2)
    return turned.reshape(rows, -1)

def weighted(scores, allowed, values):
    highest = lax.optimization_barrier(jnp.max(jnp.where(allowed, scores, masked_low), axis=-1, keepdims=True))
    weights = jnp.where(allowed, jnp.exp(scores - highest), 0.0)
    totals = lax.optimization_barrier(jnp.sum(weights, axis=-1))
    rounded = lax.optimization_barrier(weights.astype(jnp.bfloat16))
    mixed = jnp.einsum('hqk,khd->qhd', rounded.astype(jnp.float32), values.astype(jnp.float32))
    return mixed / jnp.transpose(totals)[:, :, None]

def fine_attention(query, keys, values):
    length = query.shape[0]
    block = min(512, length)
    padding = jnp.zeros((WINDOW,) + keys.shape[1:], keys.dtype)
    keys_long = jnp.concatenate([padding, keys])
    values_long = jnp.concatenate([padding, values])
    offsets = jnp.arange(block, dtype=jnp.int32)
    reaches = jnp.arange(block + WINDOW, dtype=jnp.int32)
    scale = HEAD_DIM ** (-0.5)

    def one_block(index):
        begin = index * block
        query_rows = lax.dynamic_slice_in_dim(query, begin, block, 0)
        key_rows = lax.dynamic_slice_in_dim(keys_long, begin, block + WINDOW, 0)
        value_rows = lax.dynamic_slice_in_dim(values_long, begin, block + WINDOW, 0)
        scores = jnp.einsum('qhd,khd->hqk', query_rows.astype(jnp.float32), key_rows.astype(jnp.float32)) * scale
        allowed = (reaches[None, :] > offsets[:, None]) & (reaches[None, :] <= offsets[:, None] + WINDOW) & (begin + reaches[None, :] >= WINDOW)
        return weighted(scores, allowed[None], value_rows)
    mixed = lax.map(one_block, jnp.arange(length // block, dtype=jnp.int32))
    return mixed.reshape(length, -1).astype(jnp.bfloat16)

def coarse_attention(query, keys, values):
    length = query.shape[0]
    block = min(512, length)
    positions = jnp.arange(length, dtype=jnp.int32)
    offsets = jnp.arange(block, dtype=jnp.int32)
    scale = HEAD_DIM ** (-0.5)

    def one_block(index):
        begin = index * block
        query_rows = lax.dynamic_slice_in_dim(query, begin, block, 0)
        scores = jnp.einsum('qhd,khd->hqk', query_rows.astype(jnp.float32), keys.astype(jnp.float32)) * scale
        allowed = positions[None, :] <= begin + offsets[:, None]
        return weighted(scores, allowed[None], values)
    mixed = lax.map(one_block, jnp.arange(length // block, dtype=jnp.int32))
    return mixed.reshape(length, -1).astype(jnp.bfloat16)

def split_heads(values):
    return values.reshape(values.shape[0], HEADS, HEAD_DIM)

def reference(token_ids, embedding, fine_norm, fine_query, fine_key, fine_value, fine_output, shorten_weight, coarse_norm, coarse_query, coarse_key, coarse_value, coarse_output, ffn_norm, ffn_up, ffn_down, upsample_weight):
    fine_pos = jnp.arange(TOKENS, dtype=jnp.int32)
    coarse_pos = jnp.arange(COARSE, dtype=jnp.int32)
    start = embedding[token_ids]
    fine_in = rms_scale(start, fine_norm)
    fine_q = split_heads(rotate(project(fine_in, fine_query), fine_pos).astype(jnp.bfloat16))
    fine_k = split_heads(rotate(project(fine_in, fine_key), fine_pos).astype(jnp.bfloat16))
    fine_v = split_heads(project(fine_in, fine_value).astype(jnp.bfloat16))
    fine_mixed = fine_attention(fine_q, fine_k, fine_v)
    fine = (start.astype(jnp.float32) + project(fine_mixed, fine_output)).astype(jnp.bfloat16)
    padded = jnp.concatenate([jnp.zeros((SHORTEN - 1, D), jnp.bfloat16), fine])
    grouped = jnp.concatenate([padded[offset:offset + TOKENS:SHORTEN] for offset in range(SHORTEN)], axis=1)
    short = project(grouped, shorten_weight.reshape(SHORTEN * D, D)).astype(jnp.bfloat16)
    coarse_in = rms_scale(short, coarse_norm)
    coarse_q = split_heads(rotate(project(coarse_in, coarse_query), coarse_pos).astype(jnp.bfloat16))
    coarse_k = split_heads(rotate(project(coarse_in, coarse_key), coarse_pos).astype(jnp.bfloat16))
    coarse_v = split_heads(project(coarse_in, coarse_value).astype(jnp.bfloat16))
    coarse_mixed = coarse_attention(coarse_q, coarse_k, coarse_v)
    first = short.astype(jnp.float32) + project(coarse_mixed, coarse_output)
    inner = jax.nn.gelu(project(rms_scale(first, ffn_norm), ffn_up)).astype(jnp.bfloat16)
    second = (first + project(inner, ffn_down)).astype(jnp.bfloat16)
    lifted = project(second, upsample_weight.reshape(D, SHORTEN * D)).reshape(TOKENS, D)
    return (fine.astype(jnp.float32) + lifted).astype(jnp.bfloat16)
```

```python
import math

import jax
import jax.numpy as jnp
from jax import lax
from jax.experimental import pallas as pl
from jax.experimental.pallas import tpu as pltpu
from jax.sharding import PartitionSpec as P

D = 1024
HEAD_DIM = 64
HALF = HEAD_DIM // 2
SHORTEN = 4
WINDOW = 1024
LEAD = 128
CARRY = 16

epsilon = 1e-06
masked_low = -1e30
MESH = pl.DeviceIdType.MESH
EXP2_SCALE = HEAD_DIM ** (-0.5) * math.log2(math.e)
VMEM_SPEC = pl.BlockSpec(memory_space=pltpu.VMEM)
ANY_SPEC = pl.BlockSpec(memory_space=pl.ANY)

RELAY, FINISH, MIDDLE, TOTAL, PROJECT, FORWARD = (2, 3, 4, 5, 6, 8)
STEP_KEYS = 512
PIECES = 2


def dot(left, right):
    return jnp.dot(left, right, preferred_element_type=jnp.float32)


def dot_nt(left, right):
    return lax.dot_general(left, right, (((1,), (1,)), ((), ())), preferred_element_type=jnp.float32)


def dot_tn(left, right):
    return lax.dot_general(left, right, (((0,), (0,)), ((), ())), preferred_element_type=jnp.float32)


def normed(data, gain):
    power = jnp.mean(data * data, axis=1, keepdims=True)
    return (data * lax.rsqrt(power + epsilon) * gain).astype(jnp.bfloat16)


def aligned(start, size, unit):
    return pl.ds(pl.multiple_of(start, unit), size)


def periods(column):
    log = 4 + lax.shift_right_logical(column * 14, 5)
    return jnp.left_shift(jnp.ones_like(log), log)


def phase(position, period):
    cycle = jnp.bitwise_and(position, period - 1).astype(jnp.float32)
    return cycle * (2.0 * math.pi / period.astype(jnp.float32))


def remote(source, target, send, receive, device):
    return pltpu.make_async_remote_copy(
        src_ref=source, dst_ref=target, send_sem=send, recv_sem=receive, device_id=device, device_id_type=MESH
    )


class HeadSum:
    def __init__(self, index, peers, part, out, buffers, send_sem, recv_sem):
        self.index = index
        self.me, self.sibling, self.across = peers
        self.part, self.out = part, out
        self.send_a, self.recv_a, self.send_b, self.recv_b, self.final = (buffer.at[index] for buffer in buffers)
        self.send_sem, self.recv_sem = send_sem, recv_sem
        half = part.shape[1] // 2
        self.mine = aligned((self.me % 2) * half, half, half)
        self.theirs = aligned((self.sibling % 2) * half, half, half)

    def copy(self, kind, piece, source, target, device):
        return remote(
            source, target, self.send_sem.at[self.index, kind, piece], self.recv_sem.at[self.index, kind, piece],
            {"head": device},
        )

    def copy_a(self, piece, at):
        return self.copy(0, piece, self.send_a.at[at, :], self.recv_a.at[at, :], self.sibling)

    def copy_b(self, piece, at):
        return self.copy(1, piece, self.send_b.at[at, :], self.recv_b.at[at, :], self.across)

    def copy_c(self, piece, at):
        return self.copy(2, piece, self.final.at[at, :], self.out.at[at, self.mine], self.sibling)

    def begin(self, piece, at):
        self.send_a[at, :] = self.part[at, self.theirs].astype(jnp.bfloat16)
        self.copy_a(piece, at).start()

    def middle(self, piece, at):
        self.copy_a(piece, at).wait_recv()
        summed = self.part[at, self.mine] + self.recv_a[at, :].astype(jnp.float32)
        self.part[at, self.mine] = summed
        self.send_b[at, :] = summed.astype(jnp.bfloat16)
        self.copy_b(piece, at).start()

    def total(self, piece, at, residual=None):
        self.copy_b(piece, at).wait_recv()
        value = self.part[at, self.mine] + self.recv_b[at, :].astype(jnp.float32)
        if residual is not None:
            value = value + residual[at, self.mine]
        value = value.astype(jnp.bfloat16)
        self.final[at, :] = value
        self.copy_c(piece, at).start()
        self.out[at, self.mine] = value

    def end(self, piece, at):
        self.copy_c(piece, at).wait_recv()

    def drain(self, piece, at):
        self.copy_a(piece, at).wait_send()
        self.copy_b(piece, at).wait_send()
        self.copy_c(piece, at).wait_send()


def scratch_list(count, width, chunks, places):
    full = 4 * width
    rows = count // SHORTEN
    frame = LEAD + WINDOW + count
    low = jnp.bfloat16
    wide = jnp.float32
    dma = pltpu.SemaphoreType.DMA
    return [
        ("emb", pltpu.VMEM((256, full), low)),
        ("fq", pltpu.VMEM((full, width), low)),
        ("fk", pltpu.VMEM((full, width), low)),
        ("fv", pltpu.VMEM((full, width), low)),
        ("cols", pltpu.VMEM((full, width), low)),
        ("ws", pltpu.VMEM((SHORTEN, width, full), low)),
        ("cq", pltpu.VMEM((full, width), low)),
        ("ck", pltpu.VMEM((full, width), low)),
        ("cv", pltpu.VMEM((full, width), low)),
        ("co", pltpu.VMEM((width, full), low)),
        ("up", pltpu.VMEM((full, full), low)),
        ("down", pltpu.VMEM((full, full), low)),
        ("lift", pltpu.VMEM((full, SHORTEN * width), low)),
        ("load_sem", dma((13,))),
        ("ids", pltpu.VMEM((1, frame), jnp.int32)),
        ("id_send", dma((2,))),
        ("id_recv", dma((2,))),
        ("col_send", dma((4,))),
        ("col_recv", dma((4,))),
        ("tabs", pltpu.VMEM((6, 256, width), low)),
        ("cos_t", pltpu.VMEM((HALF, frame), wide)),
        ("sin_t", pltpu.VMEM((HALF, frame), wide)),
        ("keys", pltpu.VMEM((width, frame), low)),
        ("values", pltpu.VMEM((width, frame), low)),
        ("query", pltpu.VMEM((LEAD + count, width), low)),
        ("start", pltpu.VMEM((LEAD + count, width), low)),
        ("mixed", pltpu.VMEM((CARRY + count, width), low)),
        ("others", pltpu.VMEM((CARRY + count, 3 * width), low)),
        ("mix_send", dma((3, chunks + 1))),
        ("mix_recv", dma((3, chunks + 1))),
        ("stream", pltpu.VMEM((width // 128, CARRY + count, 128), wide)),
        ("part", pltpu.VMEM((rows, full), wide)),
        ("part_b", pltpu.VMEM((rows, full), wide)),
        ("short", pltpu.VMEM((rows, full), low)),
        ("summed", pltpu.VMEM((rows, full), low)),
        ("first", pltpu.VMEM((rows, full), wide)),
        ("second", pltpu.VMEM((rows, full), low)),
        ("send_a", pltpu.VMEM((3, rows, full // 2), low)),
        ("recv_a", pltpu.VMEM((3, rows, full // 2), low)),
        ("send_b", pltpu.VMEM((3, rows, full // 2), low)),
        ("recv_b", pltpu.VMEM((3, rows, full // 2), low)),
        ("final", pltpu.VMEM((3, rows, full // 2), low)),
        ("sum_send", dma((3, 3, chunks))),
        ("sum_recv", dma((3, 3, chunks))),
        ("coarse_cos", pltpu.VMEM((rows, width), wide)),
        ("coarse_sin", pltpu.VMEM((rows, width), wide)),
        ("pair_out", pltpu.VMEM((2, rows, width), low)),
        ("query_out", pltpu.VMEM((2, rows, width // 2), low)),
        ("pairs", pltpu.VMEM((places * rows, width), low)),
        ("queries", pltpu.VMEM((2 * rows, width // 2), low)),
        ("pair_send", dma((places, chunks))),
        ("pair_recv", dma((places, chunks))),
        ("query_send", dma((chunks,))),
        ("query_recv", dma((chunks,))),
        ("top", pltpu.VMEM((2, 2 * rows, 1), wide)),
        ("norm", pltpu.VMEM((2, 2 * rows, 1), wide)),
        ("acc", pltpu.VMEM((2, 2 * rows, width // 2), wide)),
        ("turn", pltpu.VMEM((rows, width // 2), low)),
        ("heads_in", pltpu.VMEM((rows, width), low)),
        ("turn_send", dma((1,))),
        ("turn_recv", dma((1,))),
        ("spread", pltpu.VMEM((width // 128, count, 128), wide)),
    ]


class Names:
    pass


def block_kernel(names, chunk_rows, *refs):
    (ids_ref, fine_gain, coarse_gain, ffn_gain, emb_h, fq_h, fk_h, fv_h, fo_h, ws_h,
     cq_h, ck_h, cv_h, co_h, up_h, down_h, lift_h, out_ref) = refs[:18]
    s = Names()
    for name, ref in zip(names, refs[18:]):
        setattr(s, name, ref)
    count, width = out_ref.shape
    full = 4 * width
    heads = width // HEAD_DIM
    chunks = count // chunk_rows
    group = chunk_rows // SHORTEN
    rows = count // SHORTEN
    frame = LEAD + WINDOW + count
    span = WINDOW + chunk_rows
    lanes = width // 128
    pair = width // 2

    places = lax.axis_size("seq")
    place = lax.axis_index("seq")
    levels = places // 2
    side = place % 2
    level = place // 2
    cross = place + 1 - 2 * side
    me = lax.axis_index("head")
    sibling = me + 1 - 2 * (me % 2)
    across = (me + 2) % 4
    diagonal = (sibling + 2) % 4

    barrier = pltpu.get_barrier_semaphore()
    for device in (sibling, across, diagonal):
        pl.semaphore_signal(barrier, inc=1, device_id={"head": device}, device_id_type=MESH)

    def greet(step, state):
        pl.semaphore_signal(
            barrier, inc=1, device_id={"seq": (place + step) % places}, device_id_type=MESH
        )
        return state

    lax.fori_loop(1, places, greet, 0)

    own_columns = aligned(me * width, width, width)
    loads = {
        name: pltpu.make_async_copy(source, target, s.load_sem.at[index])
        for index, (name, source, target) in enumerate((
            ("emb", emb_h, s.emb), ("fk", fk_h, s.fk), ("fv", fv_h, s.fv), ("fq", fq_h, s.fq),
            ("cols", fo_h.at[:, own_columns], s.cols.at[pl.ds(0, width), :]),
            ("ws", ws_h, s.ws), ("cq", cq_h, s.cq), ("ck", ck_h, s.ck), ("cv", cv_h, s.cv), ("co", co_h, s.co),
            ("up", up_h, s.up), ("down", down_h, s.down), ("lift", lift_h, s.lift),
        ))
    }
    for load in loads.values():
        load.start()

    s.ids[:, LEAD + WINDOW :] = ids_ref[...]

    @pl.when(place < 1)
    def _():
        s.ids[:, LEAD : LEAD + WINDOW] = jnp.zeros((1, WINDOW), jnp.int32)

    @pl.when(place < 2)
    def _():
        s.ids[:, :LEAD] = jnp.zeros((1, LEAD), jnp.int32)

    def clear(index, state):
        chunk = index // (places - 2)
        blank = index % (places - 2)

        @pl.when(blank + 2 >= 2 * level + 2)
        def _():
            at = aligned((chunk * places + blank + 2) * group, group, group)
            s.pairs[at, :] = jnp.zeros((group, width), jnp.bfloat16)

        return state

    lax.fori_loop(0, chunks * (places - 2), clear, 0)

    column = lax.broadcasted_iota(jnp.int32, (HALF, 128), 0)
    lane = lax.broadcasted_iota(jnp.int32, (HALF, 128), 1)
    period = periods(column)
    small = phase(lane, period)
    base = (place - 1) * count - LEAD
    large = phase(base + 128 * lane, period)
    cos_b, sin_b, cos_a, sin_a = jnp.cos(small), jnp.sin(small), jnp.cos(large), jnp.sin(large)
    for block in range(frame // 128):
        at = slice(block * 128, block * 128 + 128)
        cos_k, sin_k = cos_a[:, block : block + 1], sin_a[:, block : block + 1]
        s.cos_t[:, at] = cos_b * cos_k - sin_b * sin_k
        s.sin_t[:, at] = sin_b * cos_k + cos_b * sin_k

    pl.semaphore_wait(barrier, places + 2)

    def id_copy(steps):
        if steps == 1:
            target = s.ids.at[:, pl.ds(LEAD, WINDOW)]
            source = ids_ref
        else:
            target = s.ids.at[:, pl.ds(0, LEAD)]
            source = ids_ref.at[:, pl.ds(count - LEAD, LEAD)]
        device = (place + steps) % places
        return remote(source, target, s.id_send.at[steps - 1], s.id_recv.at[steps - 1], {"seq": device})

    for steps in (1, 2):
        @pl.when(place + steps < places)
        def _():
            id_copy(steps).start()

    def column_copy(flip, device):
        return remote(
            fo_h.at[:, aligned(device * width, width, width)], s.cols.at[pl.ds(flip * width, width), :],
            s.col_send.at[flip], s.col_recv.at[flip], {"head": device},
        )

    column_copies = [column_copy(flip, device) for flip, device in ((1, sibling), (2, across), (3, diagonal))]
    for copy in column_copies:
        copy.start()

    loads["emb"].wait()
    level_in = normed(s.emb[...].astype(jnp.float32), fine_gain[...])

    def split(values):
        high = values.astype(jnp.bfloat16)
        return high, (values - high.astype(jnp.float32)).astype(jnp.bfloat16)

    loads["fk"].wait()
    s.tabs[0], s.tabs[1] = split(dot(level_in, s.fk[...]).T)
    loads["fv"].wait()
    s.tabs[2] = dot(level_in, s.fv[...]).T.astype(jnp.bfloat16)
    loads["fq"].wait()
    s.tabs[3], s.tabs[4] = split(dot(level_in, s.fq[...]).T)
    s.tabs[5] = s.emb[:, own_columns]

    for steps in (1, 2):
        @pl.when(place >= steps)
        def _():
            id_copy(steps).wait_recv()

    def turned(joined, at):
        cosine, sine = s.cos_t[:, at], s.sin_t[:, at]
        pieces = []
        for head in range(heads):
            low = joined[head * HEAD_DIM : head * HEAD_DIM + HALF]
            high = joined[head * HEAD_DIM + HALF : (head + 1) * HEAD_DIM]
            pieces += [low * cosine - high * sine, high * cosine + low * sine]
        return jnp.concatenate(pieces, axis=0)

    def token_rows(begin, size, queries):
        at = aligned(begin, size, 128)
        levels_at = lax.broadcasted_iota(jnp.int32, (256, size), 0)
        hot = jnp.where(levels_at == s.ids[:, at], 1.0, 0.0).astype(jnp.bfloat16)
        s.keys[:, at] = turned(dot(s.tabs[0], hot) + dot(s.tabs[1], hot), at).astype(jnp.bfloat16)
        s.values[:, at] = dot(s.tabs[2], hot).astype(jnp.bfloat16)
        if queries:
            to = aligned(begin - WINDOW, size, 128)
            turned_q = turned(dot(s.tabs[3], hot) + dot(s.tabs[4], hot), at)
            s.query[to, :] = turned_q.T.astype(jnp.bfloat16)
            s.start[to, :] = dot_tn(hot, s.tabs[5]).astype(jnp.bfloat16)

    early = 256
    late = (LEAD + count) // 3

    def early_rows(index, state):
        token_rows(index * early, early, False)
        return state

    def late_rows(index, state):
        token_rows(WINDOW + index * late, late, True)
        return state

    lax.fori_loop(0, WINDOW // early, early_rows, 0)
    lax.fori_loop(0, 3, late_rows, 0)

    def attend(query, key_at, mask):
        size = query.shape[0]
        lane_head = lax.broadcasted_iota(jnp.int32, (size, width), 1) // HEAD_DIM
        result = jnp.zeros((size, width), jnp.float32)
        for head in range(heads):
            masked_q = jnp.where(lane_head == head, query, jnp.zeros_like(query))
            pieces = mask(dot(masked_q, s.keys[:, key_at]))
            top = pieces[0]
            for piece in pieces[1:]:
                top = jnp.maximum(top, piece)
            top = jnp.max(top, axis=1, keepdims=True)
            weights = [jnp.exp2((piece - top) * EXP2_SCALE) for piece in pieces]
            total = weights[0]
            for piece in weights[1:]:
                total = total + piece
            total = jnp.sum(total, axis=1, keepdims=True)
            rounded = jnp.concatenate([piece.astype(jnp.bfloat16) for piece in weights], axis=1)
            out = dot_nt(rounded, s.values[:, key_at])
            result = jnp.where(lane_head == head, out / total, result)
        return result.astype(jnp.bfloat16)

    def mixed_rows(chunk):
        return aligned(CARRY + chunk * chunk_rows, chunk_rows, CARRY)

    def mix_copies(chunk, at):
        def slot(which):
            return s.others.at[at, pl.ds((which - 1) * width, width)]

        def copy(kind, source, target, device):
            return remote(source, target, s.mix_send.at[kind, chunk], s.mix_recv.at[kind, chunk], {"head": device})

        return (
            copy(0, s.mixed.at[at, :], slot(2), across),
            copy(1, s.mixed.at[at, :], slot(1), sibling),
            copy(2, slot(2), slot(3), sibling),
        )

    carry_at = pl.ds(0, CARRY)
    carry_copies = mix_copies(chunks, carry_at)

    def carry_mask(scores):
        key = lax.broadcasted_iota(jnp.int32, scores.shape, 1)
        row = lax.broadcasted_iota(jnp.int32, scores.shape, 0)
        floor = jnp.where(place < 2, LEAD, 0)
        allowed = (key > row + (LEAD - CARRY)) & (key <= row + (LEAD - CARRY + WINDOW)) & (key >= floor)
        return [jnp.where(allowed, scores, masked_low)]

    s.mixed[carry_at, :] = attend(s.query[LEAD - CARRY : LEAD, :], pl.ds(0, LEAD + WINDOW), carry_mask)
    carry_copies[0].start()
    carry_copies[1].start()

    row = lax.broadcasted_iota(jnp.int32, (chunk_rows, chunk_rows), 0)
    column = lax.broadcasted_iota(jnp.int32, (chunk_rows, chunk_rows), 1)

    def attend_chunk(chunk):
        begin = chunk * chunk_rows
        floor = jnp.where(place == 0, WINDOW - begin, 0)

        def mask(scores):
            pieces = []
            for at in range(0, span, chunk_rows):
                piece = scores[:, at : at + chunk_rows]
                if at == span - chunk_rows:
                    allowed = column <= row
                else:
                    allowed = column >= floor - at
                    if at == 0:
                        allowed = allowed & (column > row)
                pieces.append(jnp.where(allowed, piece, masked_low))
            return pieces

        query = s.query[aligned(LEAD + begin, chunk_rows, chunk_rows), :]
        at = mixed_rows(chunk)
        s.mixed[at, :] = attend(query, aligned(LEAD + begin, span, 128), mask)
        copies = mix_copies(chunk, at)
        copies[0].start()
        copies[1].start()

    def fine_rows(at, start_at):
        merged = dot(s.mixed[at, :], s.cols[:width, :]) + dot(s.others[at, :], s.cols[width:, :])
        value = (s.start[start_at, :].astype(jnp.float32) + merged).astype(jnp.bfloat16).astype(jnp.float32)
        for block in range(lanes):
            s.stream[block, at, :] = value[:, block * 128 : block * 128 + 128]

    peers = (me, sibling, across)
    buffers = (s.send_a, s.recv_a, s.send_b, s.recv_b, s.final)
    short_sum = HeadSum(0, peers, s.part, s.short, buffers, s.sum_send, s.sum_recv)

    def short_rows(chunk):
        return aligned(chunk * group, group, group)

    def relay_chunk(chunk):
        @pl.when(chunk == 0)
        def _():
            carry_copies[0].wait_recv()
            carry_copies[2].start()

        copies = mix_copies(chunk, mixed_rows(chunk))
        copies[0].wait_recv()
        copies[2].start()

    def finish_chunk(chunk):
        @pl.when(chunk == 0)
        def _():
            for copy in column_copies:
                copy.wait_recv()
            loads["cols"].wait()
            loads["ws"].wait()
            carry_copies[1].wait_recv()
            carry_copies[2].wait_recv()
            fine_rows(carry_at, pl.ds(LEAD - CARRY, CARRY))

            @pl.when(place == 0)
            def _():
                s.stream[:, 0:CARRY, :] = jnp.zeros((lanes, CARRY, 128), jnp.float32)

        at = mixed_rows(chunk)
        copies = mix_copies(chunk, at)
        copies[1].wait_recv()
        copies[2].wait_recv()
        fine_rows(at, aligned(LEAD + chunk * chunk_rows, chunk_rows, chunk_rows))
        total = jnp.zeros((group, full), jnp.float32)
        for offset in range(SHORTEN):
            begin = CARRY - (SHORTEN - 1) + offset + chunk * chunk_rows
            member = jnp.concatenate(
                [s.stream[block, pl.ds(begin, group, stride=SHORTEN), :] for block in range(lanes)], axis=1
            )
            total = total + dot(member.astype(jnp.bfloat16), s.ws[offset])
        s.part[short_rows(chunk), :] = total
        short_sum.begin(chunk, short_rows(chunk))

    lane_f = lax.broadcasted_iota(jnp.int32, (rows, 128), 1) % HEAD_DIM
    period_f = periods(lane_f % HALF)
    angle_f = phase(place * rows + lax.broadcasted_iota(jnp.int32, (rows, 128), 0), period_f)
    cos_f = jnp.cos(angle_f)
    sin_f = jnp.where(lane_f < HALF, -jnp.sin(angle_f), jnp.sin(angle_f))
    for block in range(lanes):
        s.coarse_cos[:, block * 128 : block * 128 + 128] = cos_f
        s.coarse_sin[:, block * 128 : block * 128 + 128] = sin_f

    def pair_rows(chunk, source):
        return aligned((chunk * places + source) * group, group, group)

    def pair_copy(chunk, target):
        at = pair_rows(chunk, place)
        return remote(
            s.pair_out.at[target % 2, short_rows(chunk), :], s.pairs.at[at, :],
            s.pair_send.at[target, chunk], s.pair_recv.at[place, chunk], {"seq": target},
        )

    def pair_arrival(chunk, source):
        at = pair_rows(chunk, source)
        return remote(
            s.pairs.at[at, :], s.pairs.at[at, :], s.pair_send.at[source, chunk], s.pair_recv.at[source, chunk],
            {"seq": cross},
        )

    def query_copy(chunk):
        at = short_rows(chunk)
        return remote(
            s.query_out.at[1 - side, at, :], s.queries.at[aligned(side * rows + chunk * group, group, group), :],
            s.query_send.at[chunk], s.query_recv.at[chunk], {"seq": cross},
        )

    def for_targets(action):
        def one(index, state):
            target = places - 1 - index

            @pl.when(target != place)
            def _():
                action(target)

            return state

        lax.fori_loop(0, places - 2 * level, one, 0)

    def project_chunk(chunk):
        @pl.when(chunk == 0)
        def _():
            for name in ("cq", "ck", "cv"):
                loads[name].wait()

        at = short_rows(chunk)
        short_sum.end(chunk, at)
        coarse_in = normed(s.short[at, :].astype(jnp.float32), coarse_gain[...])
        cosine, sine = s.coarse_cos[at, :], s.coarse_sin[at, :]
        is_low = lax.broadcasted_iota(jnp.int32, (group, width), 1) % HEAD_DIM < HALF

        def rotated(values):
            other = jnp.where(is_low, pltpu.roll(values, width - HALF, 1), pltpu.roll(values, HALF, 1))
            return (values * cosine + other * sine).astype(jnp.bfloat16)

        key = rotated(dot(coarse_in, s.ck[...]))
        value = dot(coarse_in, s.cv[...]).astype(jnp.bfloat16)
        for half in range(2):
            s.pair_out[half, at, :pair] = key[:, half * pair : half * pair + pair]
            s.pair_out[half, at, pair:] = value[:, half * pair : half * pair + pair]
        for_targets(lambda target: pair_copy(chunk, target).start())
        query = rotated(dot(coarse_in, s.cq[...]))
        for half in range(2):
            s.query_out[half, at, :] = query[:, half * pair : half * pair + pair]
        query_copy(chunk).start()
        s.pairs[pair_rows(chunk, place), :] = s.pair_out[side, at, :]
        s.queries[aligned(side * rows + chunk * group, group, group), :] = s.query_out[side, at, :]

    def one_step(step, state):
        def staged(lag, action):
            chunk = step - lag

            @pl.when((chunk >= 0) & (chunk < chunks))
            def _():
                action(chunk)

        staged(0, attend_chunk)
        staged(PROJECT, project_chunk)
        staged(TOTAL, lambda chunk: short_sum.total(chunk, short_rows(chunk)))
        staged(MIDDLE, lambda chunk: short_sum.middle(chunk, short_rows(chunk)))
        staged(FINISH, finish_chunk)
        staged(RELAY, relay_chunk)
        return state

    lax.fori_loop(0, chunks + PROJECT, one_step, 0)

    def wait_chunk(chunk):
        def one(source, state):
            @pl.when(source != place)
            def _():
                pair_arrival(chunk, source).wait_recv()

            return state

        lax.fori_loop(0, 2 * level + 2, one, 0)

    def wait_queries(chunk, state):
        query_copy(chunk).wait_recv()
        return state

    lax.fori_loop(0, chunks, wait_queries, 0)

    s.top[...] = jnp.full(s.top.shape, masked_low, jnp.float32)
    s.norm[...] = jnp.zeros(s.norm.shape, jnp.float32)
    s.acc[...] = jnp.zeros(s.acc.shape, jnp.float32)
    per_chunk = places * group
    pair_lane = lax.broadcasted_iota(jnp.int32, (2 * rows, pair), 1) // HEAD_DIM
    queries = s.queries[...]

    def key_step(step, state):
        if per_chunk <= STEP_KEYS:
            for inner in range(STEP_KEYS // per_chunk):
                wait_chunk(step * (STEP_KEYS // per_chunk) + inner)
        else:
            ratio = per_chunk // STEP_KEYS

            @pl.when(step % ratio == 0)
            def _():
                wait_chunk(step // ratio)

        block = s.pairs[aligned(step * STEP_KEYS, STEP_KEYS, STEP_KEYS), :]
        keys, values = block[:, :pair], block[:, pair:]
        index = step * STEP_KEYS + lax.broadcasted_iota(jnp.int32, (1, STEP_KEYS), 1)
        inside = index % per_chunk
        key_at = (inside // group) * rows + (index // per_chunk) * group + inside % group
        query_at = 2 * level * rows + lax.broadcasted_iota(jnp.int32, (2 * rows, 1), 0)
        allowed = key_at <= query_at
        for head in range(pair // HEAD_DIM):
            masked_q = jnp.where(pair_lane == head, queries, jnp.zeros_like(queries))
            scores = jnp.where(allowed, dot_nt(masked_q, keys), masked_low)
            fresh = jnp.maximum(s.top[head], jnp.max(scores, axis=1, keepdims=True))
            factor = jnp.exp2((s.top[head] - fresh) * EXP2_SCALE)
            weights = jnp.exp2((scores - fresh) * EXP2_SCALE)
            s.norm[head] = s.norm[head] * factor + jnp.sum(weights, axis=1, keepdims=True)
            s.acc[head] = s.acc[head] * factor + dot(weights.astype(jnp.bfloat16), values)
            s.top[head] = fresh
        return state

    lax.fori_loop(0, places * rows // STEP_KEYS, key_step, 0)

    def turn_copy():
        return remote(
            s.turn, s.heads_in.at[:, aligned(side * pair, pair, pair)],
            s.turn_send.at[0], s.turn_recv.at[0], {"seq": cross},
        )

    def mixed_of(at):
        result = jnp.zeros((rows, pair), jnp.float32)
        for head in range(pair // HEAD_DIM):
            result = jnp.where(pair_lane[:rows] == head, s.acc[head, at, :] / s.norm[head, at, :], result)
        return result.astype(jnp.bfloat16)

    s.turn[...] = mixed_of(aligned((1 - side) * rows, rows, rows))
    turn_copy().start()
    s.heads_in[:, aligned(side * pair, pair, pair)] = mixed_of(aligned(side * rows, rows, rows))
    loads["co"].wait()
    turn_copy().wait_recv()

    out_sum = HeadSum(1, peers, s.part, s.summed, buffers, s.sum_send, s.sum_recv)
    ffn_sum = HeadSum(2, peers, s.part_b, s.second, buffers, s.sum_send, s.sum_recv)
    size = rows // PIECES
    at = [pl.ds(piece * size, size) for piece in range(PIECES)]

    for piece in range(PIECES):
        s.part[at[piece], :] = dot(s.heads_in[at[piece], :], s.co[...])
        out_sum.begin(piece, at[piece])
    for name in ("up", "down", "lift"):
        loads[name].wait()
    for piece in range(PIECES):
        out_sum.middle(piece, at[piece])

    def feed(piece):
        out_sum.end(piece, at[piece])
        value = s.short[at[piece], :].astype(jnp.float32) + s.summed[at[piece], :].astype(jnp.float32)
        s.first[at[piece], :] = value
        inner = jax.nn.gelu(dot(normed(value, ffn_gain[...]), s.up[...])).astype(jnp.bfloat16)
        s.part_b[at[piece], :] = dot(inner, s.down[...])
        ffn_sum.begin(piece, at[piece])

    def raise_rows(piece):
        ffn_sum.end(piece, at[piece])
        for member in range(SHORTEN):
            lifted = dot(s.second[at[piece], :], s.lift[:, member * width : (member + 1) * width])
            for block in range(lanes):
                s.spread[block, pl.ds(SHORTEN * size * piece + member, size, stride=SHORTEN), :] = lifted[
                    :, block * 128 : block * 128 + 128
                ]
        for block in range(lanes):
            to = slice(SHORTEN * size * piece, SHORTEN * size * (piece + 1))
            base_at = slice(CARRY + SHORTEN * size * piece, CARRY + SHORTEN * size * (piece + 1))
            out_ref[to, block * 128 : block * 128 + 128] = (
                s.stream[block, base_at, :] + s.spread[block, to, :]
            ).astype(jnp.bfloat16)

    for step in range(PIECES + 4):
        if step < PIECES:
            out_sum.total(step, at[step])
        if 0 <= step - 1 < PIECES:
            feed(step - 1)
        if 0 <= step - 2 < PIECES:
            ffn_sum.middle(step - 2, at[step - 2])
        if 0 <= step - 3 < PIECES:
            ffn_sum.total(step - 3, at[step - 3], s.first)
        if 0 <= step - 4 < PIECES:
            raise_rows(step - 4)

    for steps in (1, 2):
        @pl.when(place + steps < places)
        def _():
            id_copy(steps).wait_send()

    for copy in column_copies:
        copy.wait_send()
    for copy in carry_copies:
        copy.wait_send()

    def drain(chunk, state):
        for copy in mix_copies(chunk, mixed_rows(chunk)):
            copy.wait_send()
        short_sum.drain(chunk, short_rows(chunk))
        for_targets(lambda target: pair_copy(chunk, target).wait_send())
        query_copy(chunk).wait_send()
        return state

    lax.fori_loop(0, chunks, drain, 0)
    turn_copy().wait_send()
    for piece in range(PIECES):
        out_sum.drain(piece, at[piece])
        ffn_sum.drain(piece, at[piece])


def local(
    token_ids,
    embedding,
    fine_norm,
    fine_query,
    fine_key,
    fine_value,
    fine_output,
    shorten_weight,
    coarse_norm,
    coarse_query,
    coarse_key,
    coarse_value,
    coarse_output,
    ffn_norm,
    ffn_up,
    ffn_down,
    upsample_weight,
):
    count = token_ids.shape[0]
    width = fine_query.shape[1]
    chunk_rows = min(128, count)
    chunks = count // chunk_rows
    scratch = scratch_list(count, width, chunks, lax.axis_size("seq"))
    names = [name for name, _ in scratch]

    def kernel(*refs):
        block_kernel(names, chunk_rows, *refs)

    return pl.pallas_call(
        kernel,
        out_shape=jax.ShapeDtypeStruct((count, width), jnp.bfloat16),
        in_specs=[VMEM_SPEC] * 4 + [ANY_SPEC] * 13,
        out_specs=VMEM_SPEC,
        scratch_shapes=[shape for _, shape in scratch],
        compiler_params=pltpu.CompilerParams(
            collective_id=1, has_side_effects=True, vmem_limit_bytes=60 * 2**20
        ),
        name="block_kernel",
    )(
        token_ids.reshape(1, count),
        fine_norm.reshape(1, D),
        coarse_norm.reshape(1, D),
        ffn_norm.reshape(1, D),
        embedding,
        fine_query,
        fine_key,
        fine_value,
        fine_output,
        shorten_weight,
        coarse_query,
        coarse_key,
        coarse_value,
        coarse_output,
        ffn_up,
        ffn_down,
        upsample_weight.reshape(D, SHORTEN * width),
    )


def solution(mesh):
    return jax.shard_map(
        local,
        mesh=mesh,
        in_specs=(
            P("seq"),
            P(),
            P(),
            P(None, "head"),
            P(None, "head"),
            P(None, "head"),
            P("head", None),
            P(None, "head", None),
            P(),
            P(None, "head"),
            P(None, "head"),
            P(None, "head"),
            P("head", None),
            P(),
            P(None, "head"),
            P("head", None),
            P(None, None, "head"),
        ),
        out_specs=P("seq", "head"),
        check_vma=False,
    )
```

```python
import math

import jax
import jax.numpy as jnp
from jax import lax
from jax.experimental import pallas as pl
from jax.experimental.pallas import tpu as pltpu
from jax.sharding import PartitionSpec as P

D = 1024
HEAD_DIM = 64
HALF = HEAD_DIM // 2
SHORTEN = 4
WINDOW = 1024
LEAD = 128
CARRY = 16

epsilon = 1e-06
masked_low = -1e30
MESH = pl.DeviceIdType.MESH
EXP2_SCALE = HEAD_DIM ** (-0.5) * math.log2(math.e)
VMEM_SPEC = pl.BlockSpec(memory_space=pltpu.VMEM)
ANY_SPEC = pl.BlockSpec(memory_space=pl.ANY)

RELAY, FINISH, MIDDLE, TOTAL, PROJECT = (2, 3, 4, 6, 7)
STEP_KEYS = 512
PIECES = 2


def dot(left, right):
    return jnp.dot(left, right, preferred_element_type=jnp.float32)


def dot_nt(left, right):
    return lax.dot_general(left, right, (((1,), (1,)), ((), ())), preferred_element_type=jnp.float32)


def dot_tn(left, right):
    return lax.dot_general(left, right, (((0,), (0,)), ((), ())), preferred_element_type=jnp.float32)


def normed(data, gain):
    power = jnp.mean(data * data, axis=1, keepdims=True)
    return (data * lax.rsqrt(power + epsilon) * gain).astype(jnp.bfloat16)


def aligned(start, size, unit):
    return pl.ds(pl.multiple_of(start, unit), size)


def periods(column):
    log = 4 + lax.shift_right_logical(column * 14, 5)
    return jnp.left_shift(jnp.ones_like(log), log)


def phase(position, period):
    cycle = jnp.bitwise_and(position, period - 1).astype(jnp.float32)
    return cycle * (2.0 * math.pi / period.astype(jnp.float32))


def remote(source, target, send, receive, device):
    return pltpu.make_async_remote_copy(
        src_ref=source, dst_ref=target, send_sem=send, recv_sem=receive, device_id=device, device_id_type=MESH
    )


class HeadSum:
    def __init__(self, index, peers, part, out, buffers, send_sem, recv_sem):
        self.index = index
        self.me, self.sibling, self.across = peers
        self.part, self.out = part, out
        self.send_a, self.recv_a, self.send_b, self.recv_b, self.final = (buffer.at[index] for buffer in buffers)
        self.send_sem, self.recv_sem = send_sem, recv_sem
        half = part.shape[1] // 2
        self.mine = aligned((self.me % 2) * half, half, half)
        self.theirs = aligned((self.sibling % 2) * half, half, half)

    def copy(self, kind, piece, source, target, device):
        return remote(
            source, target, self.send_sem.at[self.index, kind, piece], self.recv_sem.at[self.index, kind, piece],
            {"head": device},
        )

    def copy_a(self, piece, at):
        return self.copy(0, piece, self.send_a.at[at, :], self.recv_a.at[at, :], self.sibling)

    def copy_b(self, piece, at):
        return self.copy(1, piece, self.send_b.at[at, :], self.recv_b.at[at, :], self.across)

    def copy_c(self, piece, at):
        return self.copy(2, piece, self.final.at[at, :], self.out.at[at, self.mine], self.sibling)

    def begin(self, piece, at):
        self.send_a[at, :] = self.part[at, self.theirs].astype(jnp.bfloat16)
        self.copy_a(piece, at).start()

    def middle(self, piece, at):
        self.copy_a(piece, at).wait_recv()
        summed = self.part[at, self.mine] + self.recv_a[at, :].astype(jnp.float32)
        self.part[at, self.mine] = summed
        self.send_b[at, :] = summed.astype(jnp.bfloat16)
        self.copy_b(piece, at).start()

    def total(self, piece, at, residual=None):
        self.copy_b(piece, at).wait_recv()
        value = self.part[at, self.mine] + self.recv_b[at, :].astype(jnp.float32)
        if residual is not None:
            value = value + residual[at, self.mine]
        value = value.astype(jnp.bfloat16)
        self.final[at, :] = value
        self.copy_c(piece, at).start()
        self.out[at, self.mine] = value

    def end(self, piece, at):
        self.copy_c(piece, at).wait_recv()

    def drain(self, piece, at):
        self.copy_a(piece, at).wait_send()
        self.copy_b(piece, at).wait_send()
        self.copy_c(piece, at).wait_send()


def scratch_list(count, width, chunks, places):
    full = 4 * width
    rows = count // SHORTEN
    frame = LEAD + WINDOW + count
    low = jnp.bfloat16
    wide = jnp.float32
    dma = pltpu.SemaphoreType.DMA
    return [
        ("emb", pltpu.VMEM((256, full), low)),
        ("fq", pltpu.VMEM((full, width), low)),
        ("fk", pltpu.VMEM((full, width), low)),
        ("fv", pltpu.VMEM((full, width), low)),
        ("cols", pltpu.VMEM((full, width), low)),
        ("ws", pltpu.VMEM((SHORTEN, width, full), low)),
        ("cq", pltpu.VMEM((full, width), low)),
        ("ck", pltpu.VMEM((full, width), low)),
        ("cv", pltpu.VMEM((full, width), low)),
        ("co", pltpu.VMEM((width, full), low)),
        ("up", pltpu.VMEM((full, full), low)),
        ("down", pltpu.VMEM((full, full), low)),
        ("lift", pltpu.VMEM((full, SHORTEN * width), low)),
        ("load_sem", dma((13,))),
        ("ids", pltpu.VMEM((1, frame), jnp.int32)),
        ("id_send", dma((2,))),
        ("id_recv", dma((2,))),
        ("col_send", dma((4,))),
        ("col_recv", dma((4,))),
        ("tabs", pltpu.VMEM((6, 256, width), low)),
        ("cos_t", pltpu.VMEM((HALF, frame), wide)),
        ("sin_t", pltpu.VMEM((HALF, frame), wide)),
        ("keys", pltpu.VMEM((frame, width), low)),
        ("values", pltpu.VMEM((width, frame), low)),
        ("query", pltpu.VMEM((width, LEAD + count), low)),
        ("start", pltpu.VMEM((LEAD + count, width), low)),
        ("mixed", pltpu.VMEM((CARRY + count, width), low)),
        ("others", pltpu.VMEM((CARRY + count, 3 * width), low)),
        ("mix_send", dma((3, chunks + 1))),
        ("mix_recv", dma((3, chunks + 1))),
        ("stream", pltpu.VMEM((width // 128, CARRY + count, 128), wide)),
        ("part", pltpu.VMEM((rows, full), wide)),
        ("part_b", pltpu.VMEM((rows, full), wide)),
        ("short", pltpu.VMEM((rows, full), low)),
        ("summed", pltpu.VMEM((rows, full), low)),
        ("first", pltpu.VMEM((rows, full), wide)),
        ("second", pltpu.VMEM((rows, full), low)),
        ("send_a", pltpu.VMEM((3, rows, full // 2), low)),
        ("recv_a", pltpu.VMEM((3, rows, full // 2), low)),
        ("send_b", pltpu.VMEM((3, rows, full // 2), low)),
        ("recv_b", pltpu.VMEM((3, rows, full // 2), low)),
        ("final", pltpu.VMEM((3, rows, full // 2), low)),
        ("sum_send", dma((3, 3, chunks))),
        ("sum_recv", dma((3, 3, chunks))),
        ("coarse_cos", pltpu.VMEM((rows, width), wide)),
        ("coarse_sin", pltpu.VMEM((rows, width), wide)),
        ("pair_out", pltpu.VMEM((2, rows, width), low)),
        ("query_out", pltpu.VMEM((2, rows, width // 2), low)),
        ("pairs", pltpu.VMEM((places * rows, width), low)),
        ("queries", pltpu.VMEM((2 * rows, width // 2), low)),
        ("pair_send", dma((places, chunks))),
        ("pair_recv", dma((places, chunks))),
        ("query_send", dma((chunks,))),
        ("query_recv", dma((chunks,))),
        ("top", pltpu.VMEM((2, 1, 2 * rows), wide)),
        ("norm", pltpu.VMEM((2, 1, 2 * rows), wide)),
        ("acc", pltpu.VMEM((width // 2, 2 * rows), wide)),
        ("turn", pltpu.VMEM((rows, width // 2), low)),
        ("heads_in", pltpu.VMEM((rows, width), low)),
        ("turn_send", dma((1,))),
        ("turn_recv", dma((1,))),
        ("spread", pltpu.VMEM((width // 128, count, 128), wide)),
    ]


class Names:
    pass


def block_kernel(names, chunk_rows, *refs):
    (ids_ref, fine_gain, coarse_gain, ffn_gain, emb_h, fq_h, fk_h, fv_h, fo_h, ws_h,
     cq_h, ck_h, cv_h, co_h, up_h, down_h, lift_h, out_ref) = refs[:18]
    s = Names()
    for name, ref in zip(names, refs[18:]):
        setattr(s, name, ref)
    count, width = out_ref.shape
    full = 4 * width
    heads = width // HEAD_DIM
    chunks = count // chunk_rows
    group = chunk_rows // SHORTEN
    rows = count // SHORTEN
    frame = LEAD + WINDOW + count
    span = WINDOW + chunk_rows
    lanes = width // 128
    pair = width // 2

    places = lax.axis_size("seq")
    place = lax.axis_index("seq")
    levels = places // 2
    side = place % 2
    level = place // 2
    cross = place + 1 - 2 * side
    me = lax.axis_index("head")
    sibling = me + 1 - 2 * (me % 2)
    across = (me + 2) % 4
    diagonal = (sibling + 2) % 4

    barrier = pltpu.get_barrier_semaphore()
    for device in (sibling, across, diagonal):
        pl.semaphore_signal(barrier, inc=1, device_id={"head": device}, device_id_type=MESH)

    def greet(step, state):
        pl.semaphore_signal(
            barrier, inc=1, device_id={"seq": (place + step) % places}, device_id_type=MESH
        )
        return state

    lax.fori_loop(1, places, greet, 0)

    own_columns = aligned(me * width, width, width)
    loads = {
        name: pltpu.make_async_copy(source, target, s.load_sem.at[index])
        for index, (name, source, target) in enumerate((
            ("emb", emb_h, s.emb), ("fk", fk_h, s.fk), ("fv", fv_h, s.fv), ("fq", fq_h, s.fq),
            ("cols", fo_h.at[:, own_columns], s.cols.at[pl.ds(0, width), :]),
            ("ws", ws_h, s.ws), ("cq", cq_h, s.cq), ("ck", ck_h, s.ck), ("cv", cv_h, s.cv), ("co", co_h, s.co),
            ("up", up_h, s.up), ("down", down_h, s.down), ("lift", lift_h, s.lift),
        ))
    }
    for load in loads.values():
        load.start()

    s.ids[:, LEAD + WINDOW :] = ids_ref[...]

    @pl.when(place < 1)
    def _():
        s.ids[:, LEAD : LEAD + WINDOW] = jnp.zeros((1, WINDOW), jnp.int32)

    @pl.when(place < 2)
    def _():
        s.ids[:, :LEAD] = jnp.zeros((1, LEAD), jnp.int32)

    def clear(index, state):
        chunk = index // (places - 2)
        blank = index % (places - 2)

        @pl.when(blank + 2 >= 2 * level + 2)
        def _():
            at = aligned((chunk * places + blank + 2) * group, group, group)
            s.pairs[at, :] = jnp.zeros((group, width), jnp.bfloat16)

        return state

    lax.fori_loop(0, chunks * (places - 2), clear, 0)

    column = lax.broadcasted_iota(jnp.int32, (HALF, 128), 0)
    lane = lax.broadcasted_iota(jnp.int32, (HALF, 128), 1)
    period = periods(column)
    small = phase(lane, period)
    base = (place - 1) * count - LEAD
    large = phase(base + 128 * lane, period)
    cos_b, sin_b, cos_a, sin_a = jnp.cos(small), jnp.sin(small), jnp.cos(large), jnp.sin(large)
    for block in range(frame // 128):
        at = slice(block * 128, block * 128 + 128)
        cos_k, sin_k = cos_a[:, block : block + 1], sin_a[:, block : block + 1]
        s.cos_t[:, at] = cos_b * cos_k - sin_b * sin_k
        s.sin_t[:, at] = sin_b * cos_k + cos_b * sin_k

    pl.semaphore_wait(barrier, places + 2)

    def id_copy(steps):
        if steps == 1:
            target = s.ids.at[:, pl.ds(LEAD, WINDOW)]
            source = ids_ref
        else:
            target = s.ids.at[:, pl.ds(0, LEAD)]
            source = ids_ref.at[:, pl.ds(count - LEAD, LEAD)]
        device = (place + steps) % places
        return remote(source, target, s.id_send.at[steps - 1], s.id_recv.at[steps - 1], {"seq": device})

    for steps in (1, 2):
        @pl.when(place + steps < places)
        def _():
            id_copy(steps).start()

    def column_copy(flip, device):
        return remote(
            fo_h.at[:, aligned(device * width, width, width)], s.cols.at[pl.ds(flip * width, width), :],
            s.col_send.at[flip], s.col_recv.at[flip], {"head": device},
        )

    column_copies = [column_copy(flip, device) for flip, device in ((1, sibling), (2, across), (3, diagonal))]
    for copy in column_copies:
        copy.start()

    loads["emb"].wait()
    level_in = normed(s.emb[...].astype(jnp.float32), fine_gain[...])

    def split(values):
        high = values.astype(jnp.bfloat16)
        return high, (values - high.astype(jnp.float32)).astype(jnp.bfloat16)

    loads["fk"].wait()
    s.tabs[0], s.tabs[1] = split(dot(level_in, s.fk[...]).T)
    loads["fv"].wait()
    s.tabs[2] = dot(level_in, s.fv[...]).T.astype(jnp.bfloat16)
    loads["fq"].wait()
    s.tabs[3], s.tabs[4] = split(dot(level_in, s.fq[...]).T)
    s.tabs[5] = s.emb[:, own_columns]

    def turned(joined, at):
        cosine, sine = s.cos_t[:, at], s.sin_t[:, at]
        pieces = []
        for head in range(heads):
            low = joined[head * HEAD_DIM : head * HEAD_DIM + HALF]
            high = joined[head * HEAD_DIM + HALF : (head + 1) * HEAD_DIM]
            pieces += [low * cosine - high * sine, high * cosine + low * sine]
        return jnp.concatenate(pieces, axis=0)

    def hot_rows(at, size):
        levels_at = lax.broadcasted_iota(jnp.int32, (256, size), 0)
        return jnp.where(levels_at == s.ids[:, at], 1.0, 0.0).astype(jnp.bfloat16)

    def key_rows(begin, size):
        at = aligned(begin, size, 128)
        hot = hot_rows(at, size)
        s.keys[at, :] = turned(dot(s.tabs[0], hot) + dot(s.tabs[1], hot), at).T.astype(jnp.bfloat16)
        s.values[:, at] = dot(s.tabs[2], hot).astype(jnp.bfloat16)

    def query_rows(begin, size):
        at = aligned(begin, size, 128)
        to = aligned(begin - WINDOW, size, 128)
        hot = hot_rows(at, size)
        s.query[:, to] = turned(dot(s.tabs[3], hot) + dot(s.tabs[4], hot), at).astype(jnp.bfloat16)
        s.start[to, :] = dot_tn(hot, s.tabs[5]).astype(jnp.bfloat16)

    own_block = min(512, count)

    def own_rows(index, state):
        key_rows(LEAD + WINDOW + index * own_block, own_block)
        query_rows(LEAD + WINDOW + index * own_block, own_block)
        return state

    def prior_rows(index, state):
        key_rows(index * 384, 384)
        return state

    lax.fori_loop(0, count // own_block, own_rows, 0)
    for steps in (1, 2):
        @pl.when(place >= steps)
        def _():
            id_copy(steps).wait_recv()

    lax.fori_loop(0, (LEAD + WINDOW) // 384, prior_rows, 0)
    query_rows(WINDOW, LEAD)

    def weigh(scores):
        top = scores[0]
        for piece in scores[1:]:
            top = jnp.maximum(top, piece)
        top = jnp.max(top, axis=0, keepdims=True)
        weights = [jnp.exp2((piece - top) * EXP2_SCALE) for piece in scores]
        total = weights[0]
        for piece in weights[1:]:
            total = total + piece
        total = jnp.sum(total, axis=0, keepdims=True)
        return jnp.concatenate([piece.astype(jnp.bfloat16) for piece in weights], axis=0), total

    def mixed_rows(chunk):
        return aligned(CARRY + chunk * chunk_rows, chunk_rows, CARRY)

    def mix_copies(chunk, at):
        def slot(which):
            return s.others.at[at, pl.ds((which - 1) * width, width)]

        def copy(kind, source, target, device):
            return remote(source, target, s.mix_send.at[kind, chunk], s.mix_recv.at[kind, chunk], {"head": device})

        return (
            copy(0, s.mixed.at[at, :], slot(2), across),
            copy(1, s.mixed.at[at, :], slot(1), sibling),
            copy(2, slot(2), slot(3), sibling),
        )

    carry_at = pl.ds(0, CARRY)
    carry_copies = mix_copies(chunks, carry_at)

    lane_slot = lax.broadcasted_iota(jnp.int32, (HEAD_DIM, LEAD), 1) // 32
    packed = []
    for head in range(heads):
        rolled = pltpu.roll(s.query[head * HEAD_DIM : (head + 1) * HEAD_DIM, :LEAD].astype(jnp.float32), (32 * head + 32) % LEAD, 1)
        packed.append(jnp.where(lane_slot == head, rolled, 0.0))
    packed = jnp.concatenate(packed, axis=0).astype(jnp.bfloat16)
    scores = dot(s.keys[: LEAD + WINDOW, :], packed)
    key = lax.broadcasted_iota(jnp.int32, scores.shape, 0)
    last = lax.broadcasted_iota(jnp.int32, scores.shape, 1) % 32 + (LEAD + WINDOW - 32)
    floor = jnp.where(place < 2, LEAD, 0)
    allowed = (key > last - WINDOW) & (key <= last) & (key >= floor)
    weights, total = weigh([jnp.where(allowed, scores, masked_low)])
    out = dot(s.values[:, : LEAD + WINDOW], weights) / total
    unpacked = [
        pltpu.roll(out[head * HEAD_DIM : (head + 1) * HEAD_DIM, :], (LEAD - 32 * head) % LEAD, 1) for head in range(heads)
    ]
    s.mixed[carry_at, :] = jnp.concatenate(unpacked, axis=0).T[32 - CARRY : 32, :].astype(jnp.bfloat16)
    carry_copies[0].start()
    carry_copies[1].start()

    row = lax.broadcasted_iota(jnp.int32, (chunk_rows, chunk_rows), 0)
    column = lax.broadcasted_iota(jnp.int32, (chunk_rows, chunk_rows), 1)
    row_head = lax.broadcasted_iota(jnp.int32, (width, chunk_rows), 0) // HEAD_DIM

    def attend_chunk(chunk):
        begin = chunk * chunk_rows
        floor = jnp.where(place == 0, WINDOW - begin, 0)
        key_at = aligned(LEAD + begin, span, 128)
        query = s.query[:, aligned(LEAD + begin, chunk_rows, chunk_rows)]
        outs = []
        for head in range(heads):
            scores = dot(s.keys[key_at, :], jnp.where(row_head == head, query, jnp.zeros_like(query)))
            pieces = []
            for at in range(0, span, chunk_rows):
                piece = scores[at : at + chunk_rows, :]
                if at == span - chunk_rows:
                    allowed = row <= column
                else:
                    allowed = row >= floor - at
                    if at == 0:
                        allowed = allowed & (row > column)
                pieces.append(jnp.where(allowed, piece, masked_low))
            weights, total = weigh(pieces)
            outs.append(dot(s.values[head * HEAD_DIM : (head + 1) * HEAD_DIM, key_at], weights) / total)
        at = mixed_rows(chunk)
        s.mixed[at, :] = jnp.concatenate(outs, axis=0).T.astype(jnp.bfloat16)
        copies = mix_copies(chunk, at)
        copies[0].start()
        copies[1].start()

    def fine_rows(at, start_at):
        merged = dot(s.mixed[at, :], s.cols[:width, :]) + dot(s.others[at, :], s.cols[width:, :])
        value = (s.start[start_at, :].astype(jnp.float32) + merged).astype(jnp.bfloat16).astype(jnp.float32)
        for block in range(lanes):
            s.stream[block, at, :] = value[:, block * 128 : block * 128 + 128]

    peers = (me, sibling, across)
    buffers = (s.send_a, s.recv_a, s.send_b, s.recv_b, s.final)
    short_sum = HeadSum(0, peers, s.part, s.short, buffers, s.sum_send, s.sum_recv)

    def short_rows(chunk):
        return aligned(chunk * group, group, group)

    def relay_chunk(chunk):
        @pl.when(chunk == 0)
        def _():
            carry_copies[0].wait_recv()
            carry_copies[2].start()

        copies = mix_copies(chunk, mixed_rows(chunk))
        copies[0].wait_recv()
        copies[2].start()

    def finish_chunk(chunk):
        @pl.when(chunk == 0)
        def _():
            for copy in column_copies:
                copy.wait_recv()
            loads["cols"].wait()
            loads["ws"].wait()
            carry_copies[1].wait_recv()
            carry_copies[2].wait_recv()
            fine_rows(carry_at, pl.ds(LEAD - CARRY, CARRY))

            @pl.when(place == 0)
            def _():
                s.stream[:, 0:CARRY, :] = jnp.zeros((lanes, CARRY, 128), jnp.float32)

        at = mixed_rows(chunk)
        copies = mix_copies(chunk, at)
        copies[1].wait_recv()
        copies[2].wait_recv()
        fine_rows(at, aligned(LEAD + chunk * chunk_rows, chunk_rows, chunk_rows))
        total = jnp.zeros((group, full), jnp.float32)
        for offset in range(SHORTEN):
            begin = CARRY - (SHORTEN - 1) + offset + chunk * chunk_rows
            member = jnp.concatenate(
                [s.stream[block, pl.ds(begin, group, stride=SHORTEN), :] for block in range(lanes)], axis=1
            )
            total = total + dot(member.astype(jnp.bfloat16), s.ws[offset])
        s.part[short_rows(chunk), :] = total
        short_sum.begin(chunk, short_rows(chunk))

    lane_f = lax.broadcasted_iota(jnp.int32, (rows, 128), 1) % HEAD_DIM
    period_f = periods(lane_f % HALF)
    angle_f = phase(place * rows + lax.broadcasted_iota(jnp.int32, (rows, 128), 0), period_f)
    cos_f = jnp.cos(angle_f)
    sin_f = jnp.where(lane_f < HALF, -jnp.sin(angle_f), jnp.sin(angle_f))
    for block in range(lanes):
        s.coarse_cos[:, block * 128 : block * 128 + 128] = cos_f
        s.coarse_sin[:, block * 128 : block * 128 + 128] = sin_f

    def pair_rows(chunk, source):
        return aligned((chunk * places + source) * group, group, group)

    def pair_copy(chunk, target):
        at = pair_rows(chunk, place)
        return remote(
            s.pair_out.at[target % 2, short_rows(chunk), :], s.pairs.at[at, :],
            s.pair_send.at[target, chunk], s.pair_recv.at[place, chunk], {"seq": target},
        )

    def pair_arrival(chunk, source):
        at = pair_rows(chunk, source)
        return remote(
            s.pairs.at[at, :], s.pairs.at[at, :], s.pair_send.at[source, chunk], s.pair_recv.at[source, chunk],
            {"seq": cross},
        )

    def query_copy(chunk):
        at = short_rows(chunk)
        return remote(
            s.query_out.at[1 - side, at, :], s.queries.at[aligned(side * rows + chunk * group, group, group), :],
            s.query_send.at[chunk], s.query_recv.at[chunk], {"seq": cross},
        )

    def for_targets(action):
        def one(index, state):
            target = places - 1 - index

            @pl.when(target != place)
            def _():
                action(target)

            return state

        lax.fori_loop(0, places - 2 * level, one, 0)

    def project_chunk(chunk):
        @pl.when(chunk == 0)
        def _():
            for name in ("cq", "ck", "cv"):
                loads[name].wait()

        at = short_rows(chunk)
        short_sum.end(chunk, at)
        coarse_in = normed(s.short[at, :].astype(jnp.float32), coarse_gain[...])
        cosine, sine = s.coarse_cos[at, :], s.coarse_sin[at, :]
        is_low = lax.broadcasted_iota(jnp.int32, (group, width), 1) % HEAD_DIM < HALF

        def rotated(values):
            other = jnp.where(is_low, pltpu.roll(values, width - HALF, 1), pltpu.roll(values, HALF, 1))
            return (values * cosine + other * sine).astype(jnp.bfloat16)

        key = rotated(dot(coarse_in, s.ck[...]))
        value = dot(coarse_in, s.cv[...]).astype(jnp.bfloat16)
        for half in range(2):
            s.pair_out[half, at, :pair] = key[:, half * pair : half * pair + pair]
            s.pair_out[half, at, pair:] = value[:, half * pair : half * pair + pair]
        for_targets(lambda target: pair_copy(chunk, target).start())
        query = rotated(dot(coarse_in, s.cq[...]))
        for half in range(2):
            s.query_out[half, at, :] = query[:, half * pair : half * pair + pair]
        query_copy(chunk).start()
        s.pairs[pair_rows(chunk, place), :] = s.pair_out[side, at, :]
        s.queries[aligned(side * rows + chunk * group, group, group), :] = s.query_out[side, at, :]

    stages = (
        (PROJECT, project_chunk),
        (TOTAL, lambda chunk: short_sum.total(chunk, short_rows(chunk))),
        (MIDDLE, lambda chunk: short_sum.middle(chunk, short_rows(chunk))),
        (FINISH, finish_chunk),
        (RELAY, relay_chunk),
    )

    def one_step(step, state):
        attend_chunk(step)
        for lag, action in stages:
            @pl.when(step >= lag)
            def _():
                action(step - lag)

        return state

    lax.fori_loop(0, chunks, one_step, 0)

    left = {action: max(0, chunks - lag) for lag, action in stages}
    project, total_up, middle_up, finish, relay = (action for _, action in stages)

    def rest(action, upto):
        for chunk in range(left[action], min(upto, chunks)):
            action(chunk)
        left[action] = max(left[action], min(upto, chunks))

    for action, upto in (
        (total_up, chunks - 5), (project, chunks - 6), (relay, chunks - 1), (total_up, chunks - 4), (project, chunks - 5),
        (finish, chunks - 2), (project, chunks - 4), (middle_up, chunks - 3), (relay, chunks), (finish, chunks - 1),
        (middle_up, chunks - 2), (finish, chunks), (middle_up, chunks - 1), (total_up, chunks - 3), (middle_up, chunks),
        (project, chunks - 3), (total_up, chunks - 2), (project, chunks - 2), (total_up, chunks - 1), (total_up, chunks),
        (project, chunks - 1), (project, chunks),
    ):
        rest(action, upto)

    def wait_chunk(chunk):
        def one(source, state):
            @pl.when(source != place)
            def _():
                pair_arrival(chunk, source).wait_recv()

            return state

        lax.fori_loop(0, 2 * level + 2, one, 0)

    def wait_queries(chunk, state):
        query_copy(chunk).wait_recv()
        return state

    lax.fori_loop(0, chunks, wait_queries, 0)

    s.top[...] = jnp.full(s.top.shape, masked_low, jnp.float32)
    s.norm[...] = jnp.zeros(s.norm.shape, jnp.float32)
    s.acc[...] = jnp.zeros(s.acc.shape, jnp.float32)
    per_chunk = places * group
    pair_lane = lax.broadcasted_iota(jnp.int32, (2 * rows, pair), 1) // HEAD_DIM
    queries = s.queries[...]

    def key_step(step, state):
        if per_chunk <= STEP_KEYS:
            for inner in range(STEP_KEYS // per_chunk):
                wait_chunk(step * (STEP_KEYS // per_chunk) + inner)
        else:
            ratio = per_chunk // STEP_KEYS

            @pl.when(step % ratio == 0)
            def _():
                wait_chunk(step // ratio)

        block = s.pairs[aligned(step * STEP_KEYS, STEP_KEYS, STEP_KEYS), :]
        keys, values = block[:, :pair], block[:, pair:]
        index = step * STEP_KEYS + lax.broadcasted_iota(jnp.int32, (STEP_KEYS, 1), 0)
        inside = index % per_chunk
        key_at = (inside // group) * rows + (index // per_chunk) * group + inside % group
        query_at = 2 * level * rows + lax.broadcasted_iota(jnp.int32, (1, 2 * rows), 1)
        allowed = key_at <= query_at
        values_t = values.astype(jnp.float32).T.astype(jnp.bfloat16)
        for head in range(pair // HEAD_DIM):
            masked_q = jnp.where(pair_lane == head, queries, jnp.zeros_like(queries))
            scores = jnp.where(allowed, dot_nt(keys, masked_q), masked_low)
            fresh = jnp.maximum(s.top[head], jnp.max(scores, axis=0, keepdims=True))
            factor = jnp.exp2((s.top[head] - fresh) * EXP2_SCALE)
            weights = jnp.exp2((scores - fresh) * EXP2_SCALE)
            s.norm[head] = s.norm[head] * factor + jnp.sum(weights, axis=0, keepdims=True)
            of = slice(head * HEAD_DIM, (head + 1) * HEAD_DIM)
            s.acc[of, :] = s.acc[of, :] * factor + dot(values_t[of, :], weights.astype(jnp.bfloat16))
            s.top[head] = fresh
        return state

    lax.fori_loop(0, places * rows // STEP_KEYS, key_step, 0)

    def turn_copy():
        return remote(
            s.turn, s.heads_in.at[:, aligned(side * pair, pair, pair)],
            s.turn_send.at[0], s.turn_recv.at[0], {"seq": cross},
        )

    def mixed_of(at):
        shares = [
            s.acc[head * HEAD_DIM : (head + 1) * HEAD_DIM, at] / s.norm[head, :, at] for head in range(pair // HEAD_DIM)
        ]
        return jnp.concatenate(shares, axis=0).T.astype(jnp.bfloat16)

    s.turn[...] = mixed_of(aligned((1 - side) * rows, rows, rows))
    turn_copy().start()
    s.heads_in[:, aligned(side * pair, pair, pair)] = mixed_of(aligned(side * rows, rows, rows))
    loads["co"].wait()
    turn_copy().wait_recv()

    out_sum = HeadSum(1, peers, s.part, s.summed, buffers, s.sum_send, s.sum_recv)
    ffn_sum = HeadSum(2, peers, s.part_b, s.second, buffers, s.sum_send, s.sum_recv)
    size = rows // PIECES
    at = [pl.ds(piece * size, size) for piece in range(PIECES)]

    for piece in range(PIECES):
        s.part[at[piece], :] = dot(s.heads_in[at[piece], :], s.co[...])
        out_sum.begin(piece, at[piece])
    for name in ("up", "down", "lift"):
        loads[name].wait()
    for piece in range(PIECES):
        out_sum.middle(piece, at[piece])

    def feed(piece):
        out_sum.end(piece, at[piece])
        value = s.short[at[piece], :].astype(jnp.float32) + s.summed[at[piece], :].astype(jnp.float32)
        s.first[at[piece], :] = value
        inner = jax.nn.gelu(dot(normed(value, ffn_gain[...]), s.up[...])).astype(jnp.bfloat16)
        s.part_b[at[piece], :] = dot(inner, s.down[...])
        ffn_sum.begin(piece, at[piece])

    def raise_rows(piece):
        ffn_sum.end(piece, at[piece])
        for member in range(SHORTEN):
            lifted = dot(s.second[at[piece], :], s.lift[:, member * width : (member + 1) * width])
            for block in range(lanes):
                s.spread[block, pl.ds(SHORTEN * size * piece + member, size, stride=SHORTEN), :] = lifted[
                    :, block * 128 : block * 128 + 128
                ]
        for block in range(lanes):
            to = slice(SHORTEN * size * piece, SHORTEN * size * (piece + 1))
            base_at = slice(CARRY + SHORTEN * size * piece, CARRY + SHORTEN * size * (piece + 1))
            out_ref[to, block * 128 : block * 128 + 128] = (
                s.stream[block, base_at, :] + s.spread[block, to, :]
            ).astype(jnp.bfloat16)

    for step in range(PIECES + 4):
        if step < PIECES:
            out_sum.total(step, at[step])
        if 0 <= step - 1 < PIECES:
            feed(step - 1)
        if 0 <= step - 2 < PIECES:
            ffn_sum.middle(step - 2, at[step - 2])
        if 0 <= step - 3 < PIECES:
            ffn_sum.total(step - 3, at[step - 3], s.first)
        if 0 <= step - 4 < PIECES:
            raise_rows(step - 4)

    for steps in (1, 2):
        @pl.when(place + steps < places)
        def _():
            id_copy(steps).wait_send()

    for copy in column_copies:
        copy.wait_send()
    for copy in carry_copies:
        copy.wait_send()

    def drain(chunk, state):
        for copy in mix_copies(chunk, mixed_rows(chunk)):
            copy.wait_send()
        short_sum.drain(chunk, short_rows(chunk))
        for_targets(lambda target: pair_copy(chunk, target).wait_send())
        query_copy(chunk).wait_send()
        return state

    lax.fori_loop(0, chunks, drain, 0)
    turn_copy().wait_send()
    for piece in range(PIECES):
        out_sum.drain(piece, at[piece])
        ffn_sum.drain(piece, at[piece])


def local(
    token_ids,
    embedding,
    fine_norm,
    fine_query,
    fine_key,
    fine_value,
    fine_output,
    shorten_weight,
    coarse_norm,
    coarse_query,
    coarse_key,
    coarse_value,
    coarse_output,
    ffn_norm,
    ffn_up,
    ffn_down,
    upsample_weight,
):
    count = token_ids.shape[0]
    width = fine_query.shape[1]
    chunk_rows = min(128, count)
    chunks = count // chunk_rows
    scratch = scratch_list(count, width, chunks, lax.axis_size("seq"))
    names = [name for name, _ in scratch]

    def kernel(*refs):
        block_kernel(names, chunk_rows, *refs)

    return pl.pallas_call(
        kernel,
        out_shape=jax.ShapeDtypeStruct((count, width), jnp.bfloat16),
        in_specs=[VMEM_SPEC] * 4 + [ANY_SPEC] * 13,
        out_specs=VMEM_SPEC,
        scratch_shapes=[shape for _, shape in scratch],
        compiler_params=pltpu.CompilerParams(
            collective_id=1, has_side_effects=True, vmem_limit_bytes=42 * 2**20
        ),
        name="block_kernel",
    )(
        token_ids.reshape(1, count),
        fine_norm.reshape(1, D),
        coarse_norm.reshape(1, D),
        ffn_norm.reshape(1, D),
        embedding,
        fine_query,
        fine_key,
        fine_value,
        fine_output,
        shorten_weight,
        coarse_query,
        coarse_key,
        coarse_value,
        coarse_output,
        ffn_up,
        ffn_down,
        upsample_weight.reshape(D, SHORTEN * width),
    )


def solution(mesh):
    return jax.shard_map(
        local,
        mesh=mesh,
        in_specs=(
            P("seq"),
            P(),
            P(),
            P(None, "head"),
            P(None, "head"),
            P(None, "head"),
            P("head", None),
            P(None, "head", None),
            P(),
            P(None, "head"),
            P(None, "head"),
            P(None, "head"),
            P("head", None),
            P(),
            P(None, "head"),
            P("head", None),
            P(None, None, "head"),
        ),
        out_specs=P("seq", "head"),
        check_vma=False,
    )
```

```python
import math

import jax
import jax.numpy as jnp
from jax import lax
from jax.experimental import pallas as pl
from jax.experimental.pallas import tpu as pltpu
from jax.sharding import PartitionSpec as P

D = 1024
HEAD_DIM = 64
HALF = HEAD_DIM // 2
SHORTEN = 4
WINDOW = 1024
LEAD = 128
CARRY = 16

epsilon = 1e-06
masked_low = -1e30
MESH = pl.DeviceIdType.MESH
EXP2_SCALE = HEAD_DIM ** (-0.5) * math.log2(math.e)
VMEM_SPEC = pl.BlockSpec(memory_space=pltpu.VMEM)
HBM_SPEC = pl.BlockSpec(memory_space=pltpu.HBM)

RELAY, FINISH, MIDDLE, TOTAL, PROJECT = (2, 3, 4, 6, 7)
STEP_KEYS = 512
PIECES = 2


def dot(left, right):
    return jnp.dot(left, right, preferred_element_type=jnp.float32)


def dot_nt(left, right):
    return lax.dot_general(left, right, (((1,), (1,)), ((), ())), preferred_element_type=jnp.float32)


def dot_tn(left, right):
    return lax.dot_general(left, right, (((0,), (0,)), ((), ())), preferred_element_type=jnp.float32)


def normed(data, gain):
    power = jnp.mean(data * data, axis=1, keepdims=True)
    return (data * lax.rsqrt(power + epsilon) * gain).astype(jnp.bfloat16)


def aligned(start, size, unit):
    return pl.ds(pl.multiple_of(start, unit), size)


def periods(column):
    log = 4 + lax.shift_right_logical(column * 14, 5)
    return jnp.left_shift(jnp.ones_like(log), log)


def phase(position, period):
    cycle = jnp.bitwise_and(position, period - 1).astype(jnp.float32)
    return cycle * (2.0 * math.pi / period.astype(jnp.float32))


def remote(source, target, send, receive, device):
    return pltpu.make_async_remote_copy(
        src_ref=source, dst_ref=target, send_sem=send, recv_sem=receive, device_id=device, device_id_type=MESH
    )


class HeadSum:
    def __init__(self, index, peers, part, out, buffers, send_sem, recv_sem):
        self.index = index
        self.me, self.sibling, self.across = peers
        self.part, self.out = part, out
        self.send_a, self.recv_a, self.send_b, self.recv_b, self.final = (buffer.at[index] for buffer in buffers)
        self.send_sem, self.recv_sem = send_sem, recv_sem
        half = part.shape[1] // 2
        self.mine = aligned((self.me % 2) * half, half, half)
        self.theirs = aligned((self.sibling % 2) * half, half, half)

    def copy(self, kind, piece, source, target, device):
        return remote(
            source, target, self.send_sem.at[self.index, kind, piece], self.recv_sem.at[self.index, kind, piece],
            {"head": device},
        )

    def copy_a(self, piece, at):
        return self.copy(0, piece, self.send_a.at[at, :], self.recv_a.at[at, :], self.sibling)

    def copy_b(self, piece, at):
        return self.copy(1, piece, self.send_b.at[at, :], self.recv_b.at[at, :], self.across)

    def copy_c(self, piece, at):
        return self.copy(2, piece, self.final.at[at, :], self.out.at[at, self.mine], self.sibling)

    def begin(self, piece, at):
        self.send_a[at, :] = self.part[at, self.theirs].astype(jnp.bfloat16)
        self.copy_a(piece, at).start()

    def middle(self, piece, at):
        self.copy_a(piece, at).wait_recv()
        summed = self.part[at, self.mine] + self.recv_a[at, :].astype(jnp.float32)
        self.part[at, self.mine] = summed
        self.send_b[at, :] = summed.astype(jnp.bfloat16)
        self.copy_b(piece, at).start()

    def total(self, piece, at, residual=None):
        self.copy_b(piece, at).wait_recv()
        value = self.part[at, self.mine] + self.recv_b[at, :].astype(jnp.float32)
        if residual is not None:
            value = value + residual[at, self.mine]
        value = value.astype(jnp.bfloat16)
        self.final[at, :] = value
        self.copy_c(piece, at).start()
        self.out[at, self.mine] = value

    def end(self, piece, at):
        self.copy_c(piece, at).wait_recv()

    def drain(self, piece, at):
        self.copy_a(piece, at).wait_send()
        self.copy_b(piece, at).wait_send()
        self.copy_c(piece, at).wait_send()


def scratch_list(count, width, chunks, places):
    full = 4 * width
    rows = count // SHORTEN
    frame = LEAD + WINDOW + count
    low = jnp.bfloat16
    wide = jnp.float32
    dma = pltpu.SemaphoreType.DMA
    return [
        ("emb", pltpu.VMEM((256, full), low)),
        ("fq", pltpu.VMEM((full, width), low)),
        ("fk", pltpu.VMEM((full, width), low)),
        ("fv", pltpu.VMEM((full, width), low)),
        ("cols", pltpu.VMEM((full, width), low)),
        ("ws", pltpu.VMEM((SHORTEN, width, full), low)),
        ("cq", pltpu.VMEM((full, width), low)),
        ("ck", pltpu.VMEM((full, width), low)),
        ("cv", pltpu.VMEM((full, width), low)),
        ("co", pltpu.VMEM((width, full), low)),
        ("up", pltpu.VMEM((full, full), low)),
        ("down", pltpu.VMEM((full, full), low)),
        ("lift", pltpu.VMEM((full, SHORTEN * width), low)),
        ("raw", pltpu.VMEM((width // 128, full, SHORTEN, 128), low)),
        ("fine_gain", pltpu.VMEM((1, full), wide)),
        ("coarse_gain", pltpu.VMEM((1, full), wide)),
        ("ffn_gain", pltpu.VMEM((1, full), wide)),
        ("load_sem", dma((17 + width // 128,))),
        ("ids", pltpu.VMEM((1, frame), jnp.int32)),
        ("id_send", dma((2,))),
        ("id_recv", dma((2,))),
        ("col_send", dma((4,))),
        ("col_recv", dma((4,))),
        ("tabs", pltpu.VMEM((6, 256, width), low)),
        ("cos_t", pltpu.VMEM((HALF, frame), wide)),
        ("sin_t", pltpu.VMEM((HALF, frame), wide)),
        ("keys", pltpu.VMEM((frame, width), low)),
        ("values", pltpu.VMEM((width, frame), low)),
        ("query", pltpu.VMEM((width, LEAD + count), low)),
        ("start", pltpu.VMEM((LEAD + count, width), low)),
        ("mixed", pltpu.VMEM((CARRY + count, width), low)),
        ("others", pltpu.VMEM((CARRY + count, 3 * width), low)),
        ("mix_send", dma((3, chunks + 1))),
        ("mix_recv", dma((3, chunks + 1))),
        ("stream", pltpu.VMEM((width // 128, CARRY + count, 128), wide)),
        ("part", pltpu.VMEM((rows, full), wide)),
        ("part_b", pltpu.VMEM((rows, full), wide)),
        ("short", pltpu.VMEM((rows, full), low)),
        ("summed", pltpu.VMEM((rows, full), low)),
        ("first", pltpu.VMEM((rows, full), wide)),
        ("second", pltpu.VMEM((rows, full), low)),
        ("send_a", pltpu.VMEM((3, rows, full // 2), low)),
        ("recv_a", pltpu.VMEM((3, rows, full // 2), low)),
        ("send_b", pltpu.VMEM((3, rows, full // 2), low)),
        ("recv_b", pltpu.VMEM((3, rows, full // 2), low)),
        ("final", pltpu.VMEM((3, rows, full // 2), low)),
        ("sum_send", dma((3, 3, chunks))),
        ("sum_recv", dma((3, 3, chunks))),
        ("coarse_cos", pltpu.VMEM((rows, width), wide)),
        ("coarse_sin", pltpu.VMEM((rows, width), wide)),
        ("pair_out", pltpu.VMEM((2, rows, width), low)),
        ("query_out", pltpu.VMEM((2, rows, width // 2), low)),
        ("pairs", pltpu.VMEM((places * rows, width), low)),
        ("queries", pltpu.VMEM((2 * rows, width // 2), low)),
        ("pair_send", dma((places, chunks))),
        ("pair_recv", dma((places, chunks))),
        ("query_send", dma((chunks,))),
        ("query_recv", dma((chunks,))),
        ("top", pltpu.VMEM((2, 1, 2 * rows), wide)),
        ("norm", pltpu.VMEM((2, 1, 2 * rows), wide)),
        ("acc", pltpu.VMEM((width // 2, 2 * rows), wide)),
        ("turn", pltpu.VMEM((rows, width // 2), low)),
        ("heads_in", pltpu.VMEM((rows, width), low)),
        ("turn_send", dma((1,))),
        ("turn_recv", dma((1,))),
        ("spread", pltpu.VMEM((width // 128, count, 128), wide)),
    ]


class Names:
    pass


def block_kernel(names, chunk_rows, *refs):
    (ids_h, fine_gain_h, coarse_gain_h, ffn_gain_h, emb_h, fq_h, fk_h, fv_h, fo_h, ws_h,
     cq_h, ck_h, cv_h, co_h, up_h, down_h, lift_h, out_ref) = refs[:18]
    s = Names()
    for name, ref in zip(names, refs[18:]):
        setattr(s, name, ref)
    count, width = out_ref.shape
    full = 4 * width
    heads = width // HEAD_DIM
    chunks = count // chunk_rows
    group = chunk_rows // SHORTEN
    rows = count // SHORTEN
    frame = LEAD + WINDOW + count
    span = WINDOW + chunk_rows
    lanes = width // 128
    pair = width // 2

    places = lax.axis_size("seq")
    place = lax.axis_index("seq")
    levels = places // 2
    side = place % 2
    level = place // 2
    cross = place + 1 - 2 * side
    me = lax.axis_index("head")
    sibling = me + 1 - 2 * (me % 2)
    across = (me + 2) % 4
    diagonal = (sibling + 2) % 4

    barrier = pltpu.get_barrier_semaphore()
    for device in (sibling, across, diagonal):
        pl.semaphore_signal(barrier, inc=1, device_id={"head": device}, device_id_type=MESH)

    def greet(step, state):
        pl.semaphore_signal(
            barrier, inc=1, device_id={"seq": (place + step) % places}, device_id_type=MESH
        )
        return state

    lax.fori_loop(1, places, greet, 0)

    own_columns = aligned(me * width, width, width)
    own_ids = s.ids.at[:, pl.ds(LEAD + WINDOW, count)]
    loads = {
        name: pltpu.make_async_copy(source, target, s.load_sem.at[index])
        for index, (name, source, target) in enumerate((
            ("ids", ids_h, own_ids), ("emb", emb_h, s.emb), ("fine_gain", fine_gain_h, s.fine_gain),
            ("fk", fk_h, s.fk), ("fv", fv_h, s.fv), ("fq", fq_h, s.fq),
            ("coarse_gain", coarse_gain_h, s.coarse_gain), ("ffn_gain", ffn_gain_h, s.ffn_gain),
            ("cols", fo_h.at[:, own_columns], s.cols.at[pl.ds(0, width), :]),
            ("ws", ws_h, s.ws), ("cq", cq_h, s.cq), ("ck", ck_h, s.ck), ("cv", cv_h, s.cv), ("co", co_h, s.co),
            ("up", up_h, s.up), ("down", down_h, s.down),
            *((f"lift{b}", lift_h.at[:, :, pl.ds(b * 128, 128)], s.raw.at[b]) for b in range(lanes)),
        ))
    }
    lift_names = tuple(f"lift{block}" for block in range(lanes))

    def start_loads(*names):
        for name in names:
            loads[name].start()

    start_loads("ids", "emb", "fine_gain", "fk", "fv", "fq")

    @pl.when(place < 1)
    def _():
        s.ids[:, LEAD : LEAD + WINDOW] = jnp.zeros((1, WINDOW), jnp.int32)

    @pl.when(place < 2)
    def _():
        s.ids[:, :LEAD] = jnp.zeros((1, LEAD), jnp.int32)

    def clear(index, state):
        chunk = index // (places - 2)
        blank = index % (places - 2)

        @pl.when(blank + 2 >= 2 * level + 2)
        def _():
            at = aligned((chunk * places + blank + 2) * group, group, group)
            s.pairs[at, :] = jnp.zeros((group, width), jnp.bfloat16)

        return state

    lax.fori_loop(0, chunks * (places - 2), clear, 0)

    column = lax.broadcasted_iota(jnp.int32, (HALF, 128), 0)
    lane = lax.broadcasted_iota(jnp.int32, (HALF, 128), 1)
    period = periods(column)
    small = phase(lane, period)
    base = (place - 1) * count - LEAD
    large = phase(base + 128 * lane, period)
    cos_b, sin_b, cos_a, sin_a = jnp.cos(small), jnp.sin(small), jnp.cos(large), jnp.sin(large)
    for block in range(frame // 128):
        at = slice(block * 128, block * 128 + 128)
        cos_k, sin_k = cos_a[:, block : block + 1], sin_a[:, block : block + 1]
        s.cos_t[:, at] = cos_b * cos_k - sin_b * sin_k
        s.sin_t[:, at] = sin_b * cos_k + cos_b * sin_k

    pl.semaphore_wait(barrier, places + 2)

    def id_copy(steps):
        if steps == 1:
            target = s.ids.at[:, pl.ds(LEAD, WINDOW)]
            source = ids_h
        else:
            target = s.ids.at[:, pl.ds(0, LEAD)]
            source = ids_h.at[:, pl.ds(count - LEAD, LEAD)]
        device = (place + steps) % places
        return remote(source, target, s.id_send.at[steps - 1], s.id_recv.at[steps - 1], {"seq": device})

    for steps in (1, 2):
        @pl.when(place + steps < places)
        def _():
            id_copy(steps).start()

    def column_copy(flip, device):
        return remote(
            fo_h.at[:, aligned(device * width, width, width)], s.cols.at[pl.ds(flip * width, width), :],
            s.col_send.at[flip], s.col_recv.at[flip], {"head": device},
        )

    column_copies = [column_copy(flip, device) for flip, device in ((1, sibling), (2, across), (3, diagonal))]
    for copy in column_copies:
        copy.start()

    loads["emb"].wait()
    loads["fine_gain"].wait()
    level_in = normed(s.emb[...].astype(jnp.float32), s.fine_gain[...])

    def split(values):
        high = values.astype(jnp.bfloat16)
        return high, (values - high.astype(jnp.float32)).astype(jnp.bfloat16)

    loads["fk"].wait()
    s.tabs[0], s.tabs[1] = split(dot(level_in, s.fk[...]).T)
    loads["fv"].wait()
    s.tabs[2] = dot(level_in, s.fv[...]).T.astype(jnp.bfloat16)
    loads["fq"].wait()
    s.tabs[3], s.tabs[4] = split(dot(level_in, s.fq[...]).T)
    s.tabs[5] = s.emb[:, own_columns]
    loads["ids"].wait()
    start_loads("cols", "ws", "coarse_gain", "ffn_gain", "cq", "ck", "cv")

    def turned(joined, at):
        cosine, sine = s.cos_t[:, at], s.sin_t[:, at]
        pieces = []
        for head in range(heads):
            low = joined[head * HEAD_DIM : head * HEAD_DIM + HALF]
            high = joined[head * HEAD_DIM + HALF : (head + 1) * HEAD_DIM]
            pieces += [low * cosine - high * sine, high * cosine + low * sine]
        return jnp.concatenate(pieces, axis=0)

    def hot_rows(at, size):
        levels_at = lax.broadcasted_iota(jnp.int32, (256, size), 0)
        return jnp.where(levels_at == s.ids[:, at], 1.0, 0.0).astype(jnp.bfloat16)

    def key_rows(begin, size):
        at = aligned(begin, size, 128)
        hot = hot_rows(at, size)
        s.keys[at, :] = turned(dot(s.tabs[0], hot) + dot(s.tabs[1], hot), at).T.astype(jnp.bfloat16)
        s.values[:, at] = dot(s.tabs[2], hot).astype(jnp.bfloat16)

    def query_rows(begin, size):
        at = aligned(begin, size, 128)
        to = aligned(begin - WINDOW, size, 128)
        hot = hot_rows(at, size)
        s.query[:, to] = turned(dot(s.tabs[3], hot) + dot(s.tabs[4], hot), at).astype(jnp.bfloat16)
        s.start[to, :] = dot_tn(hot, s.tabs[5]).astype(jnp.bfloat16)

    own_block = min(512, count)

    def own_rows(index, state):
        key_rows(LEAD + WINDOW + index * own_block, own_block)
        query_rows(LEAD + WINDOW + index * own_block, own_block)
        return state

    def prior_rows(index, state):
        key_rows(index * 384, 384)
        return state

    lax.fori_loop(0, count // own_block, own_rows, 0)
    for steps in (1, 2):
        @pl.when(place >= steps)
        def _():
            id_copy(steps).wait_recv()

    lax.fori_loop(0, (LEAD + WINDOW) // 384, prior_rows, 0)
    query_rows(WINDOW, LEAD)

    def weigh(scores):
        top = scores[0]
        for piece in scores[1:]:
            top = jnp.maximum(top, piece)
        top = jnp.max(top, axis=0, keepdims=True)
        weights = [jnp.exp2((piece - top) * EXP2_SCALE) for piece in scores]
        total = weights[0]
        for piece in weights[1:]:
            total = total + piece
        total = jnp.sum(total, axis=0, keepdims=True)
        return jnp.concatenate([piece.astype(jnp.bfloat16) for piece in weights], axis=0), total

    def mixed_rows(chunk):
        return aligned(CARRY + chunk * chunk_rows, chunk_rows, CARRY)

    def mix_copies(chunk, at):
        def slot(which):
            return s.others.at[at, pl.ds((which - 1) * width, width)]

        def copy(kind, source, target, device):
            return remote(source, target, s.mix_send.at[kind, chunk], s.mix_recv.at[kind, chunk], {"head": device})

        return (
            copy(0, s.mixed.at[at, :], slot(2), across),
            copy(1, s.mixed.at[at, :], slot(1), sibling),
            copy(2, slot(2), slot(3), sibling),
        )

    carry_at = pl.ds(0, CARRY)
    carry_copies = mix_copies(chunks, carry_at)

    start_loads("co", "up", "down", *lift_names)

    lane_slot = lax.broadcasted_iota(jnp.int32, (HEAD_DIM, LEAD), 1) // 32
    packed = []
    for head in range(heads):
        rolled = pltpu.roll(s.query[head * HEAD_DIM : (head + 1) * HEAD_DIM, :LEAD].astype(jnp.float32), (32 * head + 32) % LEAD, 1)
        packed.append(jnp.where(lane_slot == head, rolled, 0.0))
    packed = jnp.concatenate(packed, axis=0).astype(jnp.bfloat16)
    scores = dot(s.keys[: LEAD + WINDOW, :], packed)
    key = lax.broadcasted_iota(jnp.int32, scores.shape, 0)
    last = lax.broadcasted_iota(jnp.int32, scores.shape, 1) % 32 + (LEAD + WINDOW - 32)
    floor = jnp.where(place < 2, LEAD, 0)
    allowed = (key > last - WINDOW) & (key <= last) & (key >= floor)
    weights, total = weigh([jnp.where(allowed, scores, masked_low)])
    out = dot(s.values[:, : LEAD + WINDOW], weights) / total
    unpacked = [
        pltpu.roll(out[head * HEAD_DIM : (head + 1) * HEAD_DIM, :], (LEAD - 32 * head) % LEAD, 1) for head in range(heads)
    ]
    s.mixed[carry_at, :] = jnp.concatenate(unpacked, axis=0).T[32 - CARRY : 32, :].astype(jnp.bfloat16)
    carry_copies[0].start()
    carry_copies[1].start()

    row = lax.broadcasted_iota(jnp.int32, (chunk_rows, chunk_rows), 0)
    column = lax.broadcasted_iota(jnp.int32, (chunk_rows, chunk_rows), 1)
    row_head = lax.broadcasted_iota(jnp.int32, (width, chunk_rows), 0) // HEAD_DIM

    def attend_chunk(chunk):
        begin = chunk * chunk_rows
        floor = jnp.where(place == 0, WINDOW - begin, 0)
        key_at = aligned(LEAD + begin, span, 128)
        query = s.query[:, aligned(LEAD + begin, chunk_rows, chunk_rows)]
        outs = []
        for head in range(heads):
            scores = dot(s.keys[key_at, :], jnp.where(row_head == head, query, jnp.zeros_like(query)))
            pieces = []
            for at in range(0, span, chunk_rows):
                piece = scores[at : at + chunk_rows, :]
                if at == span - chunk_rows:
                    allowed = row <= column
                else:
                    allowed = row >= floor - at
                    if at == 0:
                        allowed = allowed & (row > column)
                pieces.append(jnp.where(allowed, piece, masked_low))
            weights, total = weigh(pieces)
            outs.append(dot(s.values[head * HEAD_DIM : (head + 1) * HEAD_DIM, key_at], weights) / total)
        at = mixed_rows(chunk)
        s.mixed[at, :] = jnp.concatenate(outs, axis=0).T.astype(jnp.bfloat16)
        copies = mix_copies(chunk, at)
        copies[0].start()
        copies[1].start()

    def fine_rows(at, start_at):
        merged = dot(s.mixed[at, :], s.cols[:width, :]) + dot(s.others[at, :], s.cols[width:, :])
        value = (s.start[start_at, :].astype(jnp.float32) + merged).astype(jnp.bfloat16).astype(jnp.float32)
        for block in range(lanes):
            s.stream[block, at, :] = value[:, block * 128 : block * 128 + 128]

    peers = (me, sibling, across)
    buffers = (s.send_a, s.recv_a, s.send_b, s.recv_b, s.final)
    short_sum = HeadSum(0, peers, s.part, s.short, buffers, s.sum_send, s.sum_recv)

    def short_rows(chunk):
        return aligned(chunk * group, group, group)

    def relay_chunk(chunk):
        @pl.when(chunk == 0)
        def _():
            carry_copies[0].wait_recv()
            carry_copies[2].start()

        copies = mix_copies(chunk, mixed_rows(chunk))
        copies[0].wait_recv()
        copies[2].start()

    def finish_chunk(chunk):
        @pl.when(chunk == 0)
        def _():
            for copy in column_copies:
                copy.wait_recv()
            loads["cols"].wait()
            loads["ws"].wait()
            carry_copies[1].wait_recv()
            carry_copies[2].wait_recv()
            fine_rows(carry_at, pl.ds(LEAD - CARRY, CARRY))

            @pl.when(place == 0)
            def _():
                s.stream[:, 0:CARRY, :] = jnp.zeros((lanes, CARRY, 128), jnp.float32)

        at = mixed_rows(chunk)
        copies = mix_copies(chunk, at)
        copies[1].wait_recv()
        copies[2].wait_recv()
        fine_rows(at, aligned(LEAD + chunk * chunk_rows, chunk_rows, chunk_rows))
        total = jnp.zeros((group, full), jnp.float32)
        for offset in range(SHORTEN):
            begin = CARRY - (SHORTEN - 1) + offset + chunk * chunk_rows
            member = jnp.concatenate(
                [s.stream[block, pl.ds(begin, group, stride=SHORTEN), :] for block in range(lanes)], axis=1
            )
            total = total + dot(member.astype(jnp.bfloat16), s.ws[offset])
        s.part[short_rows(chunk), :] = total
        short_sum.begin(chunk, short_rows(chunk))

    lane_f = lax.broadcasted_iota(jnp.int32, (rows, 128), 1) % HEAD_DIM
    period_f = periods(lane_f % HALF)
    angle_f = phase(place * rows + lax.broadcasted_iota(jnp.int32, (rows, 128), 0), period_f)
    cos_f = jnp.cos(angle_f)
    sin_f = jnp.where(lane_f < HALF, -jnp.sin(angle_f), jnp.sin(angle_f))
    for block in range(lanes):
        s.coarse_cos[:, block * 128 : block * 128 + 128] = cos_f
        s.coarse_sin[:, block * 128 : block * 128 + 128] = sin_f

    def pair_rows(chunk, source):
        return aligned((chunk * places + source) * group, group, group)

    def pair_copy(chunk, target):
        at = pair_rows(chunk, place)
        return remote(
            s.pair_out.at[target % 2, short_rows(chunk), :], s.pairs.at[at, :],
            s.pair_send.at[target, chunk], s.pair_recv.at[place, chunk], {"seq": target},
        )

    def pair_arrival(chunk, source):
        at = pair_rows(chunk, source)
        return remote(
            s.pairs.at[at, :], s.pairs.at[at, :], s.pair_send.at[source, chunk], s.pair_recv.at[source, chunk],
            {"seq": cross},
        )

    def query_copy(chunk):
        at = short_rows(chunk)
        return remote(
            s.query_out.at[1 - side, at, :], s.queries.at[aligned(side * rows + chunk * group, group, group), :],
            s.query_send.at[chunk], s.query_recv.at[chunk], {"seq": cross},
        )

    def for_targets(action):
        def one(index, state):
            target = places - 1 - index

            @pl.when(target != place)
            def _():
                action(target)

            return state

        lax.fori_loop(0, places - 2 * level, one, 0)

    def project_chunk(chunk):
        @pl.when(chunk == 0)
        def _():
            for name in ("coarse_gain", "cq", "ck", "cv"):
                loads[name].wait()

        at = short_rows(chunk)
        short_sum.end(chunk, at)
        coarse_in = normed(s.short[at, :].astype(jnp.float32), s.coarse_gain[...])
        cosine, sine = s.coarse_cos[at, :], s.coarse_sin[at, :]
        is_low = lax.broadcasted_iota(jnp.int32, (group, width), 1) % HEAD_DIM < HALF

        def rotated(values):
            other = jnp.where(is_low, pltpu.roll(values, width - HALF, 1), pltpu.roll(values, HALF, 1))
            return (values * cosine + other * sine).astype(jnp.bfloat16)

        key = rotated(dot(coarse_in, s.ck[...]))
        value = dot(coarse_in, s.cv[...]).astype(jnp.bfloat16)
        for half in range(2):
            s.pair_out[half, at, :pair] = key[:, half * pair : half * pair + pair]
            s.pair_out[half, at, pair:] = value[:, half * pair : half * pair + pair]
        for_targets(lambda target: pair_copy(chunk, target).start())
        query = rotated(dot(coarse_in, s.cq[...]))
        for half in range(2):
            s.query_out[half, at, :] = query[:, half * pair : half * pair + pair]
        query_copy(chunk).start()
        s.pairs[pair_rows(chunk, place), :] = s.pair_out[side, at, :]
        s.queries[aligned(side * rows + chunk * group, group, group), :] = s.query_out[side, at, :]

    stages = (
        (PROJECT, project_chunk),
        (TOTAL, lambda chunk: short_sum.total(chunk, short_rows(chunk))),
        (MIDDLE, lambda chunk: short_sum.middle(chunk, short_rows(chunk))),
        (FINISH, finish_chunk),
        (RELAY, relay_chunk),
    )

    def one_step(step, state):
        attend_chunk(step)
        for lag, action in stages:
            @pl.when(step >= lag)
            def _():
                action(step - lag)

        return state

    lax.fori_loop(0, chunks, one_step, 0)

    left = {action: max(0, chunks - lag) for lag, action in stages}
    project, total_up, middle_up, finish, relay = (action for _, action in stages)

    def rest(action, upto):
        for chunk in range(left[action], min(upto, chunks)):
            action(chunk)
        left[action] = max(left[action], min(upto, chunks))

    for action, upto in (
        (total_up, chunks - 5), (project, chunks - 6), (relay, chunks - 1), (total_up, chunks - 4), (project, chunks - 5),
        (finish, chunks - 2), (project, chunks - 4), (middle_up, chunks - 3), (relay, chunks), (finish, chunks - 1),
        (middle_up, chunks - 2), (finish, chunks), (middle_up, chunks - 1), (total_up, chunks - 3), (middle_up, chunks),
        (project, chunks - 3), (total_up, chunks - 2), (project, chunks - 2), (total_up, chunks - 1), (total_up, chunks),
        (project, chunks - 1), (project, chunks),
    ):
        rest(action, upto)

    def wait_chunk(chunk):
        def one(source, state):
            @pl.when(source != place)
            def _():
                pair_arrival(chunk, source).wait_recv()

            return state

        lax.fori_loop(0, 2 * level + 2, one, 0)

    for name in lift_names:
        loads[name].wait()
    part_rows = count // SHORTEN
    for block in range(lanes):
        for begin in range(0, full, part_rows):
            flat = s.raw.at[block, pl.ds(begin, part_rows)].reshape(part_rows * SHORTEN, 128)
            s.spread[block] = flat[...].astype(jnp.float32)
            for member in range(SHORTEN):
                s.lift[begin : begin + part_rows, member * width + block * 128 : member * width + block * 128 + 128] = (
                    s.spread[block, pl.ds(member, part_rows, stride=SHORTEN), :].astype(jnp.bfloat16)
                )

    def wait_queries(chunk, state):
        query_copy(chunk).wait_recv()
        return state

    lax.fori_loop(0, chunks, wait_queries, 0)

    s.top[...] = jnp.full(s.top.shape, masked_low, jnp.float32)
    s.norm[...] = jnp.zeros(s.norm.shape, jnp.float32)
    s.acc[...] = jnp.zeros(s.acc.shape, jnp.float32)
    per_chunk = places * group
    pair_lane = lax.broadcasted_iota(jnp.int32, (2 * rows, pair), 1) // HEAD_DIM
    queries = s.queries[...]

    def key_step(step, state):
        if per_chunk <= STEP_KEYS:
            for inner in range(STEP_KEYS // per_chunk):
                wait_chunk(step * (STEP_KEYS // per_chunk) + inner)
        else:
            ratio = per_chunk // STEP_KEYS

            @pl.when(step % ratio == 0)
            def _():
                wait_chunk(step // ratio)

        block = s.pairs[aligned(step * STEP_KEYS, STEP_KEYS, STEP_KEYS), :]
        keys, values = block[:, :pair], block[:, pair:]
        index = step * STEP_KEYS + lax.broadcasted_iota(jnp.int32, (STEP_KEYS, 1), 0)
        inside = index % per_chunk
        key_at = (inside // group) * rows + (index // per_chunk) * group + inside % group
        query_at = 2 * level * rows + lax.broadcasted_iota(jnp.int32, (1, 2 * rows), 1)
        allowed = key_at <= query_at
        values_t = values.astype(jnp.float32).T.astype(jnp.bfloat16)
        for head in range(pair // HEAD_DIM):
            masked_q = jnp.where(pair_lane == head, queries, jnp.zeros_like(queries))
            scores = jnp.where(allowed, dot_nt(keys, masked_q), masked_low)
            fresh = jnp.maximum(s.top[head], jnp.max(scores, axis=0, keepdims=True))
            factor = jnp.exp2((s.top[head] - fresh) * EXP2_SCALE)
            weights = jnp.exp2((scores - fresh) * EXP2_SCALE)
            s.norm[head] = s.norm[head] * factor + jnp.sum(weights, axis=0, keepdims=True)
            of = slice(head * HEAD_DIM, (head + 1) * HEAD_DIM)
            s.acc[of, :] = s.acc[of, :] * factor + dot(values_t[of, :], weights.astype(jnp.bfloat16))
            s.top[head] = fresh
        return state

    lax.fori_loop(0, places * rows // STEP_KEYS, key_step, 0)

    def turn_copy():
        return remote(
            s.turn, s.heads_in.at[:, aligned(side * pair, pair, pair)],
            s.turn_send.at[0], s.turn_recv.at[0], {"seq": cross},
        )

    def mixed_of(at):
        shares = [
            s.acc[head * HEAD_DIM : (head + 1) * HEAD_DIM, at] / s.norm[head, :, at] for head in range(pair // HEAD_DIM)
        ]
        return jnp.concatenate(shares, axis=0).T.astype(jnp.bfloat16)

    s.turn[...] = mixed_of(aligned((1 - side) * rows, rows, rows))
    turn_copy().start()
    s.heads_in[:, aligned(side * pair, pair, pair)] = mixed_of(aligned(side * rows, rows, rows))
    loads["co"].wait()
    turn_copy().wait_recv()

    out_sum = HeadSum(1, peers, s.part, s.summed, buffers, s.sum_send, s.sum_recv)
    ffn_sum = HeadSum(2, peers, s.part_b, s.second, buffers, s.sum_send, s.sum_recv)
    size = rows // PIECES
    at = [pl.ds(piece * size, size) for piece in range(PIECES)]

    for piece in range(PIECES):
        s.part[at[piece], :] = dot(s.heads_in[at[piece], :], s.co[...])
        out_sum.begin(piece, at[piece])
    for name in ("ffn_gain", "up", "down"):
        loads[name].wait()
    for piece in range(PIECES):
        out_sum.middle(piece, at[piece])

    def feed(piece):
        out_sum.end(piece, at[piece])
        value = s.short[at[piece], :].astype(jnp.float32) + s.summed[at[piece], :].astype(jnp.float32)
        s.first[at[piece], :] = value
        inner = jax.nn.gelu(dot(normed(value, s.ffn_gain[...]), s.up[...])).astype(jnp.bfloat16)
        s.part_b[at[piece], :] = dot(inner, s.down[...])
        ffn_sum.begin(piece, at[piece])

    def raise_rows(piece):
        ffn_sum.end(piece, at[piece])
        for member in range(SHORTEN):
            lifted = dot(s.second[at[piece], :], s.lift[:, member * width : (member + 1) * width])
            for block in range(lanes):
                s.spread[block, pl.ds(SHORTEN * size * piece + member, size, stride=SHORTEN), :] = lifted[
                    :, block * 128 : block * 128 + 128
                ]
        for block in range(lanes):
            to = slice(SHORTEN * size * piece, SHORTEN * size * (piece + 1))
            base_at = slice(CARRY + SHORTEN * size * piece, CARRY + SHORTEN * size * (piece + 1))
            out_ref[to, block * 128 : block * 128 + 128] = (
                s.stream[block, base_at, :] + s.spread[block, to, :]
            ).astype(jnp.bfloat16)

    for step in range(PIECES + 4):
        if step < PIECES:
            out_sum.total(step, at[step])
        if 0 <= step - 1 < PIECES:
            feed(step - 1)
        if 0 <= step - 2 < PIECES:
            ffn_sum.middle(step - 2, at[step - 2])
        if 0 <= step - 3 < PIECES:
            ffn_sum.total(step - 3, at[step - 3], s.first)
        if 0 <= step - 4 < PIECES:
            raise_rows(step - 4)

    for steps in (1, 2):
        @pl.when(place + steps < places)
        def _():
            id_copy(steps).wait_send()

    for copy in column_copies:
        copy.wait_send()
    for copy in carry_copies:
        copy.wait_send()

    def drain(chunk, state):
        for copy in mix_copies(chunk, mixed_rows(chunk)):
            copy.wait_send()
        short_sum.drain(chunk, short_rows(chunk))
        for_targets(lambda target: pair_copy(chunk, target).wait_send())
        query_copy(chunk).wait_send()
        return state

    lax.fori_loop(0, chunks, drain, 0)
    turn_copy().wait_send()
    for piece in range(PIECES):
        out_sum.drain(piece, at[piece])
        ffn_sum.drain(piece, at[piece])


def local(
    token_ids,
    embedding,
    fine_norm,
    fine_query,
    fine_key,
    fine_value,
    fine_output,
    shorten_weight,
    coarse_norm,
    coarse_query,
    coarse_key,
    coarse_value,
    coarse_output,
    ffn_norm,
    ffn_up,
    ffn_down,
    upsample_weight,
):
    count = token_ids.shape[0]
    width = fine_query.shape[1]
    chunk_rows = min(128, count)
    chunks = count // chunk_rows
    scratch = scratch_list(count, width, chunks, lax.axis_size("seq"))
    names = [name for name, _ in scratch]

    def kernel(*refs):
        block_kernel(names, chunk_rows, *refs)

    return pl.pallas_call(
        kernel,
        out_shape=jax.ShapeDtypeStruct((count, width), jnp.bfloat16),
        in_specs=[HBM_SPEC] * 17,
        out_specs=VMEM_SPEC,
        scratch_shapes=[shape for _, shape in scratch],
        compiler_params=pltpu.CompilerParams(
            collective_id=1, has_side_effects=True, vmem_limit_bytes=42 * 2**20
        ),
        name="block_kernel",
    )(
        *(
            pltpu.with_memory_space_constraint(array, pltpu.HBM)
            for array in (
                token_ids.reshape(1, count), fine_norm.reshape(1, D), coarse_norm.reshape(1, D), ffn_norm.reshape(1, D),
                embedding, fine_query, fine_key, fine_value, fine_output, shorten_weight, coarse_query, coarse_key,
                coarse_value, coarse_output, ffn_up, ffn_down, upsample_weight,
            )
        ),
    )


def solution(mesh):
    return jax.shard_map(
        local,
        mesh=mesh,
        in_specs=(
            P("seq"),
            P(),
            P(),
            P(None, "head"),
            P(None, "head"),
            P(None, "head"),
            P("head", None),
            P(None, "head", None),
            P(),
            P(None, "head"),
            P(None, "head"),
            P(None, "head"),
            P("head", None),
            P(),
            P(None, "head"),
            P("head", None),
            P(None, None, "head"),
        ),
        out_specs=P("seq", "head"),
        check_vma=False,
    )
```

```python
import math

import jax
import jax.numpy as jnp
from jax import lax
from jax.experimental import pallas as pl
from jax.experimental.pallas import tpu as pltpu
from jax.sharding import PartitionSpec as P

D = 1024
HEAD_DIM = 64
HALF = HEAD_DIM // 2
SHORTEN = 4
WINDOW = 1024
LEAD = 128
CARRY = 16

epsilon = 1e-06
masked_low = -1e30
MESH = pl.DeviceIdType.MESH
EXP2_SCALE = HEAD_DIM ** (-0.5) * math.log2(math.e)
VMEM_SPEC = pl.BlockSpec(memory_space=pltpu.VMEM)
HBM_SPEC = pl.BlockSpec(memory_space=pltpu.HBM)

RELAY, FINISH, MIDDLE, TOTAL, PROJECT = (2, 3, 4, 6, 7)
STEP_KEYS = 512
PIECES = 2


def dot(left, right):
    return jnp.dot(left, right, preferred_element_type=jnp.float32)


def dot_nt(left, right):
    return lax.dot_general(left, right, (((1,), (1,)), ((), ())), preferred_element_type=jnp.float32)


def dot_tn(left, right):
    return lax.dot_general(left, right, (((0,), (0,)), ((), ())), preferred_element_type=jnp.float32)


def normed(data, gain):
    power = jnp.mean(data * data, axis=1, keepdims=True)
    return (data * lax.rsqrt(power + epsilon) * gain).astype(jnp.bfloat16)


def aligned(start, size, unit):
    return pl.ds(pl.multiple_of(start, unit), size)


def periods(column):
    log = 4 + lax.shift_right_logical(column * 14, 5)
    return jnp.left_shift(jnp.ones_like(log), log)


def phase(position, period):
    cycle = jnp.bitwise_and(position, period - 1).astype(jnp.float32)
    return cycle * (2.0 * math.pi / period.astype(jnp.float32))


def remote(source, target, send, receive, device):
    return pltpu.make_async_remote_copy(
        src_ref=source, dst_ref=target, send_sem=send, recv_sem=receive, device_id=device, device_id_type=MESH
    )


class HeadSum:
    def __init__(self, index, peers, part, out, buffers, send_sem, recv_sem):
        self.index = index
        self.me, self.sibling, self.across = peers
        self.part, self.out = part, out
        self.send_a, self.recv_a, self.send_b, self.recv_b, self.final = (buffer.at[index] for buffer in buffers)
        self.send_sem, self.recv_sem = send_sem, recv_sem
        half = part.shape[1] // 2
        self.mine = aligned((self.me % 2) * half, half, half)
        self.theirs = aligned((self.sibling % 2) * half, half, half)

    def copy(self, kind, piece, source, target, device):
        return remote(
            source, target, self.send_sem.at[self.index, kind, piece], self.recv_sem.at[self.index, kind, piece],
            {"head": device},
        )

    def copy_a(self, piece, at):
        return self.copy(0, piece, self.send_a.at[at, :], self.recv_a.at[at, :], self.sibling)

    def copy_b(self, piece, at):
        return self.copy(1, piece, self.send_b.at[at, :], self.recv_b.at[at, :], self.across)

    def copy_c(self, piece, at):
        return self.copy(2, piece, self.final.at[at, :], self.out.at[at, self.mine], self.sibling)

    def begin(self, piece, at):
        self.send_a[at, :] = self.part[at, self.theirs].astype(jnp.bfloat16)
        self.copy_a(piece, at).start()

    def middle(self, piece, at):
        self.copy_a(piece, at).wait_recv()
        summed = self.part[at, self.mine] + self.recv_a[at, :].astype(jnp.float32)
        self.part[at, self.mine] = summed
        self.send_b[at, :] = summed.astype(jnp.bfloat16)
        self.copy_b(piece, at).start()

    def total(self, piece, at, residual=None):
        self.copy_b(piece, at).wait_recv()
        value = self.part[at, self.mine] + self.recv_b[at, :].astype(jnp.float32)
        if residual is not None:
            value = value + residual[at, self.mine]
        value = value.astype(jnp.bfloat16)
        self.final[at, :] = value
        self.copy_c(piece, at).start()
        self.out[at, self.mine] = value

    def end(self, piece, at):
        self.copy_c(piece, at).wait_recv()

    def drain(self, piece, at):
        self.copy_a(piece, at).wait_send()
        self.copy_b(piece, at).wait_send()
        self.copy_c(piece, at).wait_send()


def scratch_list(count, width, chunks, places):
    full = 4 * width
    rows = count // SHORTEN
    frame = LEAD + WINDOW + count
    low = jnp.bfloat16
    wide = jnp.float32
    dma = pltpu.SemaphoreType.DMA
    return [
        ("emb", pltpu.VMEM((256, full), low)),
        ("fq", pltpu.VMEM((full, width), low)),
        ("fk", pltpu.VMEM((full, width), low)),
        ("fv", pltpu.VMEM((full, width), low)),
        ("cols", pltpu.VMEM((full, width), low)),
        ("ws", pltpu.VMEM((SHORTEN, width, full), low)),
        ("cq", pltpu.VMEM((full, width), low)),
        ("ck", pltpu.VMEM((full, width), low)),
        ("cv", pltpu.VMEM((full, width), low)),
        ("co", pltpu.VMEM((width, full), low)),
        ("up", pltpu.VMEM((full, full), low)),
        ("down", pltpu.VMEM((full, full), low)),
        ("lift", pltpu.VMEM((full, SHORTEN * width), low)),
        ("raw", pltpu.VMEM((width // 128, full, SHORTEN, 128), low)),
        ("fine_gain", pltpu.VMEM((1, full), wide)),
        ("coarse_gain", pltpu.VMEM((1, full), wide)),
        ("ffn_gain", pltpu.VMEM((1, full), wide)),
        ("load_sem", dma((17 + width // 128,))),
        ("ids", pltpu.VMEM((1, frame), jnp.int32)),
        ("id_send", dma((2,))),
        ("id_recv", dma((2,))),
        ("col_send", dma((4,))),
        ("col_recv", dma((4,))),
        ("tabs", pltpu.VMEM((6, 256, width), low)),
        ("cos_t", pltpu.VMEM((HALF, frame), wide)),
        ("sin_t", pltpu.VMEM((HALF, frame), wide)),
        ("keys", pltpu.VMEM((frame, width), low)),
        ("values", pltpu.VMEM((width, frame), low)),
        ("query", pltpu.VMEM((width, LEAD + count), low)),
        ("start", pltpu.VMEM((LEAD + count, width), low)),
        ("scores", pltpu.VMEM((WINDOW + count // chunks, 4 * (count // chunks)), wide)),
        ("weights", pltpu.VMEM((WINDOW + count // chunks, 4 * (count // chunks)), low)),
        ("mixed", pltpu.VMEM((CARRY + count, width), low)),
        ("others", pltpu.VMEM((CARRY + count, 3 * width), low)),
        ("mix_send", dma((3, chunks + 1))),
        ("mix_recv", dma((3, chunks + 1))),
        ("stream", pltpu.VMEM((width // 128, CARRY + count, 128), wide)),
        ("part", pltpu.VMEM((rows, full), wide)),
        ("part_b", pltpu.VMEM((rows, full), wide)),
        ("short", pltpu.VMEM((rows, full), low)),
        ("summed", pltpu.VMEM((rows, full), low)),
        ("first", pltpu.VMEM((rows, full), wide)),
        ("second", pltpu.VMEM((rows, full), low)),
        ("send_a", pltpu.VMEM((3, rows, full // 2), low)),
        ("recv_a", pltpu.VMEM((3, rows, full // 2), low)),
        ("send_b", pltpu.VMEM((3, rows, full // 2), low)),
        ("recv_b", pltpu.VMEM((3, rows, full // 2), low)),
        ("final", pltpu.VMEM((3, rows, full // 2), low)),
        ("sum_send", dma((3, 3, chunks))),
        ("sum_recv", dma((3, 3, chunks))),
        ("coarse_cos", pltpu.VMEM((rows, width), wide)),
        ("coarse_sin", pltpu.VMEM((rows, width), wide)),
        ("pair_out", pltpu.VMEM((2, rows, width), low)),
        ("query_out", pltpu.VMEM((2, rows, width // 2), low)),
        ("pairs", pltpu.VMEM((places * rows, width), low)),
        ("queries", pltpu.VMEM((2 * rows, width // 2), low)),
        ("pair_send", dma((places, chunks))),
        ("pair_recv", dma((places, chunks))),
        ("query_send", dma((chunks,))),
        ("query_recv", dma((chunks,))),
        ("top", pltpu.VMEM((2, 1, 2 * rows), wide)),
        ("norm", pltpu.VMEM((2, 1, 2 * rows), wide)),
        ("acc", pltpu.VMEM((width // 2, 2 * rows), wide)),
        ("turn", pltpu.VMEM((rows, width // 2), low)),
        ("heads_in", pltpu.VMEM((rows, width), low)),
        ("turn_send", dma((1,))),
        ("turn_recv", dma((1,))),
        ("spread", pltpu.VMEM((width // 128, count, 128), wide)),
    ]


class Names:
    pass


def block_kernel(names, chunk_rows, *refs):
    (ids_h, fine_gain_h, coarse_gain_h, ffn_gain_h, emb_h, fq_h, fk_h, fv_h, fo_h, ws_h,
     cq_h, ck_h, cv_h, co_h, up_h, down_h, lift_h, out_ref) = refs[:18]
    s = Names()
    for name, ref in zip(names, refs[18:]):
        setattr(s, name, ref)
    count, width = out_ref.shape
    full = 4 * width
    heads = width // HEAD_DIM
    chunks = count // chunk_rows
    group = chunk_rows // SHORTEN
    rows = count // SHORTEN
    frame = LEAD + WINDOW + count
    span = WINDOW + chunk_rows
    lanes = width // 128
    pair = width // 2

    places = lax.axis_size("seq")
    place = lax.axis_index("seq")
    levels = places // 2
    side = place % 2
    level = place // 2
    cross = place + 1 - 2 * side
    me = lax.axis_index("head")
    sibling = me + 1 - 2 * (me % 2)
    across = (me + 2) % 4
    diagonal = (sibling + 2) % 4

    barrier = pltpu.get_barrier_semaphore()
    for device in (sibling, across, diagonal):
        pl.semaphore_signal(barrier, inc=1, device_id={"head": device}, device_id_type=MESH)

    def greet(step, state):
        pl.semaphore_signal(
            barrier, inc=1, device_id={"seq": (place + step) % places}, device_id_type=MESH
        )
        return state

    lax.fori_loop(1, places, greet, 0)

    own_columns = aligned(me * width, width, width)
    own_ids = s.ids.at[:, pl.ds(LEAD + WINDOW, count)]
    loads = {
        name: pltpu.make_async_copy(source, target, s.load_sem.at[index])
        for index, (name, source, target) in enumerate((
            ("ids", ids_h, own_ids), ("emb", emb_h, s.emb), ("fine_gain", fine_gain_h, s.fine_gain),
            ("fk", fk_h, s.fk), ("fv", fv_h, s.fv), ("fq", fq_h, s.fq),
            ("coarse_gain", coarse_gain_h, s.coarse_gain), ("ffn_gain", ffn_gain_h, s.ffn_gain),
            ("cols", fo_h.at[:, own_columns], s.cols.at[pl.ds(0, width), :]),
            ("ws", ws_h, s.ws), ("cq", cq_h, s.cq), ("ck", ck_h, s.ck), ("cv", cv_h, s.cv), ("co", co_h, s.co),
            ("up", up_h, s.up), ("down", down_h, s.down),
            *((f"lift{b}", lift_h.at[:, :, pl.ds(b * 128, 128)], s.raw.at[b]) for b in range(lanes)),
        ))
    }
    lift_names = tuple(f"lift{block}" for block in range(lanes))

    def start_loads(*names):
        for name in names:
            loads[name].start()

    start_loads("ids", "emb", "fine_gain", "fk", "fv", "fq")

    @pl.when(place < 1)
    def _():
        s.ids[:, LEAD : LEAD + WINDOW] = jnp.zeros((1, WINDOW), jnp.int32)

    @pl.when(place < 2)
    def _():
        s.ids[:, :LEAD] = jnp.zeros((1, LEAD), jnp.int32)

    def clear(index, state):
        chunk = index // (places - 2)
        blank = index % (places - 2)

        @pl.when(blank + 2 >= 2 * level + 2)
        def _():
            at = aligned((chunk * places + blank + 2) * group, group, group)
            s.pairs[at, :] = jnp.zeros((group, width), jnp.bfloat16)

        return state

    lax.fori_loop(0, chunks * (places - 2), clear, 0)

    column = lax.broadcasted_iota(jnp.int32, (HALF, 128), 0)
    lane = lax.broadcasted_iota(jnp.int32, (HALF, 128), 1)
    period = periods(column)
    small = phase(lane, period)
    base = (place - 1) * count - LEAD
    large = phase(base + 128 * lane, period)
    cos_b, sin_b, cos_a, sin_a = jnp.cos(small), jnp.sin(small), jnp.cos(large), jnp.sin(large)
    for block in range(frame // 128):
        at = slice(block * 128, block * 128 + 128)
        cos_k, sin_k = cos_a[:, block : block + 1], sin_a[:, block : block + 1]
        s.cos_t[:, at] = cos_b * cos_k - sin_b * sin_k
        s.sin_t[:, at] = sin_b * cos_k + cos_b * sin_k

    pl.semaphore_wait(barrier, places + 2)

    def id_copy(steps):
        if steps == 1:
            target = s.ids.at[:, pl.ds(LEAD, WINDOW)]
            source = ids_h
        else:
            target = s.ids.at[:, pl.ds(0, LEAD)]
            source = ids_h.at[:, pl.ds(count - LEAD, LEAD)]
        device = (place + steps) % places
        return remote(source, target, s.id_send.at[steps - 1], s.id_recv.at[steps - 1], {"seq": device})

    for steps in (1, 2):
        @pl.when(place + steps < places)
        def _():
            id_copy(steps).start()

    def column_copy(flip, device):
        return remote(
            fo_h.at[:, aligned(device * width, width, width)], s.cols.at[pl.ds(flip * width, width), :],
            s.col_send.at[flip], s.col_recv.at[flip], {"head": device},
        )

    column_copies = [column_copy(flip, device) for flip, device in ((1, sibling), (2, across), (3, diagonal))]
    for copy in column_copies:
        copy.start()

    loads["emb"].wait()
    loads["fine_gain"].wait()
    level_in = normed(s.emb[...].astype(jnp.float32), s.fine_gain[...])

    def split(values):
        high = values.astype(jnp.bfloat16)
        return high, (values - high.astype(jnp.float32)).astype(jnp.bfloat16)

    loads["fk"].wait()
    s.tabs[0], s.tabs[1] = split(dot(level_in, s.fk[...]).T)
    loads["fv"].wait()
    s.tabs[2] = dot(level_in, s.fv[...]).T.astype(jnp.bfloat16)
    loads["fq"].wait()
    s.tabs[3], s.tabs[4] = split(dot(level_in, s.fq[...]).T)
    s.tabs[5] = s.emb[:, own_columns]
    loads["ids"].wait()
    start_loads("cols", "ws", "coarse_gain", "ffn_gain", "cq", "ck", "cv")

    def turned(joined, at):
        cosine, sine = s.cos_t[:, at], s.sin_t[:, at]
        pieces = []
        for head in range(heads):
            low = joined[head * HEAD_DIM : head * HEAD_DIM + HALF]
            high = joined[head * HEAD_DIM + HALF : (head + 1) * HEAD_DIM]
            pieces += [low * cosine - high * sine, high * cosine + low * sine]
        return jnp.concatenate(pieces, axis=0)

    def hot_rows(at, size):
        levels_at = lax.broadcasted_iota(jnp.int32, (256, size), 0)
        return jnp.where(levels_at == s.ids[:, at], 1.0, 0.0).astype(jnp.bfloat16)

    def key_rows(begin, size):
        at = aligned(begin, size, 128)
        hot = hot_rows(at, size)
        s.keys[at, :] = turned(dot(s.tabs[0], hot) + dot(s.tabs[1], hot), at).T.astype(jnp.bfloat16)
        s.values[:, at] = dot(s.tabs[2], hot).astype(jnp.bfloat16)

    def query_rows(begin, size):
        at = aligned(begin, size, 128)
        to = aligned(begin - WINDOW, size, 128)
        hot = hot_rows(at, size)
        s.query[:, to] = turned(dot(s.tabs[3], hot) + dot(s.tabs[4], hot), at).astype(jnp.bfloat16)
        s.start[to, :] = dot_tn(hot, s.tabs[5]).astype(jnp.bfloat16)

    own_block = min(512, count)

    def own_rows(index, state):
        key_rows(LEAD + WINDOW + index * own_block, own_block)
        query_rows(LEAD + WINDOW + index * own_block, own_block)
        return state

    def prior_rows(index, state):
        key_rows(index * 384, 384)
        return state

    lax.fori_loop(0, count // own_block, own_rows, 0)
    for steps in (1, 2):
        @pl.when(place >= steps)
        def _():
            id_copy(steps).wait_recv()

    lax.fori_loop(0, (LEAD + WINDOW) // 384, prior_rows, 0)
    query_rows(WINDOW, LEAD)

    def weigh(scores):
        top = scores[0]
        for piece in scores[1:]:
            top = jnp.maximum(top, piece)
        top = jnp.max(top, axis=0, keepdims=True)
        weights = [jnp.exp2((piece - top) * EXP2_SCALE) for piece in scores]
        total = weights[0]
        for piece in weights[1:]:
            total = total + piece
        total = jnp.sum(total, axis=0, keepdims=True)
        return jnp.concatenate([piece.astype(jnp.bfloat16) for piece in weights], axis=0), total

    def mixed_rows(chunk):
        return aligned(CARRY + chunk * chunk_rows, chunk_rows, CARRY)

    def mix_copies(chunk, at):
        def slot(which):
            return s.others.at[at, pl.ds((which - 1) * width, width)]

        def copy(kind, source, target, device):
            return remote(source, target, s.mix_send.at[kind, chunk], s.mix_recv.at[kind, chunk], {"head": device})

        return (
            copy(0, s.mixed.at[at, :], slot(2), across),
            copy(1, s.mixed.at[at, :], slot(1), sibling),
            copy(2, slot(2), slot(3), sibling),
        )

    carry_at = pl.ds(0, CARRY)
    carry_copies = mix_copies(chunks, carry_at)

    start_loads("co", "up", "down", *lift_names)

    lane_slot = lax.broadcasted_iota(jnp.int32, (HEAD_DIM, LEAD), 1) // 32
    packed = []
    for head in range(heads):
        rolled = pltpu.roll(s.query[head * HEAD_DIM : (head + 1) * HEAD_DIM, :LEAD].astype(jnp.float32), (32 * head + 32) % LEAD, 1)
        packed.append(jnp.where(lane_slot == head, rolled, 0.0))
    packed = jnp.concatenate(packed, axis=0).astype(jnp.bfloat16)
    scores = dot(s.keys[: LEAD + WINDOW, :], packed)
    key = lax.broadcasted_iota(jnp.int32, scores.shape, 0)
    last = lax.broadcasted_iota(jnp.int32, scores.shape, 1) % 32 + (LEAD + WINDOW - 32)
    floor = jnp.where(place < 2, LEAD, 0)
    allowed = (key > last - WINDOW) & (key <= last) & (key >= floor)
    weights, total = weigh([jnp.where(allowed, scores, masked_low)])
    out = dot(s.values[:, : LEAD + WINDOW], weights) / total
    unpacked = [
        pltpu.roll(out[head * HEAD_DIM : (head + 1) * HEAD_DIM, :], (LEAD - 32 * head) % LEAD, 1) for head in range(heads)
    ]
    s.mixed[carry_at, :] = jnp.concatenate(unpacked, axis=0).T[32 - CARRY : 32, :].astype(jnp.bfloat16)
    carry_copies[0].start()
    carry_copies[1].start()

    part_keys = 3 * chunk_rows if span % (3 * chunk_rows) == 0 else chunk_rows
    row = lax.broadcasted_iota(jnp.int32, (chunk_rows, heads * chunk_rows), 0)
    column = lax.broadcasted_iota(jnp.int32, (chunk_rows, heads * chunk_rows), 1) % chunk_rows

    def by_eights(values):
        return values.reshape(values.shape[0] // 8, 8, values.shape[1])

    row_head = lax.broadcasted_iota(jnp.int32, (width, chunk_rows), 0) // HEAD_DIM

    def attend_chunk(chunk):
        begin = chunk * chunk_rows
        floor = jnp.where(place == 0, WINDOW - begin, 0)
        key_at = aligned(LEAD + begin, span, 128)
        query = s.query[:, aligned(LEAD + begin, chunk_rows, chunk_rows)]
        stacked = jnp.concatenate(
            [jnp.where(row_head == head, query, jnp.zeros_like(query)) for head in range(heads)], axis=1
        )
        top = None
        for part in range(0, span, part_keys):
            scores = dot(s.keys[aligned(LEAD + begin + part, part_keys, 128), :], stacked)
            for at in range(part, part + part_keys, chunk_rows):
                piece = scores[at - part : at - part + chunk_rows, :]
                if at == span - chunk_rows:
                    allowed = row <= column
                else:
                    allowed = row >= floor - at
                    if at == 0:
                        allowed = allowed & (row > column)
                piece = jnp.where(allowed, piece, masked_low)
                s.scores[at : at + chunk_rows, :] = piece
                peak = jnp.max(by_eights(piece), axis=0)
                top = peak if top is None else jnp.maximum(top, peak)
        top = jnp.max(top, axis=0, keepdims=True)
        total = jnp.zeros((8, heads * chunk_rows), jnp.float32)
        for at in range(0, span, chunk_rows):
            weights = jnp.exp2((s.scores[at : at + chunk_rows, :] - top) * EXP2_SCALE)
            total = total + jnp.sum(by_eights(weights), axis=0)
            s.weights[at : at + chunk_rows, :] = weights.astype(jnp.bfloat16)
        total = jnp.sum(total, axis=0, keepdims=True)
        outs = []
        for head in range(heads):
            of = slice(head * chunk_rows, (head + 1) * chunk_rows)
            outs.append(
                dot(s.values[head * HEAD_DIM : (head + 1) * HEAD_DIM, key_at], s.weights[:, of]) / total[:, of]
            )
        at = mixed_rows(chunk)
        s.mixed[at, :] = jnp.concatenate(outs, axis=0).T.astype(jnp.bfloat16)
        copies = mix_copies(chunk, at)
        copies[0].start()
        copies[1].start()

    def fine_rows(at, start_at):
        merged = dot(s.mixed[at, :], s.cols[:width, :]) + dot(s.others[at, :], s.cols[width:, :])
        value = (s.start[start_at, :].astype(jnp.float32) + merged).astype(jnp.bfloat16).astype(jnp.float32)
        for block in range(lanes):
            s.stream[block, at, :] = value[:, block * 128 : block * 128 + 128]

    peers = (me, sibling, across)
    buffers = (s.send_a, s.recv_a, s.send_b, s.recv_b, s.final)
    short_sum = HeadSum(0, peers, s.part, s.short, buffers, s.sum_send, s.sum_recv)

    def short_rows(chunk):
        return aligned(chunk * group, group, group)

    def relay_chunk(chunk):
        @pl.when(chunk == 0)
        def _():
            carry_copies[0].wait_recv()
            carry_copies[2].start()

        copies = mix_copies(chunk, mixed_rows(chunk))
        copies[0].wait_recv()
        copies[2].start()

    def finish_chunk(chunk):
        @pl.when(chunk == 0)
        def _():
            for copy in column_copies:
                copy.wait_recv()
            loads["cols"].wait()
            loads["ws"].wait()
            carry_copies[1].wait_recv()
            carry_copies[2].wait_recv()
            fine_rows(carry_at, pl.ds(LEAD - CARRY, CARRY))

            @pl.when(place == 0)
            def _():
                s.stream[:, 0:CARRY, :] = jnp.zeros((lanes, CARRY, 128), jnp.float32)

        at = mixed_rows(chunk)
        copies = mix_copies(chunk, at)
        copies[1].wait_recv()
        copies[2].wait_recv()
        fine_rows(at, aligned(LEAD + chunk * chunk_rows, chunk_rows, chunk_rows))
        total = jnp.zeros((group, full), jnp.float32)
        for offset in range(SHORTEN):
            begin = CARRY - (SHORTEN - 1) + offset + chunk * chunk_rows
            member = jnp.concatenate(
                [s.stream[block, pl.ds(begin, group, stride=SHORTEN), :] for block in range(lanes)], axis=1
            )
            total = total + dot(member.astype(jnp.bfloat16), s.ws[offset])
        s.part[short_rows(chunk), :] = total
        short_sum.begin(chunk, short_rows(chunk))

    lane_f = lax.broadcasted_iota(jnp.int32, (rows, 128), 1) % HEAD_DIM
    period_f = periods(lane_f % HALF)
    angle_f = phase(place * rows + lax.broadcasted_iota(jnp.int32, (rows, 128), 0), period_f)
    cos_f = jnp.cos(angle_f)
    sin_f = jnp.where(lane_f < HALF, -jnp.sin(angle_f), jnp.sin(angle_f))
    for block in range(lanes):
        s.coarse_cos[:, block * 128 : block * 128 + 128] = cos_f
        s.coarse_sin[:, block * 128 : block * 128 + 128] = sin_f

    def pair_rows(chunk, source):
        return aligned((chunk * places + source) * group, group, group)

    def pair_copy(chunk, target):
        at = pair_rows(chunk, place)
        return remote(
            s.pair_out.at[target % 2, short_rows(chunk), :], s.pairs.at[at, :],
            s.pair_send.at[target, chunk], s.pair_recv.at[place, chunk], {"seq": target},
        )

    def pair_arrival(chunk, source):
        at = pair_rows(chunk, source)
        return remote(
            s.pairs.at[at, :], s.pairs.at[at, :], s.pair_send.at[source, chunk], s.pair_recv.at[source, chunk],
            {"seq": cross},
        )

    def query_copy(chunk):
        at = short_rows(chunk)
        return remote(
            s.query_out.at[1 - side, at, :], s.queries.at[aligned(side * rows + chunk * group, group, group), :],
            s.query_send.at[chunk], s.query_recv.at[chunk], {"seq": cross},
        )

    def for_targets(action):
        def one(index, state):
            target = places - 1 - index

            @pl.when(target != place)
            def _():
                action(target)

            return state

        lax.fori_loop(0, places - 2 * level, one, 0)

    def project_chunk(chunk):
        @pl.when(chunk == 0)
        def _():
            for name in ("coarse_gain", "cq", "ck", "cv"):
                loads[name].wait()

        at = short_rows(chunk)
        short_sum.end(chunk, at)
        coarse_in = normed(s.short[at, :].astype(jnp.float32), s.coarse_gain[...])
        cosine, sine = s.coarse_cos[at, :], s.coarse_sin[at, :]
        is_low = lax.broadcasted_iota(jnp.int32, (group, width), 1) % HEAD_DIM < HALF

        def rotated(values):
            other = jnp.where(is_low, pltpu.roll(values, width - HALF, 1), pltpu.roll(values, HALF, 1))
            return (values * cosine + other * sine).astype(jnp.bfloat16)

        key = rotated(dot(coarse_in, s.ck[...]))
        value = dot(coarse_in, s.cv[...]).astype(jnp.bfloat16)
        for half in range(2):
            s.pair_out[half, at, :pair] = key[:, half * pair : half * pair + pair]
            s.pair_out[half, at, pair:] = value[:, half * pair : half * pair + pair]
        for_targets(lambda target: pair_copy(chunk, target).start())
        query = rotated(dot(coarse_in, s.cq[...]))
        for half in range(2):
            s.query_out[half, at, :] = query[:, half * pair : half * pair + pair]
        query_copy(chunk).start()
        s.pairs[pair_rows(chunk, place), :] = s.pair_out[side, at, :]
        s.queries[aligned(side * rows + chunk * group, group, group), :] = s.query_out[side, at, :]

    stages = (
        (PROJECT, project_chunk),
        (TOTAL, lambda chunk: short_sum.total(chunk, short_rows(chunk))),
        (MIDDLE, lambda chunk: short_sum.middle(chunk, short_rows(chunk))),
        (FINISH, finish_chunk),
        (RELAY, relay_chunk),
    )

    def one_step(step, state):
        attend_chunk(step)
        for lag, action in stages:
            @pl.when(step >= lag)
            def _():
                action(step - lag)

        return state

    lax.fori_loop(0, chunks, one_step, 0)

    left = {action: max(0, chunks - lag) for lag, action in stages}
    project, total_up, middle_up, finish, relay = (action for _, action in stages)

    def rest(action, upto):
        for chunk in range(left[action], min(upto, chunks)):
            action(chunk)
        left[action] = max(left[action], min(upto, chunks))

    for action, upto in (
        (total_up, chunks - 5), (project, chunks - 6), (relay, chunks - 1), (total_up, chunks - 4), (project, chunks - 5),
        (finish, chunks - 2), (project, chunks - 4), (middle_up, chunks - 3), (relay, chunks), (finish, chunks - 1),
        (middle_up, chunks - 2), (finish, chunks), (middle_up, chunks - 1), (total_up, chunks - 3), (middle_up, chunks),
        (project, chunks - 3), (total_up, chunks - 2), (project, chunks - 2), (total_up, chunks - 1), (total_up, chunks),
        (project, chunks - 1), (project, chunks),
    ):
        rest(action, upto)

    def wait_chunk(chunk):
        def one(source, state):
            @pl.when(source != place)
            def _():
                pair_arrival(chunk, source).wait_recv()

            return state

        lax.fori_loop(0, 2 * level + 2, one, 0)

    for name in lift_names:
        loads[name].wait()
    part_rows = count // SHORTEN
    for block in range(lanes):
        for begin in range(0, full, part_rows):
            flat = s.raw.at[block, pl.ds(begin, part_rows)].reshape(part_rows * SHORTEN, 128)
            s.spread[block] = flat[...].astype(jnp.float32)
            for member in range(SHORTEN):
                s.lift[begin : begin + part_rows, member * width + block * 128 : member * width + block * 128 + 128] = (
                    s.spread[block, pl.ds(member, part_rows, stride=SHORTEN), :].astype(jnp.bfloat16)
                )

    def wait_queries(chunk, state):
        query_copy(chunk).wait_recv()
        return state

    lax.fori_loop(0, chunks, wait_queries, 0)

    s.top[...] = jnp.full(s.top.shape, masked_low, jnp.float32)
    s.norm[...] = jnp.zeros(s.norm.shape, jnp.float32)
    s.acc[...] = jnp.zeros(s.acc.shape, jnp.float32)
    per_chunk = places * group
    pair_lane = lax.broadcasted_iota(jnp.int32, (2 * rows, pair), 1) // HEAD_DIM
    queries = s.queries[...]

    def key_step(step, state):
        if per_chunk <= STEP_KEYS:
            for inner in range(STEP_KEYS // per_chunk):
                wait_chunk(step * (STEP_KEYS // per_chunk) + inner)
        else:
            ratio = per_chunk // STEP_KEYS

            @pl.when(step % ratio == 0)
            def _():
                wait_chunk(step // ratio)

        block = s.pairs[aligned(step * STEP_KEYS, STEP_KEYS, STEP_KEYS), :]
        keys, values = block[:, :pair], block[:, pair:]
        index = step * STEP_KEYS + lax.broadcasted_iota(jnp.int32, (STEP_KEYS, 1), 0)
        inside = index % per_chunk
        key_at = (inside // group) * rows + (index // per_chunk) * group + inside % group
        query_at = 2 * level * rows + lax.broadcasted_iota(jnp.int32, (1, 2 * rows), 1)
        allowed = key_at <= query_at
        values_t = values.astype(jnp.float32).T.astype(jnp.bfloat16)
        for head in range(pair // HEAD_DIM):
            masked_q = jnp.where(pair_lane == head, queries, jnp.zeros_like(queries))
            scores = jnp.where(allowed, dot_nt(keys, masked_q), masked_low)
            fresh = jnp.maximum(s.top[head], jnp.max(scores, axis=0, keepdims=True))
            factor = jnp.exp2((s.top[head] - fresh) * EXP2_SCALE)
            weights = jnp.exp2((scores - fresh) * EXP2_SCALE)
            s.norm[head] = s.norm[head] * factor + jnp.sum(weights, axis=0, keepdims=True)
            of = slice(head * HEAD_DIM, (head + 1) * HEAD_DIM)
            s.acc[of, :] = s.acc[of, :] * factor + dot(values_t[of, :], weights.astype(jnp.bfloat16))
            s.top[head] = fresh
        return state

    lax.fori_loop(0, places * rows // STEP_KEYS, key_step, 0)

    def turn_copy():
        return remote(
            s.turn, s.heads_in.at[:, aligned(side * pair, pair, pair)],
            s.turn_send.at[0], s.turn_recv.at[0], {"seq": cross},
        )

    def mixed_of(at):
        shares = [
            s.acc[head * HEAD_DIM : (head + 1) * HEAD_DIM, at] / s.norm[head, :, at] for head in range(pair // HEAD_DIM)
        ]
        return jnp.concatenate(shares, axis=0).T.astype(jnp.bfloat16)

    s.turn[...] = mixed_of(aligned((1 - side) * rows, rows, rows))
    turn_copy().start()
    s.heads_in[:, aligned(side * pair, pair, pair)] = mixed_of(aligned(side * rows, rows, rows))

    for steps in (1, 2):
        @pl.when(place + steps < places)
        def _():
            id_copy(steps).wait_send()

    for copy in column_copies:
        copy.wait_send()
    for copy in carry_copies:
        copy.wait_send()

    def drain(chunk, state):
        for copy in mix_copies(chunk, mixed_rows(chunk)):
            copy.wait_send()
        short_sum.drain(chunk, short_rows(chunk))
        for_targets(lambda target: pair_copy(chunk, target).wait_send())
        query_copy(chunk).wait_send()
        return state

    lax.fori_loop(0, chunks, drain, 0)
    loads["co"].wait()
    turn_copy().wait_recv()

    out_sum = HeadSum(1, peers, s.part, s.summed, buffers, s.sum_send, s.sum_recv)
    ffn_sum = HeadSum(2, peers, s.part_b, s.second, buffers, s.sum_send, s.sum_recv)
    size = rows // PIECES
    at = [pl.ds(piece * size, size) for piece in range(PIECES)]

    for piece in range(PIECES):
        s.part[at[piece], :] = dot(s.heads_in[at[piece], :], s.co[...])
        out_sum.begin(piece, at[piece])
    for name in ("ffn_gain", "up", "down"):
        loads[name].wait()
    for piece in range(PIECES):
        out_sum.middle(piece, at[piece])

    def feed(piece):
        out_sum.end(piece, at[piece])
        value = s.short[at[piece], :].astype(jnp.float32) + s.summed[at[piece], :].astype(jnp.float32)
        s.first[at[piece], :] = value
        inner = jax.nn.gelu(dot(normed(value, s.ffn_gain[...]), s.up[...])).astype(jnp.bfloat16)
        s.part_b[at[piece], :] = dot(inner, s.down[...])
        ffn_sum.begin(piece, at[piece])

    def raise_rows(piece):
        ffn_sum.end(piece, at[piece])
        for member in range(SHORTEN):
            lifted = dot(s.second[at[piece], :], s.lift[:, member * width : (member + 1) * width])
            for block in range(lanes):
                s.spread[block, pl.ds(SHORTEN * size * piece + member, size, stride=SHORTEN), :] = lifted[
                    :, block * 128 : block * 128 + 128
                ]
        for block in range(lanes):
            to = slice(SHORTEN * size * piece, SHORTEN * size * (piece + 1))
            base_at = slice(CARRY + SHORTEN * size * piece, CARRY + SHORTEN * size * (piece + 1))
            out_ref[to, block * 128 : block * 128 + 128] = (
                s.stream[block, base_at, :] + s.spread[block, to, :]
            ).astype(jnp.bfloat16)

    for step in range(PIECES + 4):
        if step < PIECES:
            out_sum.total(step, at[step])
        if 0 <= step - 1 < PIECES:
            feed(step - 1)
        if 0 <= step - 2 < PIECES:
            ffn_sum.middle(step - 2, at[step - 2])
        if 0 <= step - 3 < PIECES:
            ffn_sum.total(step - 3, at[step - 3], s.first)
        if 0 <= step - 4 < PIECES:
            raise_rows(step - 4)

    turn_copy().wait_send()
    for piece in range(PIECES):
        out_sum.drain(piece, at[piece])
        ffn_sum.drain(piece, at[piece])


def local(
    token_ids,
    embedding,
    fine_norm,
    fine_query,
    fine_key,
    fine_value,
    fine_output,
    shorten_weight,
    coarse_norm,
    coarse_query,
    coarse_key,
    coarse_value,
    coarse_output,
    ffn_norm,
    ffn_up,
    ffn_down,
    upsample_weight,
):
    count = token_ids.shape[0]
    width = fine_query.shape[1]
    chunk_rows = min(128, count)
    chunks = count // chunk_rows
    scratch = scratch_list(count, width, chunks, lax.axis_size("seq"))
    names = [name for name, _ in scratch]

    def kernel(*refs):
        block_kernel(names, chunk_rows, *refs)

    return pl.pallas_call(
        kernel,
        out_shape=jax.ShapeDtypeStruct((count, width), jnp.bfloat16),
        in_specs=[HBM_SPEC] * 17,
        out_specs=VMEM_SPEC,
        scratch_shapes=[shape for _, shape in scratch],
        compiler_params=pltpu.CompilerParams(
            collective_id=1, has_side_effects=True, vmem_limit_bytes=46 * 2**20
        ),
        name="block_kernel",
    )(
        *(
            pltpu.with_memory_space_constraint(array, pltpu.HBM)
            for array in (
                token_ids.reshape(1, count), fine_norm.reshape(1, D), coarse_norm.reshape(1, D), ffn_norm.reshape(1, D),
                embedding, fine_query, fine_key, fine_value, fine_output, shorten_weight, coarse_query, coarse_key,
                coarse_value, coarse_output, ffn_up, ffn_down, upsample_weight,
            )
        ),
    )


def solution(mesh):
    return jax.shard_map(
        local,
        mesh=mesh,
        in_specs=(
            P("seq"),
            P(),
            P(),
            P(None, "head"),
            P(None, "head"),
            P(None, "head"),
            P("head", None),
            P(None, "head", None),
            P(),
            P(None, "head"),
            P(None, "head"),
            P(None, "head"),
            P("head", None),
            P(),
            P(None, "head"),
            P("head", None),
            P(None, None, "head"),
        ),
        out_specs=P("seq", "head"),
        check_vma=False,
    )
```

```python
import math

import jax
import jax.numpy as jnp
from jax import lax
from jax.experimental import pallas as pl
from jax.experimental.pallas import tpu as pltpu
from jax.sharding import PartitionSpec as P

D = 1024
HEAD_DIM = 64
HALF = HEAD_DIM // 2
SHORTEN = 4
WINDOW = 1024
LEAD = 128
CARRY = 16

epsilon = 1e-06
masked_low = -1e30
MESH = pl.DeviceIdType.MESH
EXP2_SCALE = HEAD_DIM ** (-0.5) * math.log2(math.e)
VMEM_SPEC = pl.BlockSpec(memory_space=pltpu.VMEM)
HBM_SPEC = pl.BlockSpec(memory_space=pltpu.HBM)

RELAY, FINISH, MIDDLE, TOTAL, PROJECT = (2, 2, 3, 5, 5)
FORWARDED = 5
STEP_KEYS = 512
PIECES = 2
SET = 2


def dot(left, right):
    return jnp.dot(left, right, preferred_element_type=jnp.float32)


def dot_nt(left, right):
    return lax.dot_general(left, right, (((1,), (1,)), ((), ())), preferred_element_type=jnp.float32)


def dot_tn(left, right):
    return lax.dot_general(left, right, (((0,), (0,)), ((), ())), preferred_element_type=jnp.float32)


def normed(data, gain):
    power = jnp.mean(data * data, axis=1, keepdims=True)
    return (data * lax.rsqrt(power + epsilon) * gain).astype(jnp.bfloat16)


def aligned(start, size, unit):
    return pl.ds(pl.multiple_of(start, unit), size)


def periods(column):
    log = 4 + lax.shift_right_logical(column * 14, 5)
    return jnp.left_shift(jnp.ones_like(log), log)


def phase(position, period):
    cycle = jnp.bitwise_and(position, period - 1).astype(jnp.float32)
    return cycle * (2.0 * math.pi / period.astype(jnp.float32))


def remote(source, target, send, receive, device):
    return pltpu.make_async_remote_copy(
        src_ref=source, dst_ref=target, send_sem=send, recv_sem=receive, device_id=device, device_id_type=MESH
    )


class HeadSum:
    def __init__(self, index, peers, part, out, buffers, send_sem, recv_sem):
        self.index = index
        self.me, self.sibling, self.across = peers
        self.part, self.out = part, out
        self.send_a, self.recv_a, self.send_b, self.recv_b, self.final = (buffer.at[index] for buffer in buffers)
        self.send_sem, self.recv_sem = send_sem, recv_sem
        half = part.shape[1] // 2
        self.mine = aligned((self.me % 2) * half, half, half)
        self.theirs = aligned((self.sibling % 2) * half, half, half)

    def copy(self, kind, piece, source, target, device):
        return remote(
            source, target, self.send_sem.at[self.index, kind, piece], self.recv_sem.at[self.index, kind, piece],
            {"head": device},
        )

    def copy_a(self, piece, at):
        return self.copy(0, piece, self.send_a.at[at, :], self.recv_a.at[at, :], self.sibling)

    def copy_b(self, piece, at):
        return self.copy(1, piece, self.send_b.at[at, :], self.recv_b.at[at, :], self.across)

    def copy_c(self, piece, at):
        return self.copy(2, piece, self.final.at[at, :], self.out.at[at, self.mine], self.sibling)

    def begin(self, piece, at):
        self.send_a[at, :] = self.part[at, self.theirs].astype(jnp.bfloat16)
        self.copy_a(piece, at).start()

    def middle(self, piece, at):
        self.copy_a(piece, at).wait_recv()
        summed = self.part[at, self.mine] + self.recv_a[at, :].astype(jnp.float32)
        self.part[at, self.mine] = summed
        self.send_b[at, :] = summed.astype(jnp.bfloat16)
        self.copy_b(piece, at).start()

    def total(self, piece, at, residual=None):
        self.copy_b(piece, at).wait_recv()
        value = self.part[at, self.mine] + self.recv_b[at, :].astype(jnp.float32)
        if residual is not None:
            value = value + residual[at, self.mine]
        value = value.astype(jnp.bfloat16)
        self.final[at, :] = value
        self.copy_c(piece, at).start()
        self.out[at, self.mine] = value

    def end(self, piece, at):
        self.copy_c(piece, at).wait_recv()

    def drain(self, piece, at):
        self.copy_a(piece, at).wait_send()
        self.copy_b(piece, at).wait_send()
        self.copy_c(piece, at).wait_send()


def scratch_list(count, width, chunks, places):
    full = 4 * width
    rows = count // SHORTEN
    frame = LEAD + WINDOW + count
    low = jnp.bfloat16
    wide = jnp.float32
    dma = pltpu.SemaphoreType.DMA
    return [
        ("emb", pltpu.VMEM((256, full), low)),
        ("fq", pltpu.VMEM((full, width), low)),
        ("fk", pltpu.VMEM((full, width), low)),
        ("fv", pltpu.VMEM((full, width), low)),
        ("cols", pltpu.VMEM((full, width), low)),
        ("ws", pltpu.VMEM((SHORTEN, width, full), low)),
        ("cq", pltpu.VMEM((full, width), low)),
        ("ck", pltpu.VMEM((full, width), low)),
        ("cv", pltpu.VMEM((full, width), low)),
        ("co", pltpu.VMEM((width, full), low)),
        ("up", pltpu.VMEM((full, full), low)),
        ("down", pltpu.VMEM((full, full), low)),
        ("lift", pltpu.VMEM((full, SHORTEN * width), low)),
        ("raw", pltpu.VMEM((width // 128, full, SHORTEN, 128), low)),
        ("fine_gain", pltpu.VMEM((1, full), wide)),
        ("coarse_gain", pltpu.VMEM((1, full), wide)),
        ("ffn_gain", pltpu.VMEM((1, full), wide)),
        ("load_sem", dma((17 + width // 128,))),
        ("ids", pltpu.VMEM((1, frame), jnp.int32)),
        ("id_send", dma((2,))),
        ("id_recv", dma((2,))),
        ("col_send", dma((4,))),
        ("col_recv", dma((4,))),
        ("tabs", pltpu.VMEM((6, 256, width), low)),
        ("cos_t", pltpu.VMEM((HALF, frame), wide)),
        ("sin_t", pltpu.VMEM((HALF, frame), wide)),
        ("keys", pltpu.VMEM((frame, width), low)),
        ("values", pltpu.VMEM((width, frame), low)),
        ("query", pltpu.VMEM((width, LEAD + count), low)),
        ("start", pltpu.VMEM((LEAD + count, width), low)),
        ("scores", pltpu.VMEM((WINDOW + count // chunks, 4 * (count // chunks)), wide)),
        ("weights", pltpu.VMEM((WINDOW + count // chunks, 4 * (count // chunks)), low)),
        ("mixed", pltpu.VMEM((CARRY + count, width), low)),
        ("others", pltpu.VMEM((CARRY + count, 3 * width), low)),
        ("mix_send", dma((3, chunks + 1))),
        ("mix_recv", dma((3, chunks + 1))),
        ("stream", pltpu.VMEM((width // 128, CARRY + count, 128), wide)),
        ("part", pltpu.VMEM((rows, full), wide)),
        ("part_b", pltpu.VMEM((rows, full), wide)),
        ("short", pltpu.VMEM((rows, full), low)),
        ("summed", pltpu.VMEM((rows, full), low)),
        ("first", pltpu.VMEM((rows, full), wide)),
        ("second", pltpu.VMEM((rows, full), low)),
        ("send_a", pltpu.VMEM((3, rows, full // 2), low)),
        ("recv_a", pltpu.VMEM((3, rows, full // 2), low)),
        ("send_b", pltpu.VMEM((3, rows, full // 2), low)),
        ("recv_b", pltpu.VMEM((3, rows, full // 2), low)),
        ("final", pltpu.VMEM((3, rows, full // 2), low)),
        ("sum_send", dma((3, 3, chunks))),
        ("sum_recv", dma((3, 3, chunks))),
        ("coarse_cos", pltpu.VMEM((rows, width), wide)),
        ("coarse_sin", pltpu.VMEM((rows, width), wide)),
        ("pair_out", pltpu.VMEM((2, rows, width), low)),
        ("query_out", pltpu.VMEM((2, rows, width // 2), low)),
        ("pairs", pltpu.VMEM((places * rows, width), low)),
        ("queries", pltpu.VMEM((2 * rows, width // 2), low)),
        ("pair_send", dma((places, chunks))),
        ("pair_recv", dma((places, chunks))),
        ("forward_send", dma((places, chunks))),
        ("query_send", dma((chunks,))),
        ("query_recv", dma((chunks,))),
        ("top", pltpu.VMEM((2, 1, 2 * rows), wide)),
        ("norm", pltpu.VMEM((2, 1, 2 * rows), wide)),
        ("acc", pltpu.VMEM((width // 2, 2 * rows), wide)),
        ("turn", pltpu.VMEM((rows, width // 2), low)),
        ("heads_in", pltpu.VMEM((rows, width), low)),
        ("turn_send", dma((1,))),
        ("turn_recv", dma((1,))),
        ("spread", pltpu.VMEM((width // 128, count, 128), wide)),
    ]


class Names:
    pass


def block_kernel(names, chunk_rows, *refs):
    (ids_h, fine_gain_h, coarse_gain_h, ffn_gain_h, emb_h, fq_h, fk_h, fv_h, fo_h, ws_h,
     cq_h, ck_h, cv_h, co_h, up_h, down_h, lift_h, out_ref) = refs[:18]
    s = Names()
    for name, ref in zip(names, refs[18:]):
        setattr(s, name, ref)
    count, width = out_ref.shape
    full = 4 * width
    heads = width // HEAD_DIM
    chunks = count // chunk_rows
    group = chunk_rows // SHORTEN
    rows = count // SHORTEN
    frame = LEAD + WINDOW + count
    span = WINDOW + chunk_rows
    lanes = width // 128
    pair = width // 2

    places = lax.axis_size("seq")
    place = lax.axis_index("seq")
    levels = places // 2
    side = place % 2
    level = place // 2
    cross = place + 1 - 2 * side
    me = lax.axis_index("head")
    sibling = me + 1 - 2 * (me % 2)
    across = (me + 2) % 4
    diagonal = (sibling + 2) % 4

    barrier = pltpu.get_barrier_semaphore()
    for device in (sibling, across, diagonal):
        pl.semaphore_signal(barrier, inc=1, device_id={"head": device}, device_id_type=MESH)

    def greet(step, state):
        pl.semaphore_signal(
            barrier, inc=1, device_id={"seq": (place + step) % places}, device_id_type=MESH
        )
        return state

    lax.fori_loop(1, places, greet, 0)

    own_columns = aligned(me * width, width, width)
    own_ids = s.ids.at[:, pl.ds(LEAD + WINDOW, count)]
    loads = {
        name: pltpu.make_async_copy(source, target, s.load_sem.at[index])
        for index, (name, source, target) in enumerate((
            ("ids", ids_h, own_ids), ("emb", emb_h, s.emb), ("fine_gain", fine_gain_h, s.fine_gain),
            ("fk", fk_h, s.fk), ("fv", fv_h, s.fv), ("fq", fq_h, s.fq),
            ("coarse_gain", coarse_gain_h, s.coarse_gain), ("ffn_gain", ffn_gain_h, s.ffn_gain),
            ("cols", fo_h.at[:, own_columns], s.cols.at[pl.ds(0, width), :]),
            ("ws", ws_h, s.ws), ("cq", cq_h, s.cq), ("ck", ck_h, s.ck), ("cv", cv_h, s.cv), ("co", co_h, s.co),
            ("up", up_h, s.up), ("down", down_h, s.down),
            *((f"lift{b}", lift_h.at[:, :, pl.ds(b * 128, 128)], s.raw.at[b]) for b in range(lanes)),
        ))
    }
    lift_names = tuple(f"lift{block}" for block in range(lanes))

    def start_loads(*names):
        for name in names:
            loads[name].start()

    start_loads("ids", "emb", "fine_gain", "fk", "fv", "fq")

    @pl.when(place < 1)
    def _():
        s.ids[:, LEAD : LEAD + WINDOW] = jnp.zeros((1, WINDOW), jnp.int32)

    @pl.when(place < 2)
    def _():
        s.ids[:, :LEAD] = jnp.zeros((1, LEAD), jnp.int32)

    def clear(index, state):
        chunk = index // (places - 2)
        blank = index % (places - 2)

        @pl.when(blank + 2 >= 2 * level + 2)
        def _():
            at = aligned((chunk * places + blank + 2) * group, group, group)
            s.pairs[at, :] = jnp.zeros((group, width), jnp.bfloat16)

        return state

    lax.fori_loop(0, chunks * (places - 2), clear, 0)

    column = lax.broadcasted_iota(jnp.int32, (HALF, 128), 0)
    lane = lax.broadcasted_iota(jnp.int32, (HALF, 128), 1)
    period = periods(column)
    small = phase(lane, period)
    base = (place - 1) * count - LEAD
    large = phase(base + 128 * lane, period)
    cos_b, sin_b, cos_a, sin_a = jnp.cos(small), jnp.sin(small), jnp.cos(large), jnp.sin(large)
    for block in range(frame // 128):
        at = slice(block * 128, block * 128 + 128)
        cos_k, sin_k = cos_a[:, block : block + 1], sin_a[:, block : block + 1]
        s.cos_t[:, at] = cos_b * cos_k - sin_b * sin_k
        s.sin_t[:, at] = sin_b * cos_k + cos_b * sin_k

    pl.semaphore_wait(barrier, places + 2)

    def id_copy(steps):
        if steps == 1:
            target = s.ids.at[:, pl.ds(LEAD, WINDOW)]
            source = ids_h
        else:
            target = s.ids.at[:, pl.ds(0, LEAD)]
            source = ids_h.at[:, pl.ds(count - LEAD, LEAD)]
        device = (place + steps) % places
        return remote(source, target, s.id_send.at[steps - 1], s.id_recv.at[steps - 1], {"seq": device})

    for steps in (1, 2):
        @pl.when(place + steps < places)
        def _():
            id_copy(steps).start()

    def column_copy(flip, device):
        return remote(
            fo_h.at[:, aligned(device * width, width, width)], s.cols.at[pl.ds(flip * width, width), :],
            s.col_send.at[flip], s.col_recv.at[flip], {"head": device},
        )

    column_copies = [column_copy(flip, device) for flip, device in ((1, sibling), (2, across), (3, diagonal))]
    for copy in column_copies:
        copy.start()

    loads["emb"].wait()
    loads["fine_gain"].wait()
    level_in = normed(s.emb[...].astype(jnp.float32), s.fine_gain[...])

    def split(values):
        high = values.astype(jnp.bfloat16)
        return high, (values - high.astype(jnp.float32)).astype(jnp.bfloat16)

    loads["fk"].wait()
    s.tabs[0], s.tabs[1] = split(dot(level_in, s.fk[...]).T)
    loads["fv"].wait()
    s.tabs[2] = dot(level_in, s.fv[...]).T.astype(jnp.bfloat16)
    loads["fq"].wait()
    s.tabs[3], s.tabs[4] = split(dot(level_in, s.fq[...]).T)
    s.tabs[5] = s.emb[:, own_columns]
    loads["ids"].wait()
    start_loads("cols", "ws", "coarse_gain", "ffn_gain", "cq", "ck", "cv")

    def turned(joined, at):
        cosine, sine = s.cos_t[:, at], s.sin_t[:, at]
        pieces = []
        for head in range(heads):
            low = joined[head * HEAD_DIM : head * HEAD_DIM + HALF]
            high = joined[head * HEAD_DIM + HALF : (head + 1) * HEAD_DIM]
            pieces += [low * cosine - high * sine, high * cosine + low * sine]
        return jnp.concatenate(pieces, axis=0)

    def hot_rows(at, size):
        levels_at = lax.broadcasted_iota(jnp.int32, (256, size), 0)
        return jnp.where(levels_at == s.ids[:, at], 1.0, 0.0).astype(jnp.bfloat16)

    def key_rows(begin, size):
        at = aligned(begin, size, 128)
        hot = hot_rows(at, size)
        s.keys[at, :] = turned(dot(s.tabs[0], hot) + dot(s.tabs[1], hot), at).T.astype(jnp.bfloat16)
        s.values[:, at] = dot(s.tabs[2], hot).astype(jnp.bfloat16)

    def query_rows(begin, size):
        at = aligned(begin, size, 128)
        to = aligned(begin - WINDOW, size, 128)
        hot = hot_rows(at, size)
        s.query[:, to] = turned(dot(s.tabs[3], hot) + dot(s.tabs[4], hot), at).astype(jnp.bfloat16)
        s.start[to, :] = dot_tn(hot, s.tabs[5]).astype(jnp.bfloat16)

    own_block = min(512, count)

    def own_rows(index, state):
        key_rows(LEAD + WINDOW + index * own_block, own_block)
        query_rows(LEAD + WINDOW + index * own_block, own_block)
        return state

    def prior_rows(index, state):
        key_rows(index * 384, 384)
        return state

    lax.fori_loop(0, count // own_block, own_rows, 0)
    for steps in (1, 2):
        @pl.when(place >= steps)
        def _():
            id_copy(steps).wait_recv()

    lax.fori_loop(0, (LEAD + WINDOW) // 384, prior_rows, 0)
    query_rows(WINDOW, LEAD)

    def weigh(scores):
        top = scores[0]
        for piece in scores[1:]:
            top = jnp.maximum(top, piece)
        top = jnp.max(top, axis=0, keepdims=True)
        weights = [jnp.exp2((piece - top) * EXP2_SCALE) for piece in scores]
        total = weights[0]
        for piece in weights[1:]:
            total = total + piece
        total = jnp.sum(total, axis=0, keepdims=True)
        return jnp.concatenate([piece.astype(jnp.bfloat16) for piece in weights], axis=0), total

    def mixed_rows(chunk):
        return aligned(CARRY + chunk * chunk_rows, chunk_rows, CARRY)

    def mix_copies(chunk, at):
        def slot(which):
            return s.others.at[at, pl.ds((which - 1) * width, width)]

        def copy(kind, source, target, device):
            return remote(source, target, s.mix_send.at[kind, chunk], s.mix_recv.at[kind, chunk], {"head": device})

        return (
            copy(0, s.mixed.at[at, :], slot(2), across),
            copy(1, s.mixed.at[at, :], slot(1), sibling),
            copy(2, slot(2), slot(3), sibling),
        )

    carry_at = pl.ds(0, CARRY)
    carry_copies = mix_copies(chunks, carry_at)

    start_loads("co", "up", "down", *lift_names)

    lane_slot = lax.broadcasted_iota(jnp.int32, (HEAD_DIM, LEAD), 1) // 32
    packed = []
    for head in range(heads):
        rolled = pltpu.roll(s.query[head * HEAD_DIM : (head + 1) * HEAD_DIM, :LEAD].astype(jnp.float32), (32 * head + 32) % LEAD, 1)
        packed.append(jnp.where(lane_slot == head, rolled, 0.0))
    packed = jnp.concatenate(packed, axis=0).astype(jnp.bfloat16)
    scores = dot(s.keys[: LEAD + WINDOW, :], packed)
    key = lax.broadcasted_iota(jnp.int32, scores.shape, 0)
    last = lax.broadcasted_iota(jnp.int32, scores.shape, 1) % 32 + (LEAD + WINDOW - 32)
    floor = jnp.where(place < 2, LEAD, 0)
    allowed = (key > last - WINDOW) & (key <= last) & (key >= floor)
    weights, total = weigh([jnp.where(allowed, scores, masked_low)])
    out = dot(s.values[:, : LEAD + WINDOW], weights) / total
    unpacked = [
        pltpu.roll(out[head * HEAD_DIM : (head + 1) * HEAD_DIM, :], (LEAD - 32 * head) % LEAD, 1) for head in range(heads)
    ]
    s.mixed[carry_at, :] = jnp.concatenate(unpacked, axis=0).T[32 - CARRY : 32, :].astype(jnp.bfloat16)
    carry_copies[0].start()
    carry_copies[1].start()

    part_keys = 3 * chunk_rows if span % (3 * chunk_rows) == 0 else chunk_rows
    row = lax.broadcasted_iota(jnp.int32, (chunk_rows, chunk_rows), 0)
    column = lax.broadcasted_iota(jnp.int32, (chunk_rows, chunk_rows), 1)

    def each_head(allowed, piece):
        return jnp.concatenate(
            [
                jnp.where(allowed, piece[:, head * chunk_rows : (head + 1) * chunk_rows], masked_low)
                for head in range(piece.shape[1] // chunk_rows)
            ],
            axis=1,
        )

    sets = [tuple(range(first, min(first + SET, heads))) for first in range(0, heads, SET)]

    def by_eights(values):
        return values.reshape(values.shape[0] // 8, 8, values.shape[1])

    row_head = lax.broadcasted_iota(jnp.int32, (width, chunk_rows), 0) // HEAD_DIM

    def attend_chunk(chunk):
        begin = chunk * chunk_rows
        floor = jnp.where(place == 0, WINDOW - begin, 0)
        key_at = aligned(LEAD + begin, span, 128)
        query = s.query[:, aligned(LEAD + begin, chunk_rows, chunk_rows)]
        tops, totals = [], []
        for side_heads in sets:
            lanes_of = slice(side_heads[0] * chunk_rows, (side_heads[-1] + 1) * chunk_rows)
            stacked = jnp.concatenate(
                [jnp.where(row_head == head, query, jnp.zeros_like(query)) for head in side_heads], axis=1
            )
            top = None
            for part in range(0, span, part_keys):
                scores = dot(s.keys[aligned(LEAD + begin + part, part_keys, 128), :], stacked)
                for at in range(part, part + part_keys, chunk_rows):
                    piece = scores[at - part : at - part + chunk_rows, :]
                    if at == span - chunk_rows:
                        piece = each_head(row <= column, piece)
                    else:
                        piece = piece + jnp.where(at < floor, masked_low, 0.0)
                        if at == 0:
                            piece = each_head(row > column, piece)
                    s.scores[at : at + chunk_rows, lanes_of] = piece
                    peak = jnp.max(by_eights(piece), axis=0)
                    top = peak if top is None else jnp.maximum(top, peak)
            tops.append(jnp.max(top, axis=0, keepdims=True))
        outs = []
        for which, side_heads in enumerate(sets):
            lanes_of = slice(side_heads[0] * chunk_rows, (side_heads[-1] + 1) * chunk_rows)
            total = jnp.zeros((8, len(side_heads) * chunk_rows), jnp.float32)
            for at in range(0, span, chunk_rows):
                weights = jnp.exp2((s.scores[at : at + chunk_rows, lanes_of] - tops[which]) * EXP2_SCALE)
                total = total + jnp.sum(by_eights(weights), axis=0)
                s.weights[at : at + chunk_rows, lanes_of] = weights.astype(jnp.bfloat16)
            total = jnp.sum(total, axis=0, keepdims=True)
            for index, head in enumerate(side_heads):
                of = slice(head * chunk_rows, (head + 1) * chunk_rows)
                share = dot(s.values[head * HEAD_DIM : (head + 1) * HEAD_DIM, key_at], s.weights[:, of])
                outs.append(share / total[:, index * chunk_rows : (index + 1) * chunk_rows])
        at = mixed_rows(chunk)
        s.mixed[at, :] = jnp.concatenate(outs, axis=0).T.astype(jnp.bfloat16)
        copies = mix_copies(chunk, at)
        copies[0].start()
        copies[1].start()

    def fine_rows(at, start_at):
        merged = dot(s.mixed[at, :], s.cols[:width, :]) + dot(s.others[at, :], s.cols[width:, :])
        value = (s.start[start_at, :].astype(jnp.float32) + merged).astype(jnp.bfloat16).astype(jnp.float32)
        for block in range(lanes):
            s.stream[block, at, :] = value[:, block * 128 : block * 128 + 128]

    peers = (me, sibling, across)
    buffers = (s.send_a, s.recv_a, s.send_b, s.recv_b, s.final)
    short_sum = HeadSum(0, peers, s.part, s.short, buffers, s.sum_send, s.sum_recv)

    def short_rows(chunk):
        return aligned(chunk * group, group, group)

    def relay_chunk(chunk):
        @pl.when(chunk == 0)
        def _():
            carry_copies[0].wait_recv()
            carry_copies[2].start()

        copies = mix_copies(chunk, mixed_rows(chunk))
        copies[0].wait_recv()
        copies[2].start()

    def finish_chunk(chunk):
        @pl.when(chunk == 0)
        def _():
            for copy in column_copies:
                copy.wait_recv()
            loads["cols"].wait()
            loads["ws"].wait()
            carry_copies[1].wait_recv()
            carry_copies[2].wait_recv()
            fine_rows(carry_at, pl.ds(LEAD - CARRY, CARRY))

            @pl.when(place == 0)
            def _():
                s.stream[:, 0:CARRY, :] = jnp.zeros((lanes, CARRY, 128), jnp.float32)

        at = mixed_rows(chunk)
        copies = mix_copies(chunk, at)
        copies[1].wait_recv()
        copies[2].wait_recv()
        fine_rows(at, aligned(LEAD + chunk * chunk_rows, chunk_rows, chunk_rows))
        total = jnp.zeros((group, full), jnp.float32)
        for offset in range(SHORTEN):
            begin = CARRY - (SHORTEN - 1) + offset + chunk * chunk_rows
            member = jnp.concatenate(
                [s.stream[block, pl.ds(begin, group, stride=SHORTEN), :] for block in range(lanes)], axis=1
            )
            total = total + dot(member.astype(jnp.bfloat16), s.ws[offset])
        s.part[short_rows(chunk), :] = total
        short_sum.begin(chunk, short_rows(chunk))

    lane_f = lax.broadcasted_iota(jnp.int32, (rows, 128), 1) % HEAD_DIM
    period_f = periods(lane_f % HALF)
    angle_f = phase(place * rows + lax.broadcasted_iota(jnp.int32, (rows, 128), 0), period_f)
    cos_f = jnp.cos(angle_f)
    sin_f = jnp.where(lane_f < HALF, -jnp.sin(angle_f), jnp.sin(angle_f))
    for block in range(lanes):
        s.coarse_cos[:, block * 128 : block * 128 + 128] = cos_f
        s.coarse_sin[:, block * 128 : block * 128 + 128] = sin_f

    def pair_rows(chunk, source):
        return aligned((chunk * places + source) * group, group, group)

    def pair_copy(chunk, target):
        at = pair_rows(chunk, place)
        return remote(
            s.pair_out.at[target % 2, short_rows(chunk), :], s.pairs.at[at, :],
            s.pair_send.at[target, chunk], s.pair_recv.at[place, chunk], {"seq": target},
        )

    def pair_arrival(chunk, source):
        at = pair_rows(chunk, source)
        return remote(
            s.pairs.at[at, :], s.pairs.at[at, :], s.pair_send.at[source, chunk], s.pair_recv.at[source, chunk],
            {"seq": cross},
        )

    def query_copy(chunk):
        at = short_rows(chunk)
        return remote(
            s.query_out.at[1 - side, at, :], s.queries.at[aligned(side * rows + chunk * group, group, group), :],
            s.query_send.at[chunk], s.query_recv.at[chunk], {"seq": cross},
        )

    def for_targets(chunk, action):
        def one(index, state):
            target = places - 1 - index

            @pl.when((target != place) & ((target // 2 <= level + 2) | (chunk >= FORWARDED)))
            def _():
                action(target)

            return state

        lax.fori_loop(0, places - 2 * level, one, 0)

    forwards = jnp.where(level + 1 < levels, jnp.maximum(2 * (level - 1), 0), 0)

    def forward_copy(chunk, source):
        at = pair_rows(chunk, source)
        return remote(
            s.pairs.at[at, :], s.pairs.at[at, :], s.forward_send.at[source, chunk], s.pair_recv.at[source, chunk],
            {"seq": (place + 2) % places},
        )

    def forward_chunk(chunk):
        def one(source, state):
            pair_arrival(chunk, source).wait_recv()
            forward_copy(chunk, source).start()
            return state

        lax.fori_loop(0, forwards, one, 0)

    def project_chunk(chunk):
        @pl.when(chunk == 0)
        def _():
            for name in ("coarse_gain", "cq", "ck", "cv"):
                loads[name].wait()

        at = short_rows(chunk)
        short_sum.end(chunk, at)
        coarse_in = normed(s.short[at, :].astype(jnp.float32), s.coarse_gain[...])
        cosine, sine = s.coarse_cos[at, :], s.coarse_sin[at, :]
        is_low = lax.broadcasted_iota(jnp.int32, (group, width), 1) % HEAD_DIM < HALF

        def rotated(values):
            other = jnp.where(is_low, pltpu.roll(values, width - HALF, 1), pltpu.roll(values, HALF, 1))
            return (values * cosine + other * sine).astype(jnp.bfloat16)

        key = rotated(dot(coarse_in, s.ck[...]))
        value = dot(coarse_in, s.cv[...]).astype(jnp.bfloat16)
        for half in range(2):
            s.pair_out[half, at, :pair] = key[:, half * pair : half * pair + pair]
            s.pair_out[half, at, pair:] = value[:, half * pair : half * pair + pair]
        for_targets(chunk, lambda target: pair_copy(chunk, target).start())
        query = rotated(dot(coarse_in, s.cq[...]))
        for half in range(2):
            s.query_out[half, at, :] = query[:, half * pair : half * pair + pair]
        query_copy(chunk).start()
        s.pairs[pair_rows(chunk, place), :] = s.pair_out[side, at, :]
        s.queries[aligned(side * rows + chunk * group, group, group), :] = s.query_out[side, at, :]

    def total_chunk(chunk):
        short_sum.total(chunk, short_rows(chunk))

    def middle_chunk(chunk):
        short_sum.middle(chunk, short_rows(chunk))

    ahead = ((RELAY, relay_chunk), (TOTAL, total_chunk))
    behind = ((PROJECT, project_chunk), (MIDDLE, middle_chunk), (FINISH, finish_chunk))

    def one_step(step, state):
        def run(stages):
            for lag, action in stages:
                @pl.when(step >= lag)
                def _():
                    action(step - lag)

        run(ahead)
        attend_chunk(step)
        run(behind)
        return state

    lax.fori_loop(0, chunks, one_step, 0)

    left = {action: max(0, chunks - lag) for lag, action in ahead + behind}
    left[forward_chunk] = 0

    def rest(action, upto):
        upto = min(upto, FORWARDED if action is forward_chunk else chunks, chunks)
        for chunk in range(left[action], upto):
            action(chunk)
        left[action] = max(left[action], upto)

    for action, back in (
        (relay_chunk, 1), (total_chunk, 4), (middle_chunk, 2), (project_chunk, 4), (finish_chunk, 1), (total_chunk, 3),
        (relay_chunk, 0), (middle_chunk, 1), (project_chunk, 3), (finish_chunk, 0), (forward_chunk, 7), (total_chunk, 2),
        (middle_chunk, 0), (project_chunk, 2), (forward_chunk, 6), (total_chunk, 1), (project_chunk, 1),
        (forward_chunk, 5), (total_chunk, 0), (project_chunk, 0), (forward_chunk, 0),
    ):
        rest(action, chunks - back)

    def wait_chunk(chunk):
        def one(source, state):
            @pl.when((source != place) & ((source >= forwards) | (chunk >= FORWARDED)))
            def _():
                pair_arrival(chunk, source).wait_recv()

            return state

        lax.fori_loop(0, 2 * level + 2, one, 0)

    for name in lift_names:
        loads[name].wait()
    part_rows = count // SHORTEN
    for block in range(lanes):
        for begin in range(0, full, part_rows):
            flat = s.raw.at[block, pl.ds(begin, part_rows)].reshape(part_rows * SHORTEN, 128)
            s.spread[block] = flat[...].astype(jnp.float32)
            for member in range(SHORTEN):
                s.lift[begin : begin + part_rows, member * width + block * 128 : member * width + block * 128 + 128] = (
                    s.spread[block, pl.ds(member, part_rows, stride=SHORTEN), :].astype(jnp.bfloat16)
                )

    def wait_queries(chunk, state):
        query_copy(chunk).wait_recv()
        return state

    lax.fori_loop(0, chunks, wait_queries, 0)

    s.top[...] = jnp.full(s.top.shape, masked_low, jnp.float32)
    s.norm[...] = jnp.zeros(s.norm.shape, jnp.float32)
    s.acc[...] = jnp.zeros(s.acc.shape, jnp.float32)
    per_chunk = places * group
    pair_lane = lax.broadcasted_iota(jnp.int32, (2 * rows, pair), 1) // HEAD_DIM
    queries = s.queries[...]

    def key_step(step, state):
        if per_chunk <= STEP_KEYS:
            for inner in range(STEP_KEYS // per_chunk):
                wait_chunk(step * (STEP_KEYS // per_chunk) + inner)
        else:
            ratio = per_chunk // STEP_KEYS

            @pl.when(step % ratio == 0)
            def _():
                wait_chunk(step // ratio)

        block = s.pairs[aligned(step * STEP_KEYS, STEP_KEYS, STEP_KEYS), :]
        keys, values = block[:, :pair], block[:, pair:]
        index = step * STEP_KEYS + lax.broadcasted_iota(jnp.int32, (STEP_KEYS, 1), 0)
        inside = index % per_chunk
        key_at = (inside // group) * rows + (index // per_chunk) * group + inside % group
        query_at = 2 * level * rows + lax.broadcasted_iota(jnp.int32, (1, 2 * rows), 1)
        allowed = key_at <= query_at
        values_t = values.astype(jnp.float32).T.astype(jnp.bfloat16)
        for head in range(pair // HEAD_DIM):
            masked_q = jnp.where(pair_lane == head, queries, jnp.zeros_like(queries))
            scores = jnp.where(allowed, dot_nt(keys, masked_q), masked_low)
            fresh = jnp.maximum(s.top[head], jnp.max(scores, axis=0, keepdims=True))
            factor = jnp.exp2((s.top[head] - fresh) * EXP2_SCALE)
            weights = jnp.exp2((scores - fresh) * EXP2_SCALE)
            s.norm[head] = s.norm[head] * factor + jnp.sum(weights, axis=0, keepdims=True)
            of = slice(head * HEAD_DIM, (head + 1) * HEAD_DIM)
            s.acc[of, :] = s.acc[of, :] * factor + dot(values_t[of, :], weights.astype(jnp.bfloat16))
            s.top[head] = fresh
        return state

    lax.fori_loop(0, places * rows // STEP_KEYS, key_step, 0)

    def turn_copy():
        return remote(
            s.turn, s.heads_in.at[:, aligned(side * pair, pair, pair)],
            s.turn_send.at[0], s.turn_recv.at[0], {"seq": cross},
        )

    def mixed_of(at):
        shares = [
            s.acc[head * HEAD_DIM : (head + 1) * HEAD_DIM, at] / s.norm[head, :, at] for head in range(pair // HEAD_DIM)
        ]
        return jnp.concatenate(shares, axis=0).T.astype(jnp.bfloat16)

    s.turn[...] = mixed_of(aligned((1 - side) * rows, rows, rows))
    turn_copy().start()
    s.heads_in[:, aligned(side * pair, pair, pair)] = mixed_of(aligned(side * rows, rows, rows))

    for steps in (1, 2):
        @pl.when(place + steps < places)
        def _():
            id_copy(steps).wait_send()

    for copy in column_copies:
        copy.wait_send()
    for copy in carry_copies:
        copy.wait_send()

    def drain(chunk, state):
        for copy in mix_copies(chunk, mixed_rows(chunk)):
            copy.wait_send()
        short_sum.drain(chunk, short_rows(chunk))
        for_targets(chunk, lambda target: pair_copy(chunk, target).wait_send())

        @pl.when(chunk < FORWARDED)
        def _():
            def one(source, inner):
                forward_copy(chunk, source).wait_send()
                return inner

            lax.fori_loop(0, forwards, one, 0)

        query_copy(chunk).wait_send()
        return state

    lax.fori_loop(0, chunks, drain, 0)
    loads["co"].wait()
    turn_copy().wait_recv()

    out_sum = HeadSum(1, peers, s.part, s.summed, buffers, s.sum_send, s.sum_recv)
    ffn_sum = HeadSum(2, peers, s.part_b, s.second, buffers, s.sum_send, s.sum_recv)
    size = rows // PIECES
    at = [pl.ds(piece * size, size) for piece in range(PIECES)]

    for piece in range(PIECES):
        s.part[at[piece], :] = dot(s.heads_in[at[piece], :], s.co[...])
        out_sum.begin(piece, at[piece])
    for name in ("ffn_gain", "up", "down"):
        loads[name].wait()
    for piece in range(PIECES):
        out_sum.middle(piece, at[piece])

    def feed(piece):
        out_sum.end(piece, at[piece])
        value = s.short[at[piece], :].astype(jnp.float32) + s.summed[at[piece], :].astype(jnp.float32)
        s.first[at[piece], :] = value
        inner = jax.nn.gelu(dot(normed(value, s.ffn_gain[...]), s.up[...])).astype(jnp.bfloat16)
        s.part_b[at[piece], :] = dot(inner, s.down[...])
        ffn_sum.begin(piece, at[piece])

    def raise_rows(piece):
        ffn_sum.end(piece, at[piece])
        for member in range(SHORTEN):
            lifted = dot(s.second[at[piece], :], s.lift[:, member * width : (member + 1) * width])
            for block in range(lanes):
                s.spread[block, pl.ds(SHORTEN * size * piece + member, size, stride=SHORTEN), :] = lifted[
                    :, block * 128 : block * 128 + 128
                ]
        for block in range(lanes):
            to = slice(SHORTEN * size * piece, SHORTEN * size * (piece + 1))
            base_at = slice(CARRY + SHORTEN * size * piece, CARRY + SHORTEN * size * (piece + 1))
            out_ref[to, block * 128 : block * 128 + 128] = (
                s.stream[block, base_at, :] + s.spread[block, to, :]
            ).astype(jnp.bfloat16)

    for step in range(PIECES + 4):
        if step < PIECES:
            out_sum.total(step, at[step])
        if 0 <= step - 1 < PIECES:
            feed(step - 1)
        if 0 <= step - 2 < PIECES:
            ffn_sum.middle(step - 2, at[step - 2])
        if 0 <= step - 3 < PIECES:
            ffn_sum.total(step - 3, at[step - 3], s.first)
        if 0 <= step - 4 < PIECES:
            raise_rows(step - 4)

    turn_copy().wait_send()
    for piece in range(PIECES):
        out_sum.drain(piece, at[piece])
        ffn_sum.drain(piece, at[piece])


def local(
    token_ids,
    embedding,
    fine_norm,
    fine_query,
    fine_key,
    fine_value,
    fine_output,
    shorten_weight,
    coarse_norm,
    coarse_query,
    coarse_key,
    coarse_value,
    coarse_output,
    ffn_norm,
    ffn_up,
    ffn_down,
    upsample_weight,
):
    count = token_ids.shape[0]
    width = fine_query.shape[1]
    chunk_rows = min(128, count)
    chunks = count // chunk_rows
    scratch = scratch_list(count, width, chunks, lax.axis_size("seq"))
    names = [name for name, _ in scratch]

    def kernel(*refs):
        block_kernel(names, chunk_rows, *refs)

    return pl.pallas_call(
        kernel,
        out_shape=jax.ShapeDtypeStruct((count, width), jnp.bfloat16),
        in_specs=[HBM_SPEC] * 17,
        out_specs=VMEM_SPEC,
        scratch_shapes=[shape for _, shape in scratch],
        compiler_params=pltpu.CompilerParams(
            collective_id=1, has_side_effects=True, vmem_limit_bytes=46 * 2**20
        ),
        name="block_kernel",
    )(
        *(
            pltpu.with_memory_space_constraint(array, pltpu.HBM)
            for array in (
                token_ids.reshape(1, count), fine_norm.reshape(1, D), coarse_norm.reshape(1, D), ffn_norm.reshape(1, D),
                embedding, fine_query, fine_key, fine_value, fine_output, shorten_weight, coarse_query, coarse_key,
                coarse_value, coarse_output, ffn_up, ffn_down, upsample_weight,
            )
        ),
    )


def solution(mesh):
    return jax.shard_map(
        local,
        mesh=mesh,
        in_specs=(
            P("seq"),
            P(),
            P(),
            P(None, "head"),
            P(None, "head"),
            P(None, "head"),
            P("head", None),
            P(None, "head", None),
            P(),
            P(None, "head"),
            P(None, "head"),
            P(None, "head"),
            P("head", None),
            P(),
            P(None, "head"),
            P("head", None),
            P(None, None, "head"),
        ),
        out_specs=P("seq", "head"),
        check_vma=False,
    )
```

```python
import math

import jax
import jax.numpy as jnp
from jax import lax
from jax.experimental import pallas as pl
from jax.experimental.pallas import tpu as pltpu
from jax.sharding import PartitionSpec as P

D = 1024
HEAD_DIM = 64
HALF = HEAD_DIM // 2
SHORTEN = 4
WINDOW = 1024
LEAD = 128
CARRY = 16

epsilon = 1e-06
masked_low = -1e30
MESH = pl.DeviceIdType.MESH
EXP2_SCALE = HEAD_DIM ** (-0.5) * math.log2(math.e)
VMEM_SPEC = pl.BlockSpec(memory_space=pltpu.VMEM)
HBM_SPEC = pl.BlockSpec(memory_space=pltpu.HBM)

RELAY, FINISH, MIDDLE, TOTAL, PROJECT = (2, 2, 3, 5, 5)
STEP_KEYS = 512
PIECES = 4
SET = 2


def dot(left, right):
    return jnp.dot(left, right, preferred_element_type=jnp.float32)


def dot_nt(left, right):
    return lax.dot_general(left, right, (((1,), (1,)), ((), ())), preferred_element_type=jnp.float32)


def dot_tn(left, right):
    return lax.dot_general(left, right, (((0,), (0,)), ((), ())), preferred_element_type=jnp.float32)


def normed(data, gain):
    power = jnp.mean(data * data, axis=1, keepdims=True)
    return (data * lax.rsqrt(power + epsilon) * gain).astype(jnp.bfloat16)


def aligned(start, size, unit):
    return pl.ds(pl.multiple_of(start, unit), size)


def periods(column):
    log = 4 + lax.shift_right_logical(column * 14, 5)
    return jnp.left_shift(jnp.ones_like(log), log)


def phase(position, period):
    cycle = jnp.bitwise_and(position, period - 1).astype(jnp.float32)
    return cycle * (2.0 * math.pi / period.astype(jnp.float32))


def remote(source, target, send, receive, device):
    return pltpu.make_async_remote_copy(
        src_ref=source, dst_ref=target, send_sem=send, recv_sem=receive, device_id=device, device_id_type=MESH
    )


class HeadSum:
    def __init__(self, index, peers, part, out, buffers, send_sem, recv_sem):
        self.index = index
        self.me, self.sibling, self.across = peers
        self.part, self.out = part, out
        self.send_a, self.recv_a, self.send_b, self.recv_b, self.final = (buffer.at[index] for buffer in buffers)
        self.send_sem, self.recv_sem = send_sem, recv_sem
        half = part.shape[1] // 2
        self.mine = aligned((self.me % 2) * half, half, half)
        self.theirs = aligned((self.sibling % 2) * half, half, half)

    def copy(self, kind, piece, source, target, device):
        return remote(
            source, target, self.send_sem.at[self.index, kind, piece], self.recv_sem.at[self.index, kind, piece],
            {"head": device},
        )

    def copy_a(self, piece, at):
        return self.copy(0, piece, self.send_a.at[at, :], self.recv_a.at[at, :], self.sibling)

    def copy_b(self, piece, at):
        return self.copy(1, piece, self.send_b.at[at, :], self.recv_b.at[at, :], self.across)

    def copy_c(self, piece, at):
        return self.copy(2, piece, self.final.at[at, :], self.out.at[at, self.mine], self.sibling)

    def begin(self, piece, at):
        self.send_a[at, :] = self.part[at, self.theirs].astype(jnp.bfloat16)
        self.copy_a(piece, at).start()

    def middle(self, piece, at):
        self.copy_a(piece, at).wait_recv()
        summed = self.part[at, self.mine] + self.recv_a[at, :].astype(jnp.float32)
        self.part[at, self.mine] = summed
        self.send_b[at, :] = summed.astype(jnp.bfloat16)
        self.copy_b(piece, at).start()

    def total(self, piece, at, residual=None):
        self.copy_b(piece, at).wait_recv()
        value = self.part[at, self.mine] + self.recv_b[at, :].astype(jnp.float32)
        if residual is not None:
            value = value + residual[at, self.mine]
        value = value.astype(jnp.bfloat16)
        self.final[at, :] = value
        self.copy_c(piece, at).start()
        self.out[at, self.mine] = value

    def end(self, piece, at):
        self.copy_c(piece, at).wait_recv()

    def drain(self, piece, at):
        self.copy_a(piece, at).wait_send()
        self.copy_b(piece, at).wait_send()
        self.copy_c(piece, at).wait_send()


def scratch_list(count, width, chunks, places):
    full = 4 * width
    rows = count // SHORTEN
    frame = LEAD + WINDOW + count
    low = jnp.bfloat16
    wide = jnp.float32
    dma = pltpu.SemaphoreType.DMA
    return [
        ("emb", pltpu.VMEM((256, full), low)),
        ("fq", pltpu.VMEM((full, width), low)),
        ("fk", pltpu.VMEM((full, width), low)),
        ("fv", pltpu.VMEM((full, width), low)),
        ("cols", pltpu.VMEM((full, width), low)),
        ("ws", pltpu.VMEM((SHORTEN, width, full), low)),
        ("cq", pltpu.VMEM((full, width), low)),
        ("ck", pltpu.VMEM((full, width), low)),
        ("cv", pltpu.VMEM((full, width), low)),
        ("co", pltpu.VMEM((width, full), low)),
        ("up", pltpu.VMEM((full, full), low)),
        ("down", pltpu.VMEM((full, full), low)),
        ("lift", pltpu.VMEM((full, SHORTEN * width), low)),
        ("raw", pltpu.VMEM((width // 128, full, SHORTEN, 128), low)),
        ("fine_gain", pltpu.VMEM((1, full), wide)),
        ("coarse_gain", pltpu.VMEM((1, full), wide)),
        ("ffn_gain", pltpu.VMEM((1, full), wide)),
        ("load_sem", dma((17 + width // 128,))),
        ("ids", pltpu.VMEM((1, frame), jnp.int32)),
        ("id_send", dma((2,))),
        ("id_recv", dma((2,))),
        ("col_send", dma((4,))),
        ("col_recv", dma((4,))),
        ("tabs", pltpu.VMEM((6, 256, width), low)),
        ("cos_t", pltpu.VMEM((HALF, frame), wide)),
        ("sin_t", pltpu.VMEM((HALF, frame), wide)),
        ("keys", pltpu.VMEM((frame, width), low)),
        ("values", pltpu.VMEM((width, frame), low)),
        ("query", pltpu.VMEM((width, LEAD + count), low)),
        ("start", pltpu.VMEM((LEAD + count, width), low)),
        ("scores", pltpu.VMEM((WINDOW + count // chunks, 4 * (count // chunks)), wide)),
        ("weights", pltpu.VMEM((WINDOW + count // chunks, 4 * (count // chunks)), low)),
        ("mixed", pltpu.VMEM((CARRY + count, width), low)),
        ("others", pltpu.VMEM((CARRY + count, 3 * width), low)),
        ("mix_send", dma((3, chunks + 1))),
        ("mix_recv", dma((3, chunks + 1))),
        ("stream", pltpu.VMEM((width // 128, CARRY + count, 128), wide)),
        ("part", pltpu.VMEM((rows, full), wide)),
        ("part_b", pltpu.VMEM((rows, full), wide)),
        ("short", pltpu.VMEM((rows, full), low)),
        ("summed", pltpu.VMEM((rows, full), low)),
        ("first", pltpu.VMEM((rows, full), wide)),
        ("second", pltpu.VMEM((rows, full), low)),
        ("send_a", pltpu.VMEM((3, rows, full // 2), low)),
        ("recv_a", pltpu.VMEM((3, rows, full // 2), low)),
        ("send_b", pltpu.VMEM((3, rows, full // 2), low)),
        ("recv_b", pltpu.VMEM((3, rows, full // 2), low)),
        ("final", pltpu.VMEM((3, rows, full // 2), low)),
        ("sum_send", dma((3, 3, chunks))),
        ("sum_recv", dma((3, 3, chunks))),
        ("coarse_cos", pltpu.VMEM((rows, width), wide)),
        ("coarse_sin", pltpu.VMEM((rows, width), wide)),
        ("pair_out", pltpu.VMEM((2, rows, width), low)),
        ("query_out", pltpu.VMEM((2, rows, width // 2), low)),
        ("pairs", pltpu.VMEM((places * rows, width), low)),
        ("queries", pltpu.VMEM((2 * rows, width // 2), low)),
        ("pair_send", dma((places, chunks))),
        ("pair_recv", dma((places, chunks))),
        ("query_send", dma((chunks,))),
        ("query_recv", dma((chunks,))),
        ("top", pltpu.VMEM((2, 1, 2 * rows), wide)),
        ("norm", pltpu.VMEM((2, 1, 2 * rows), wide)),
        ("acc", pltpu.VMEM((width // 2, 2 * rows), wide)),
        ("turn", pltpu.VMEM((rows, width // 2), low)),
        ("heads_in", pltpu.VMEM((rows, width), low)),
        ("turn_send", dma((PIECES,))),
        ("turn_recv", dma((PIECES,))),
        ("spread", pltpu.VMEM((width // 128, count, 128), wide)),
    ]


class Names:
    pass


def block_kernel(names, chunk_rows, *refs):
    (ids_h, fine_gain_h, coarse_gain_h, ffn_gain_h, emb_h, fq_h, fk_h, fv_h, fo_h, ws_h,
     cq_h, ck_h, cv_h, co_h, up_h, down_h, lift_h, out_ref) = refs[:18]
    s = Names()
    for name, ref in zip(names, refs[18:]):
        setattr(s, name, ref)
    count, width = out_ref.shape
    full = 4 * width
    heads = width // HEAD_DIM
    chunks = count // chunk_rows
    group = chunk_rows // SHORTEN
    rows = count // SHORTEN
    frame = LEAD + WINDOW + count
    span = WINDOW + chunk_rows
    lanes = width // 128
    pair = width // 2

    places = lax.axis_size("seq")
    place = lax.axis_index("seq")
    levels = places // 2
    side = place % 2
    level = place // 2
    cross = place + 1 - 2 * side
    me = lax.axis_index("head")
    sibling = me + 1 - 2 * (me % 2)
    across = (me + 2) % 4
    diagonal = (sibling + 2) % 4

    barrier = pltpu.get_barrier_semaphore()
    for device in (sibling, across, diagonal):
        pl.semaphore_signal(barrier, inc=1, device_id={"head": device}, device_id_type=MESH)

    def greet(step, state):
        pl.semaphore_signal(
            barrier, inc=1, device_id={"seq": (place + step) % places}, device_id_type=MESH
        )
        return state

    lax.fori_loop(1, places, greet, 0)

    own_columns = aligned(me * width, width, width)
    own_ids = s.ids.at[:, pl.ds(LEAD + WINDOW, count)]
    loads = {
        name: pltpu.make_async_copy(source, target, s.load_sem.at[index])
        for index, (name, source, target) in enumerate((
            ("ids", ids_h, own_ids), ("emb", emb_h, s.emb), ("fine_gain", fine_gain_h, s.fine_gain),
            ("fk", fk_h, s.fk), ("fv", fv_h, s.fv), ("fq", fq_h, s.fq),
            ("coarse_gain", coarse_gain_h, s.coarse_gain), ("ffn_gain", ffn_gain_h, s.ffn_gain),
            ("cols", fo_h.at[:, own_columns], s.cols.at[pl.ds(0, width), :]),
            ("ws", ws_h, s.ws), ("cq", cq_h, s.cq), ("ck", ck_h, s.ck), ("cv", cv_h, s.cv), ("co", co_h, s.co),
            ("up", up_h, s.up), ("down", down_h, s.down),
            *((f"lift{b}", lift_h.at[:, :, pl.ds(b * 128, 128)], s.raw.at[b]) for b in range(lanes)),
        ))
    }
    lift_names = tuple(f"lift{block}" for block in range(lanes))

    def start_loads(*names):
        for name in names:
            loads[name].start()

    start_loads("ids", "emb", "fine_gain", "fk", "fv", "fq")

    @pl.when(place < 1)
    def _():
        s.ids[:, LEAD : LEAD + WINDOW] = jnp.zeros((1, WINDOW), jnp.int32)

    @pl.when(place < 2)
    def _():
        s.ids[:, :LEAD] = jnp.zeros((1, LEAD), jnp.int32)

    def clear(index, state):
        chunk = index // (places - 2)
        blank = index % (places - 2)

        @pl.when(blank + 2 >= 2 * level + 2)
        def _():
            at = aligned((chunk * places + blank + 2) * group, group, group)
            s.pairs[at, :] = jnp.zeros((group, width), jnp.bfloat16)

        return state

    lax.fori_loop(0, chunks * (places - 2), clear, 0)

    column = lax.broadcasted_iota(jnp.int32, (HALF, 128), 0)
    lane = lax.broadcasted_iota(jnp.int32, (HALF, 128), 1)
    period = periods(column)
    small = phase(lane, period)
    base = (place - 1) * count - LEAD
    large = phase(base + 128 * lane, period)
    cos_b, sin_b, cos_a, sin_a = jnp.cos(small), jnp.sin(small), jnp.cos(large), jnp.sin(large)
    for block in range(frame // 128):
        at = slice(block * 128, block * 128 + 128)
        cos_k, sin_k = cos_a[:, block : block + 1], sin_a[:, block : block + 1]
        s.cos_t[:, at] = cos_b * cos_k - sin_b * sin_k
        s.sin_t[:, at] = sin_b * cos_k + cos_b * sin_k

    lane_f = lax.broadcasted_iota(jnp.int32, (rows, 128), 1) % HEAD_DIM
    period_f = periods(lane_f % HALF)
    angle_f = phase(place * rows + lax.broadcasted_iota(jnp.int32, (rows, 128), 0), period_f)
    cos_f = jnp.cos(angle_f)
    sin_f = jnp.where(lane_f < HALF, -jnp.sin(angle_f), jnp.sin(angle_f))
    for block in range(lanes):
        s.coarse_cos[:, block * 128 : block * 128 + 128] = cos_f
        s.coarse_sin[:, block * 128 : block * 128 + 128] = sin_f

    pl.semaphore_wait(barrier, places + 2)

    def id_copy(steps):
        if steps == 1:
            target = s.ids.at[:, pl.ds(LEAD, WINDOW)]
            source = ids_h
        else:
            target = s.ids.at[:, pl.ds(0, LEAD)]
            source = ids_h.at[:, pl.ds(count - LEAD, LEAD)]
        device = (place + steps) % places
        return remote(source, target, s.id_send.at[steps - 1], s.id_recv.at[steps - 1], {"seq": device})

    for steps in (1, 2):
        @pl.when(place + steps < places)
        def _():
            id_copy(steps).start()

    def column_copy(flip, device):
        return remote(
            fo_h.at[:, aligned(device * width, width, width)], s.cols.at[pl.ds(flip * width, width), :],
            s.col_send.at[flip], s.col_recv.at[flip], {"head": device},
        )

    column_copies = [column_copy(flip, device) for flip, device in ((1, sibling), (2, across), (3, diagonal))]
    for copy in column_copies:
        copy.start()

    loads["emb"].wait()
    loads["fine_gain"].wait()
    level_in = normed(s.emb[...].astype(jnp.float32), s.fine_gain[...])

    def split(values):
        high = values.astype(jnp.bfloat16)
        return high, (values - high.astype(jnp.float32)).astype(jnp.bfloat16)

    loads["fk"].wait()
    s.tabs[0], s.tabs[1] = split(dot(level_in, s.fk[...]).T)
    loads["fv"].wait()
    s.tabs[2] = dot(level_in, s.fv[...]).T.astype(jnp.bfloat16)
    loads["fq"].wait()
    s.tabs[3], s.tabs[4] = split(dot(level_in, s.fq[...]).T)
    s.tabs[5] = s.emb[:, own_columns]
    loads["ids"].wait()
    start_loads("cols", "ws", "coarse_gain", "ffn_gain", "cq", "ck", "cv")

    def turned(joined, at):
        cosine, sine = s.cos_t[:, at], s.sin_t[:, at]
        pieces = []
        for head in range(heads):
            low = joined[head * HEAD_DIM : head * HEAD_DIM + HALF]
            high = joined[head * HEAD_DIM + HALF : (head + 1) * HEAD_DIM]
            pieces += [low * cosine - high * sine, high * cosine + low * sine]
        return jnp.concatenate(pieces, axis=0)

    def hot_rows(at, size):
        levels_at = lax.broadcasted_iota(jnp.int32, (256, size), 0)
        return jnp.where(levels_at == s.ids[:, at], 1.0, 0.0).astype(jnp.bfloat16)

    def key_rows(begin, size):
        at = aligned(begin, size, 128)
        hot = hot_rows(at, size)
        s.keys[at, :] = turned(dot(s.tabs[0], hot) + dot(s.tabs[1], hot), at).T.astype(jnp.bfloat16)
        s.values[:, at] = dot(s.tabs[2], hot).astype(jnp.bfloat16)

    def query_rows(begin, size):
        at = aligned(begin, size, 128)
        to = aligned(begin - WINDOW, size, 128)
        hot = hot_rows(at, size)
        s.query[:, to] = turned(dot(s.tabs[3], hot) + dot(s.tabs[4], hot), at).astype(jnp.bfloat16)
        s.start[to, :] = dot_tn(hot, s.tabs[5]).astype(jnp.bfloat16)

    own_block = min(512, count)

    def own_rows(index, state):
        key_rows(LEAD + WINDOW + index * own_block, own_block)
        query_rows(LEAD + WINDOW + index * own_block, own_block)
        return state

    def prior_rows(index, state):
        key_rows(index * 384, 384)
        return state

    lax.fori_loop(0, count // own_block, own_rows, 0)
    for steps in (1, 2):
        @pl.when(place >= steps)
        def _():
            id_copy(steps).wait_recv()

    lax.fori_loop(0, (LEAD + WINDOW) // 384, prior_rows, 0)
    query_rows(WINDOW, LEAD)

    def weigh(scores):
        top = scores[0]
        for piece in scores[1:]:
            top = jnp.maximum(top, piece)
        top = jnp.max(top, axis=0, keepdims=True)
        weights = [jnp.exp2((piece - top) * EXP2_SCALE) for piece in scores]
        total = weights[0]
        for piece in weights[1:]:
            total = total + piece
        total = jnp.sum(total, axis=0, keepdims=True)
        return jnp.concatenate([piece.astype(jnp.bfloat16) for piece in weights], axis=0), total

    def mixed_rows(chunk):
        return aligned(CARRY + chunk * chunk_rows, chunk_rows, CARRY)

    def mix_copies(chunk, at):
        def slot(which):
            return s.others.at[at, pl.ds((which - 1) * width, width)]

        def copy(kind, source, target, device):
            return remote(source, target, s.mix_send.at[kind, chunk], s.mix_recv.at[kind, chunk], {"head": device})

        return (
            copy(0, s.mixed.at[at, :], slot(2), across),
            copy(1, s.mixed.at[at, :], slot(1), sibling),
            copy(2, slot(2), slot(3), sibling),
        )

    carry_at = pl.ds(0, CARRY)
    carry_copies = mix_copies(chunks, carry_at)

    start_loads("co", "up", "down", *lift_names)

    def attend_carry():
        lane_slot = lax.broadcasted_iota(jnp.int32, (HEAD_DIM, LEAD), 1) // 32
        packed = []
        for head in range(heads):
            rolled = pltpu.roll(s.query[head * HEAD_DIM : (head + 1) * HEAD_DIM, :LEAD].astype(jnp.float32), (32 * head + 32) % LEAD, 1)
            packed.append(jnp.where(lane_slot == head, rolled, 0.0))
        packed = jnp.concatenate(packed, axis=0).astype(jnp.bfloat16)
        scores = dot(s.keys[: LEAD + WINDOW, :], packed)
        key = lax.broadcasted_iota(jnp.int32, scores.shape, 0)
        last = lax.broadcasted_iota(jnp.int32, scores.shape, 1) % 32 + (LEAD + WINDOW - 32)
        floor = jnp.where(place < 2, LEAD, 0)
        allowed = (key > last - WINDOW) & (key <= last) & (key >= floor)
        weights, total = weigh([jnp.where(allowed, scores, masked_low)])
        out = dot(s.values[:, : LEAD + WINDOW], weights) / total
        unpacked = [
            pltpu.roll(out[head * HEAD_DIM : (head + 1) * HEAD_DIM, :], (LEAD - 32 * head) % LEAD, 1) for head in range(heads)
        ]
        s.mixed[carry_at, :] = jnp.concatenate(unpacked, axis=0).T[32 - CARRY : 32, :].astype(jnp.bfloat16)
        carry_copies[0].start()
        carry_copies[1].start()

    part_keys = 3 * chunk_rows if span % (3 * chunk_rows) == 0 else chunk_rows
    row = lax.broadcasted_iota(jnp.int32, (chunk_rows, chunk_rows), 0)
    column = lax.broadcasted_iota(jnp.int32, (chunk_rows, chunk_rows), 1)

    def each_head(allowed, piece):
        return jnp.concatenate(
            [
                jnp.where(allowed, piece[:, head * chunk_rows : (head + 1) * chunk_rows], masked_low)
                for head in range(piece.shape[1] // chunk_rows)
            ],
            axis=1,
        )

    sets = [tuple(range(first, min(first + SET, heads))) for first in range(0, heads, SET)]

    def by_eights(values):
        return values.reshape(values.shape[0] // 8, 8, values.shape[1])

    row_head = lax.broadcasted_iota(jnp.int32, (width, chunk_rows), 0) // HEAD_DIM

    def attend_chunk(chunk):
        begin = chunk * chunk_rows
        floor = jnp.where(place == 0, WINDOW - begin, 0)
        key_at = aligned(LEAD + begin, span, 128)
        query = s.query[:, aligned(LEAD + begin, chunk_rows, chunk_rows)]
        tops, totals = [], []
        for side_heads in sets:
            lanes_of = slice(side_heads[0] * chunk_rows, (side_heads[-1] + 1) * chunk_rows)
            stacked = jnp.concatenate(
                [jnp.where(row_head == head, query, jnp.zeros_like(query)) for head in side_heads], axis=1
            )
            top = None
            for part in range(0, span, part_keys):
                scores = dot(s.keys[aligned(LEAD + begin + part, part_keys, 128), :], stacked)
                for at in range(part, part + part_keys, chunk_rows):
                    piece = scores[at - part : at - part + chunk_rows, :]
                    if at == span - chunk_rows:
                        piece = each_head(row <= column, piece)
                    else:
                        piece = piece + jnp.where(at < floor, masked_low, 0.0)
                        if at == 0:
                            piece = each_head(row > column, piece)
                    s.scores[at : at + chunk_rows, lanes_of] = piece
                    peak = jnp.max(by_eights(piece), axis=0)
                    top = peak if top is None else jnp.maximum(top, peak)
            tops.append(jnp.max(top, axis=0, keepdims=True))
        outs = []
        for which, side_heads in enumerate(sets):
            lanes_of = slice(side_heads[0] * chunk_rows, (side_heads[-1] + 1) * chunk_rows)
            total = jnp.zeros((8, len(side_heads) * chunk_rows), jnp.float32)
            for at in range(0, span, chunk_rows):
                weights = jnp.exp2((s.scores[at : at + chunk_rows, lanes_of] - tops[which]) * EXP2_SCALE)
                total = total + jnp.sum(by_eights(weights), axis=0)
                s.weights[at : at + chunk_rows, lanes_of] = weights.astype(jnp.bfloat16)
            total = jnp.sum(total, axis=0, keepdims=True)
            for index, head in enumerate(side_heads):
                of = slice(head * chunk_rows, (head + 1) * chunk_rows)
                share = dot(s.values[head * HEAD_DIM : (head + 1) * HEAD_DIM, key_at], s.weights[:, of])
                outs.append(share / total[:, index * chunk_rows : (index + 1) * chunk_rows])
        at = mixed_rows(chunk)
        s.mixed[at, :] = jnp.concatenate(outs, axis=0).T.astype(jnp.bfloat16)
        copies = mix_copies(chunk, at)
        copies[0].start()
        copies[1].start()

    def fine_rows(at, start_at):
        merged = dot(s.mixed[at, :], s.cols[:width, :]) + dot(s.others[at, :], s.cols[width:, :])
        value = (s.start[start_at, :].astype(jnp.float32) + merged).astype(jnp.bfloat16).astype(jnp.float32)
        for block in range(lanes):
            s.stream[block, at, :] = value[:, block * 128 : block * 128 + 128]

    peers = (me, sibling, across)
    buffers = (s.send_a, s.recv_a, s.send_b, s.recv_b, s.final)
    short_sum = HeadSum(0, peers, s.part, s.short, buffers, s.sum_send, s.sum_recv)

    def short_rows(chunk):
        return aligned(chunk * group, group, group)

    def relay_chunk(chunk):
        @pl.when(chunk == 0)
        def _():
            carry_copies[0].wait_recv()
            carry_copies[2].start()

        copies = mix_copies(chunk, mixed_rows(chunk))
        copies[0].wait_recv()
        copies[2].start()

    def finish_chunk(chunk):
        @pl.when(chunk == 0)
        def _():
            for copy in column_copies:
                copy.wait_recv()
            loads["cols"].wait()
            loads["ws"].wait()
            carry_copies[1].wait_recv()
            carry_copies[2].wait_recv()
            fine_rows(carry_at, pl.ds(LEAD - CARRY, CARRY))

            @pl.when(place == 0)
            def _():
                s.stream[:, 0:CARRY, :] = jnp.zeros((lanes, CARRY, 128), jnp.float32)

        at = mixed_rows(chunk)
        copies = mix_copies(chunk, at)
        copies[1].wait_recv()
        copies[2].wait_recv()
        fine_rows(at, aligned(LEAD + chunk * chunk_rows, chunk_rows, chunk_rows))
        total = jnp.zeros((group, full), jnp.float32)
        for offset in range(SHORTEN):
            begin = CARRY - (SHORTEN - 1) + offset + chunk * chunk_rows
            member = jnp.concatenate(
                [s.stream[block, pl.ds(begin, group, stride=SHORTEN), :] for block in range(lanes)], axis=1
            )
            total = total + dot(member.astype(jnp.bfloat16), s.ws[offset])
        s.part[short_rows(chunk), :] = total
        short_sum.begin(chunk, short_rows(chunk))

    def pair_rows(chunk, source):
        return aligned((chunk * places + source) * group, group, group)

    def pair_copy(chunk, target):
        at = pair_rows(chunk, place)
        return remote(
            s.pair_out.at[target % 2, short_rows(chunk), :], s.pairs.at[at, :],
            s.pair_send.at[target, chunk], s.pair_recv.at[place, chunk], {"seq": target},
        )

    def pair_arrival(chunk, source):
        at = pair_rows(chunk, source)
        return remote(
            s.pairs.at[at, :], s.pairs.at[at, :], s.pair_send.at[source, chunk], s.pair_recv.at[source, chunk],
            {"seq": cross},
        )

    def query_copy(chunk):
        at = short_rows(chunk)
        return remote(
            s.query_out.at[1 - side, at, :], s.queries.at[aligned(side * rows + chunk * group, group, group), :],
            s.query_send.at[chunk], s.query_recv.at[chunk], {"seq": cross},
        )

    def for_targets(action):
        def one(index, state):
            target = places - 1 - index

            @pl.when(target != place)
            def _():
                action(target)

            return state

        lax.fori_loop(0, places - 2 * level, one, 0)

    def project_chunk(chunk):
        @pl.when(chunk == 0)
        def _():
            for name in ("coarse_gain", "cq", "ck", "cv"):
                loads[name].wait()

        at = short_rows(chunk)
        short_sum.end(chunk, at)
        coarse_in = normed(s.short[at, :].astype(jnp.float32), s.coarse_gain[...])
        cosine, sine = s.coarse_cos[at, :], s.coarse_sin[at, :]
        is_low = lax.broadcasted_iota(jnp.int32, (group, width), 1) % HEAD_DIM < HALF

        def rotated(values):
            other = jnp.where(is_low, pltpu.roll(values, width - HALF, 1), pltpu.roll(values, HALF, 1))
            return (values * cosine + other * sine).astype(jnp.bfloat16)

        key = rotated(dot(coarse_in, s.ck[...]))
        value = dot(coarse_in, s.cv[...]).astype(jnp.bfloat16)
        for half in range(2):
            s.pair_out[half, at, :pair] = key[:, half * pair : half * pair + pair]
            s.pair_out[half, at, pair:] = value[:, half * pair : half * pair + pair]
        for_targets(lambda target: pair_copy(chunk, target).start())
        query = rotated(dot(coarse_in, s.cq[...]))
        for half in range(2):
            s.query_out[half, at, :] = query[:, half * pair : half * pair + pair]
        query_copy(chunk).start()
        s.pairs[pair_rows(chunk, place), :] = s.pair_out[side, at, :]
        s.queries[aligned(side * rows + chunk * group, group, group), :] = s.query_out[side, at, :]

    def total_chunk(chunk):
        short_sum.total(chunk, short_rows(chunk))

    def middle_chunk(chunk):
        short_sum.middle(chunk, short_rows(chunk))

    ahead = ((RELAY, relay_chunk), (TOTAL, total_chunk))
    behind = ((PROJECT, project_chunk), (MIDDLE, middle_chunk), (FINISH, finish_chunk))

    def one_step(step, state):
        def run(stages):
            for lag, action in stages:
                @pl.when(step >= lag)
                def _():
                    action(step - lag)

        run(ahead)
        attend_chunk(step)

        @pl.when(step == 0)
        def _():
            attend_carry()

        run(behind)
        return state

    lax.fori_loop(0, chunks, one_step, 0)

    left = {action: max(0, chunks - lag) for lag, action in ahead + behind}

    def rest(action, upto):
        for chunk in range(left[action], upto):
            action(chunk)
        left[action] = max(left[action], upto)

    for action, back in (
        (relay_chunk, 1), (total_chunk, 4), (middle_chunk, 2), (project_chunk, 4), (finish_chunk, 1), (total_chunk, 3),
        (relay_chunk, 0), (middle_chunk, 1), (project_chunk, 3), (finish_chunk, 0), (total_chunk, 2),
        (middle_chunk, 0), (project_chunk, 2), (total_chunk, 1), (project_chunk, 1),
        (total_chunk, 0), (project_chunk, 0),
    ):
        rest(action, chunks - back)

    def wait_chunk(chunk):
        def one(source, state):
            pair_arrival(chunk, source).wait_recv()
            return state

        lax.fori_loop(0, 2 * level, one, 0)

    for name in lift_names:
        loads[name].wait()
    part_rows = count // SHORTEN
    for block in range(lanes):
        for begin in range(0, full, part_rows):
            flat = s.raw.at[block, pl.ds(begin, part_rows)].reshape(part_rows * SHORTEN, 128)
            s.spread[block] = flat[...].astype(jnp.float32)
            for member in range(SHORTEN):
                s.lift[begin : begin + part_rows, member * width + block * 128 : member * width + block * 128 + 128] = (
                    s.spread[block, pl.ds(member, part_rows, stride=SHORTEN), :].astype(jnp.bfloat16)
                )

    def wait_queries(chunk, state):
        query_copy(chunk).wait_recv()
        pair_arrival(chunk, cross).wait_recv()
        return state

    lax.fori_loop(0, chunks, wait_queries, 0)

    per_chunk = places * group
    pair_lane = lax.broadcasted_iota(jnp.int32, (2 * rows, pair), 1) // HEAD_DIM
    queries = s.queries[...]
    masked = [jnp.where(pair_lane == head, queries, jnp.zeros_like(queries)) for head in range(pair // HEAD_DIM)]

    def absorb(block, mask, first):
        keys, values = block[:, :pair], block[:, pair:]
        values_t = values.astype(jnp.float32).T.astype(jnp.bfloat16)
        for head in range(pair // HEAD_DIM):
            scores = dot_nt(keys, masked[head])
            pieces = [mask(begin, scores[begin : begin + group, :]) for begin in range(0, scores.shape[0], group)]
            peak = pieces[0]
            for piece in pieces[1:]:
                peak = jnp.maximum(peak, piece)
            fresh = jnp.max(peak, axis=0, keepdims=True)
            if not first:
                fresh = jnp.maximum(s.top[head], fresh)
            weights = [jnp.exp2((piece - fresh) * EXP2_SCALE) for piece in pieces]
            total = weights[0]
            for piece in weights[1:]:
                total = total + piece
            total = jnp.sum(total, axis=0, keepdims=True)
            of = slice(head * HEAD_DIM, (head + 1) * HEAD_DIM)
            rounded = jnp.concatenate([piece.astype(jnp.bfloat16) for piece in weights], axis=0)
            share = dot(values_t[of, :], rounded)
            if not first:
                factor = jnp.exp2((s.top[head] - fresh) * EXP2_SCALE)
                total = total + s.norm[head] * factor
                share = share + s.acc[of, :] * factor
            s.top[head] = fresh
            s.norm[head] = total
            s.acc[of, :] = share

    ahead_of = lax.broadcasted_iota(jnp.int32, (group, 2 * rows), 1) - lax.broadcasted_iota(
        jnp.int32, (group, 2 * rows), 0
    )

    def own_mask(begin, piece):
        index = begin // group
        return jnp.where(ahead_of >= (index % 2) * rows + (index // 2) * group, piece, masked_low)

    own_level = jnp.concatenate(
        [s.pairs[aligned((chunk * places + 2 * level) * group, 2 * group, 2 * group), :] for chunk in range(chunks)], axis=0
    )
    absorb(own_level, own_mask, True)

    def key_step(step, state):
        if per_chunk <= STEP_KEYS:
            for inner in range(STEP_KEYS // per_chunk):
                wait_chunk(step * (STEP_KEYS // per_chunk) + inner)
        else:
            ratio = per_chunk // STEP_KEYS

            @pl.when(step % ratio == 0)
            def _():
                wait_chunk(step // ratio)

        def level_mask(begin, piece):
            source = (step * STEP_KEYS + begin) % per_chunk // group
            return piece + jnp.where(source < 2 * level, 0.0, masked_low)

        absorb(s.pairs[aligned(step * STEP_KEYS, STEP_KEYS, STEP_KEYS), :], level_mask, False)
        return state

    lax.fori_loop(0, places * rows // STEP_KEYS, key_step, 0)

    size = rows // PIECES
    at = [pl.ds(piece * size, size) for piece in range(PIECES)]

    def turn_copy(piece):
        return remote(
            s.turn.at[at[piece], :], s.heads_in.at[at[piece], aligned(side * pair, pair, pair)],
            s.turn_send.at[piece], s.turn_recv.at[piece], {"seq": cross},
        )

    def mixed_of(at):
        shares = [
            s.acc[head * HEAD_DIM : (head + 1) * HEAD_DIM, at] / s.norm[head, :, at] for head in range(pair // HEAD_DIM)
        ]
        return jnp.concatenate(shares, axis=0).T.astype(jnp.bfloat16)

    s.turn[...] = mixed_of(aligned((1 - side) * rows, rows, rows))
    for piece in range(PIECES):
        turn_copy(piece).start()
    s.heads_in[:, aligned(side * pair, pair, pair)] = mixed_of(aligned(side * rows, rows, rows))

    for steps in (1, 2):
        @pl.when(place + steps < places)
        def _():
            id_copy(steps).wait_send()

    for copy in column_copies:
        copy.wait_send()
    for copy in carry_copies:
        copy.wait_send()

    def drain(chunk, state):
        for copy in mix_copies(chunk, mixed_rows(chunk)):
            copy.wait_send()
        short_sum.drain(chunk, short_rows(chunk))
        for_targets(lambda target: pair_copy(chunk, target).wait_send())
        query_copy(chunk).wait_send()
        return state

    lax.fori_loop(0, chunks, drain, 0)
    loads["co"].wait()

    out_sum = HeadSum(1, peers, s.part, s.summed, buffers, s.sum_send, s.sum_recv)
    ffn_sum = HeadSum(2, peers, s.part_b, s.second, buffers, s.sum_send, s.sum_recv)

    for piece in range(PIECES):
        turn_copy(piece).wait_recv()
        s.part[at[piece], :] = dot(s.heads_in[at[piece], :], s.co[...])
        out_sum.begin(piece, at[piece])
    for name in ("ffn_gain", "up", "down"):
        loads[name].wait()
    for piece in range(PIECES):
        out_sum.middle(piece, at[piece])

    def feed(piece):
        out_sum.end(piece, at[piece])
        value = s.short[at[piece], :].astype(jnp.float32) + s.summed[at[piece], :].astype(jnp.float32)
        s.first[at[piece], :] = value
        inner = jax.nn.gelu(dot(normed(value, s.ffn_gain[...]), s.up[...])).astype(jnp.bfloat16)
        s.part_b[at[piece], :] = dot(inner, s.down[...])
        ffn_sum.begin(piece, at[piece])

    def raise_rows(piece):
        ffn_sum.end(piece, at[piece])
        for member in range(SHORTEN):
            lifted = dot(s.second[at[piece], :], s.lift[:, member * width : (member + 1) * width])
            for block in range(lanes):
                s.spread[block, pl.ds(SHORTEN * size * piece + member, size, stride=SHORTEN), :] = lifted[
                    :, block * 128 : block * 128 + 128
                ]
        for block in range(lanes):
            to = slice(SHORTEN * size * piece, SHORTEN * size * (piece + 1))
            base_at = slice(CARRY + SHORTEN * size * piece, CARRY + SHORTEN * size * (piece + 1))
            out_ref[to, block * 128 : block * 128 + 128] = (
                s.stream[block, base_at, :] + s.spread[block, to, :]
            ).astype(jnp.bfloat16)

    for step in range(PIECES + 4):
        if step < PIECES:
            out_sum.total(step, at[step])
        if 0 <= step - 1 < PIECES:
            feed(step - 1)
        if 0 <= step - 2 < PIECES:
            ffn_sum.middle(step - 2, at[step - 2])
        if 0 <= step - 3 < PIECES:
            ffn_sum.total(step - 3, at[step - 3], s.first)
        if 0 <= step - 4 < PIECES:
            raise_rows(step - 4)

    for piece in range(PIECES):
        turn_copy(piece).wait_send()
    for piece in range(PIECES):
        out_sum.drain(piece, at[piece])
        ffn_sum.drain(piece, at[piece])


def local(
    token_ids,
    embedding,
    fine_norm,
    fine_query,
    fine_key,
    fine_value,
    fine_output,
    shorten_weight,
    coarse_norm,
    coarse_query,
    coarse_key,
    coarse_value,
    coarse_output,
    ffn_norm,
    ffn_up,
    ffn_down,
    upsample_weight,
):
    count = token_ids.shape[0]
    width = fine_query.shape[1]
    chunk_rows = min(128, count)
    chunks = count // chunk_rows
    scratch = scratch_list(count, width, chunks, lax.axis_size("seq"))
    names = [name for name, _ in scratch]

    def kernel(*refs):
        block_kernel(names, chunk_rows, *refs)

    return pl.pallas_call(
        kernel,
        out_shape=jax.ShapeDtypeStruct((count, width), jnp.bfloat16),
        in_specs=[HBM_SPEC] * 17,
        out_specs=VMEM_SPEC,
        scratch_shapes=[shape for _, shape in scratch],
        compiler_params=pltpu.CompilerParams(
            collective_id=1, has_side_effects=True, vmem_limit_bytes=46 * 2**20
        ),
        name="block_kernel",
    )(
        *(
            pltpu.with_memory_space_constraint(array, pltpu.HBM)
            for array in (
                token_ids.reshape(1, count), fine_norm.reshape(1, D), coarse_norm.reshape(1, D), ffn_norm.reshape(1, D),
                embedding, fine_query, fine_key, fine_value, fine_output, shorten_weight, coarse_query, coarse_key,
                coarse_value, coarse_output, ffn_up, ffn_down, upsample_weight,
            )
        ),
    )


def solution(mesh):
    return jax.shard_map(
        local,
        mesh=mesh,
        in_specs=(
            P("seq"),
            P(),
            P(),
            P(None, "head"),
            P(None, "head"),
            P(None, "head"),
            P("head", None),
            P(None, "head", None),
            P(),
            P(None, "head"),
            P(None, "head"),
            P(None, "head"),
            P("head", None),
            P(),
            P(None, "head"),
            P("head", None),
            P(None, None, "head"),
        ),
        out_specs=P("seq", "head"),
        check_vma=False,
    )
```

```python
import math

import jax
import jax.numpy as jnp
from jax import lax
from jax.experimental import pallas as pl
from jax.experimental.pallas import tpu as pltpu
from jax.sharding import PartitionSpec as P

D = 1024
HEAD_DIM = 64
HALF = HEAD_DIM // 2
SHORTEN = 4
WINDOW = 1024
LEAD = 128
CARRY = 16

epsilon = 1e-06
masked_low = -1e30
MESH = pl.DeviceIdType.MESH
EXP2_SCALE = HEAD_DIM ** (-0.5) * math.log2(math.e)
VMEM_SPEC = pl.BlockSpec(memory_space=pltpu.VMEM)
HBM_SPEC = pl.BlockSpec(memory_space=pltpu.HBM)

RELAY, FINISH, MIDDLE, TOTAL, PROJECT = (2, 2, 3, 5, 5)
STEP_KEYS = 256
PIECES = 4
SET = 2


def dot(left, right):
    return jnp.dot(left, right, preferred_element_type=jnp.float32)


def dot_nt(left, right):
    return lax.dot_general(left, right, (((1,), (1,)), ((), ())), preferred_element_type=jnp.float32)


def dot_tn(left, right):
    return lax.dot_general(left, right, (((0,), (0,)), ((), ())), preferred_element_type=jnp.float32)


def normed(data, gain):
    power = jnp.mean(data * data, axis=1, keepdims=True)
    return (data * lax.rsqrt(power + epsilon) * gain).astype(jnp.bfloat16)


def aligned(start, size, unit):
    return pl.ds(pl.multiple_of(start, unit), size)


def periods(column):
    log = 4 + lax.shift_right_logical(column * 14, 5)
    return jnp.left_shift(jnp.ones_like(log), log)


def phase(position, period):
    cycle = jnp.bitwise_and(position, period - 1).astype(jnp.float32)
    return cycle * (2.0 * math.pi / period.astype(jnp.float32))


def remote(source, target, send, receive, device):
    return pltpu.make_async_remote_copy(
        src_ref=source, dst_ref=target, send_sem=send, recv_sem=receive, device_id=device, device_id_type=MESH
    )


class HeadSum:
    def __init__(self, index, peers, part, out, buffers, send_sem, recv_sem):
        self.index = index
        self.me, self.sibling, self.across = peers
        self.part, self.out = part, out
        self.send_a, self.recv_a, self.send_b, self.recv_b, self.final = (buffer.at[index] for buffer in buffers)
        self.send_sem, self.recv_sem = send_sem, recv_sem
        half = part.shape[1] // 2
        self.mine = aligned((self.me % 2) * half, half, half)
        self.theirs = aligned((self.sibling % 2) * half, half, half)

    def copy(self, kind, piece, source, target, device):
        return remote(
            source, target, self.send_sem.at[self.index, kind, piece], self.recv_sem.at[self.index, kind, piece],
            {"head": device},
        )

    def copy_a(self, piece, at):
        return self.copy(0, piece, self.send_a.at[at, :], self.recv_a.at[at, :], self.sibling)

    def copy_b(self, piece, at):
        return self.copy(1, piece, self.send_b.at[at, :], self.recv_b.at[at, :], self.across)

    def copy_c(self, piece, at):
        return self.copy(2, piece, self.final.at[at, :], self.out.at[at, self.mine], self.sibling)

    def begin(self, piece, at):
        self.send_a[at, :] = self.part[at, self.theirs].astype(jnp.bfloat16)
        self.copy_a(piece, at).start()

    def middle(self, piece, at):
        self.copy_a(piece, at).wait_recv()
        summed = self.part[at, self.mine] + self.recv_a[at, :].astype(jnp.float32)
        self.part[at, self.mine] = summed
        self.send_b[at, :] = summed.astype(jnp.bfloat16)
        self.copy_b(piece, at).start()

    def total(self, piece, at, residual=None):
        self.copy_b(piece, at).wait_recv()
        value = self.part[at, self.mine] + self.recv_b[at, :].astype(jnp.float32)
        if residual is not None:
            value = value + residual[at, self.mine]
        value = value.astype(jnp.bfloat16)
        self.final[at, :] = value
        self.copy_c(piece, at).start()
        self.out[at, self.mine] = value

    def end(self, piece, at):
        self.copy_c(piece, at).wait_recv()

    def drain(self, piece, at):
        self.copy_a(piece, at).wait_send()
        self.copy_b(piece, at).wait_send()
        self.copy_c(piece, at).wait_send()


def scratch_list(count, width, chunks, places):
    full = 4 * width
    rows = count // SHORTEN
    frame = LEAD + WINDOW + count
    low = jnp.bfloat16
    wide = jnp.float32
    dma = pltpu.SemaphoreType.DMA
    return [
        ("emb", pltpu.VMEM((256, full), low)),
        ("fq", pltpu.VMEM((full, width), low)),
        ("fk", pltpu.VMEM((full, width), low)),
        ("fv", pltpu.VMEM((full, width), low)),
        ("cols", pltpu.VMEM((full, width), low)),
        ("ws", pltpu.VMEM((SHORTEN, width, full), low)),
        ("cq", pltpu.VMEM((full, width), low)),
        ("ck", pltpu.VMEM((full, width), low)),
        ("cv", pltpu.VMEM((full, width), low)),
        ("co", pltpu.VMEM((width, full), low)),
        ("up", pltpu.VMEM((full, full), low)),
        ("down", pltpu.VMEM((full, full), low)),
        ("lift", pltpu.VMEM((full, SHORTEN * width), low)),
        ("raw", pltpu.VMEM((width // 128, full, SHORTEN, 128), low)),
        ("fine_gain", pltpu.VMEM((1, full), wide)),
        ("coarse_gain", pltpu.VMEM((1, full), wide)),
        ("ffn_gain", pltpu.VMEM((1, full), wide)),
        ("load_sem", dma((17 + width // 128,))),
        ("ids", pltpu.VMEM((1, frame), jnp.int32)),
        ("id_send", dma((2,))),
        ("id_recv", dma((2,))),
        ("col_send", dma((4,))),
        ("col_recv", dma((4,))),
        ("tabs", pltpu.VMEM((6, 256, width), low)),
        ("cos_t", pltpu.VMEM((HALF, frame), wide)),
        ("sin_t", pltpu.VMEM((HALF, frame), wide)),
        ("keys", pltpu.VMEM((frame, width), low)),
        ("values", pltpu.VMEM((width, frame), low)),
        ("query", pltpu.VMEM((width, LEAD + count), low)),
        ("start", pltpu.VMEM((LEAD + count, width), low)),
        ("scores", pltpu.VMEM((WINDOW + count // chunks, 4 * (count // chunks)), wide)),
        ("weights", pltpu.VMEM((WINDOW + count // chunks, 4 * (count // chunks)), low)),
        ("mixed", pltpu.VMEM((CARRY + count, width), low)),
        ("others", pltpu.VMEM((CARRY + count, 3 * width), low)),
        ("mix_send", dma((3, chunks + 1))),
        ("mix_recv", dma((3, chunks + 1))),
        ("stream", pltpu.VMEM((width // 128, CARRY + count, 128), wide)),
        ("part", pltpu.VMEM((rows, full), wide)),
        ("part_b", pltpu.VMEM((rows, full), wide)),
        ("short", pltpu.VMEM((rows, full), low)),
        ("summed", pltpu.VMEM((rows, full), low)),
        ("first", pltpu.VMEM((rows, full), wide)),
        ("second", pltpu.VMEM((rows, full), low)),
        ("send_a", pltpu.VMEM((3, rows, full // 2), low)),
        ("recv_a", pltpu.VMEM((3, rows, full // 2), low)),
        ("send_b", pltpu.VMEM((3, rows, full // 2), low)),
        ("recv_b", pltpu.VMEM((3, rows, full // 2), low)),
        ("final", pltpu.VMEM((3, rows, full // 2), low)),
        ("sum_send", dma((3, 3, chunks))),
        ("sum_recv", dma((3, 3, chunks))),
        ("coarse_cos", pltpu.VMEM((rows, width), wide)),
        ("coarse_sin", pltpu.VMEM((rows, width), wide)),
        ("pair_out", pltpu.VMEM((2, rows, width), low)),
        ("query_out", pltpu.VMEM((2, rows, width // 2), low)),
        ("pairs", pltpu.VMEM((places * rows, width), low)),
        ("queries", pltpu.VMEM((2 * rows, width // 2), low)),
        ("pair_send", dma((places, chunks))),
        ("pair_recv", dma((places, chunks))),
        ("query_send", dma((chunks,))),
        ("query_recv", dma((chunks,))),
        ("top", pltpu.VMEM((2, 1, 2 * rows), wide)),
        ("norm", pltpu.VMEM((2, 1, 2 * rows), wide)),
        ("acc", pltpu.VMEM((width // 2, 2 * rows), wide)),
        ("turn", pltpu.VMEM((rows, width // 2), low)),
        ("heads_in", pltpu.VMEM((rows, width), low)),
        ("turn_send", dma((PIECES,))),
        ("turn_recv", dma((PIECES,))),
        ("spread", pltpu.VMEM((width // 128, count, 128), wide)),
    ]


class Names:
    pass


def block_kernel(names, chunk_rows, *refs):
    (ids_h, fine_gain_h, coarse_gain_h, ffn_gain_h, emb_h, fq_h, fk_h, fv_h, fo_h, ws_h,
     cq_h, ck_h, cv_h, co_h, up_h, down_h, lift_h, out_ref) = refs[:18]
    s = Names()
    for name, ref in zip(names, refs[18:]):
        setattr(s, name, ref)
    count, width = out_ref.shape
    full = 4 * width
    heads = width // HEAD_DIM
    chunks = count // chunk_rows
    group = chunk_rows // SHORTEN
    rows = count // SHORTEN
    frame = LEAD + WINDOW + count
    span = WINDOW + chunk_rows
    lanes = width // 128
    pair = width // 2

    places = lax.axis_size("seq")
    place = lax.axis_index("seq")
    levels = places // 2
    side = place % 2
    level = place // 2
    cross = place + 1 - 2 * side
    me = lax.axis_index("head")
    sibling = me + 1 - 2 * (me % 2)
    across = (me + 2) % 4
    diagonal = (sibling + 2) % 4

    barrier = pltpu.get_barrier_semaphore()
    for device in (sibling, across, diagonal):
        pl.semaphore_signal(barrier, inc=1, device_id={"head": device}, device_id_type=MESH)

    def greet(step, state):
        pl.semaphore_signal(
            barrier, inc=1, device_id={"seq": (place + step) % places}, device_id_type=MESH
        )
        return state

    lax.fori_loop(1, places, greet, 0)

    own_columns = aligned(me * width, width, width)
    own_ids = s.ids.at[:, pl.ds(LEAD + WINDOW, count)]
    loads = {
        name: pltpu.make_async_copy(source, target, s.load_sem.at[index])
        for index, (name, source, target) in enumerate((
            ("ids", ids_h, own_ids), ("emb", emb_h, s.emb), ("fine_gain", fine_gain_h, s.fine_gain),
            ("fk", fk_h, s.fk), ("fv", fv_h, s.fv), ("fq", fq_h, s.fq),
            ("coarse_gain", coarse_gain_h, s.coarse_gain), ("ffn_gain", ffn_gain_h, s.ffn_gain),
            ("cols", fo_h.at[:, own_columns], s.cols.at[pl.ds(0, width), :]),
            ("ws", ws_h, s.ws), ("cq", cq_h, s.cq), ("ck", ck_h, s.ck), ("cv", cv_h, s.cv), ("co", co_h, s.co),
            ("up", up_h, s.up), ("down", down_h, s.down),
            *((f"lift{b}", lift_h.at[:, :, pl.ds(b * 128, 128)], s.raw.at[b]) for b in range(lanes)),
        ))
    }
    lift_names = tuple(f"lift{block}" for block in range(lanes))

    def start_loads(*names):
        for name in names:
            loads[name].start()

    start_loads("ids", "emb", "fine_gain", "fk", "fv", "fq")

    @pl.when(place < 1)
    def _():
        s.ids[:, LEAD : LEAD + WINDOW] = jnp.zeros((1, WINDOW), jnp.int32)

    @pl.when(place < 2)
    def _():
        s.ids[:, :LEAD] = jnp.zeros((1, LEAD), jnp.int32)

    def clear(index, state):
        chunk = index // (places - 2)
        blank = index % (places - 2)

        @pl.when(blank + 2 >= 2 * level + 2)
        def _():
            at = aligned((chunk * places + blank + 2) * group, group, group)
            s.pairs[at, :] = jnp.zeros((group, width), jnp.bfloat16)

        return state

    lax.fori_loop(0, chunks * (places - 2), clear, 0)

    column = lax.broadcasted_iota(jnp.int32, (HALF, 128), 0)
    lane = lax.broadcasted_iota(jnp.int32, (HALF, 128), 1)
    period = periods(column)
    small = phase(lane, period)
    base = (place - 1) * count - LEAD
    large = phase(base + 128 * lane, period)
    cos_b, sin_b, cos_a, sin_a = jnp.cos(small), jnp.sin(small), jnp.cos(large), jnp.sin(large)
    for block in range(frame // 128):
        at = slice(block * 128, block * 128 + 128)
        cos_k, sin_k = cos_a[:, block : block + 1], sin_a[:, block : block + 1]
        s.cos_t[:, at] = cos_b * cos_k - sin_b * sin_k
        s.sin_t[:, at] = sin_b * cos_k + cos_b * sin_k

    lane_f = lax.broadcasted_iota(jnp.int32, (rows, 128), 1) % HEAD_DIM
    period_f = periods(lane_f % HALF)
    angle_f = phase(place * rows + lax.broadcasted_iota(jnp.int32, (rows, 128), 0), period_f)
    cos_f = jnp.cos(angle_f)
    sin_f = jnp.where(lane_f < HALF, -jnp.sin(angle_f), jnp.sin(angle_f))
    for block in range(lanes):
        s.coarse_cos[:, block * 128 : block * 128 + 128] = cos_f
        s.coarse_sin[:, block * 128 : block * 128 + 128] = sin_f

    pl.semaphore_wait(barrier, places + 2)

    def id_copy(steps):
        if steps == 1:
            target = s.ids.at[:, pl.ds(LEAD, WINDOW)]
            source = ids_h
        else:
            target = s.ids.at[:, pl.ds(0, LEAD)]
            source = ids_h.at[:, pl.ds(count - LEAD, LEAD)]
        device = (place + steps) % places
        return remote(source, target, s.id_send.at[steps - 1], s.id_recv.at[steps - 1], {"seq": device})

    for steps in (1, 2):
        @pl.when(place + steps < places)
        def _():
            id_copy(steps).start()

    def column_copy(flip, device):
        return remote(
            fo_h.at[:, aligned(device * width, width, width)], s.cols.at[pl.ds(flip * width, width), :],
            s.col_send.at[flip], s.col_recv.at[flip], {"head": device},
        )

    column_copies = [column_copy(flip, device) for flip, device in ((1, sibling), (2, across), (3, diagonal))]
    for copy in column_copies:
        copy.start()

    loads["emb"].wait()
    loads["fine_gain"].wait()
    level_in = normed(s.emb[...].astype(jnp.float32), s.fine_gain[...])

    def split(values):
        high = values.astype(jnp.bfloat16)
        return high, (values - high.astype(jnp.float32)).astype(jnp.bfloat16)

    loads["fk"].wait()
    s.tabs[0], s.tabs[1] = split(dot(level_in, s.fk[...]).T)
    loads["fv"].wait()
    s.tabs[2] = dot(level_in, s.fv[...]).T.astype(jnp.bfloat16)
    loads["fq"].wait()
    s.tabs[3], s.tabs[4] = split(dot(level_in, s.fq[...]).T)
    s.tabs[5] = s.emb[:, own_columns]
    loads["ids"].wait()
    start_loads("cols", "ws", "coarse_gain", "ffn_gain", "cq", "ck", "cv")

    def turned(joined, at):
        cosine, sine = s.cos_t[:, at], s.sin_t[:, at]
        pieces = []
        for head in range(heads):
            low = joined[head * HEAD_DIM : head * HEAD_DIM + HALF]
            high = joined[head * HEAD_DIM + HALF : (head + 1) * HEAD_DIM]
            pieces += [low * cosine - high * sine, high * cosine + low * sine]
        return jnp.concatenate(pieces, axis=0)

    def hot_rows(at, size):
        levels_at = lax.broadcasted_iota(jnp.int32, (256, size), 0)
        return jnp.where(levels_at == s.ids[:, at], 1.0, 0.0).astype(jnp.bfloat16)

    def key_rows(begin, size):
        at = aligned(begin, size, 128)
        hot = hot_rows(at, size)
        s.keys[at, :] = turned(dot(s.tabs[0], hot) + dot(s.tabs[1], hot), at).T.astype(jnp.bfloat16)
        s.values[:, at] = dot(s.tabs[2], hot).astype(jnp.bfloat16)

    def query_rows(begin, size):
        at = aligned(begin, size, 128)
        to = aligned(begin - WINDOW, size, 128)
        hot = hot_rows(at, size)
        s.query[:, to] = turned(dot(s.tabs[3], hot) + dot(s.tabs[4], hot), at).astype(jnp.bfloat16)
        s.start[to, :] = dot_tn(hot, s.tabs[5]).astype(jnp.bfloat16)

    own_block = min(512, count)

    def own_rows(index, state):
        key_rows(LEAD + WINDOW + index * own_block, own_block)
        query_rows(LEAD + WINDOW + index * own_block, own_block)
        return state

    def prior_rows(index, state):
        key_rows(index * 384, 384)
        return state

    lax.fori_loop(0, count // own_block, own_rows, 0)
    for steps in (1, 2):
        @pl.when(place >= steps)
        def _():
            id_copy(steps).wait_recv()

    lax.fori_loop(0, (LEAD + WINDOW) // 384, prior_rows, 0)
    query_rows(WINDOW, LEAD)

    def weigh(scores):
        top = scores[0]
        for piece in scores[1:]:
            top = jnp.maximum(top, piece)
        top = jnp.max(top, axis=0, keepdims=True)
        weights = [jnp.exp2((piece - top) * EXP2_SCALE) for piece in scores]
        total = weights[0]
        for piece in weights[1:]:
            total = total + piece
        total = jnp.sum(total, axis=0, keepdims=True)
        return jnp.concatenate([piece.astype(jnp.bfloat16) for piece in weights], axis=0), total

    def mixed_rows(chunk):
        return aligned(CARRY + chunk * chunk_rows, chunk_rows, CARRY)

    def mix_copies(chunk, at):
        def slot(which):
            return s.others.at[at, pl.ds((which - 1) * width, width)]

        def copy(kind, source, target, device):
            return remote(source, target, s.mix_send.at[kind, chunk], s.mix_recv.at[kind, chunk], {"head": device})

        return (
            copy(0, s.mixed.at[at, :], slot(2), across),
            copy(1, s.mixed.at[at, :], slot(1), sibling),
            copy(2, slot(2), slot(3), sibling),
        )

    carry_at = pl.ds(0, CARRY)
    carry_copies = mix_copies(chunks, carry_at)

    start_loads("co", "up", "down", *lift_names)

    def attend_carry():
        lane_slot = lax.broadcasted_iota(jnp.int32, (HEAD_DIM, LEAD), 1) // 32
        packed = []
        for head in range(heads):
            rolled = pltpu.roll(s.query[head * HEAD_DIM : (head + 1) * HEAD_DIM, :LEAD].astype(jnp.float32), (32 * head + 32) % LEAD, 1)
            packed.append(jnp.where(lane_slot == head, rolled, 0.0))
        packed = jnp.concatenate(packed, axis=0).astype(jnp.bfloat16)
        scores = dot(s.keys[: LEAD + WINDOW, :], packed)
        key = lax.broadcasted_iota(jnp.int32, scores.shape, 0)
        last = lax.broadcasted_iota(jnp.int32, scores.shape, 1) % 32 + (LEAD + WINDOW - 32)
        floor = jnp.where(place < 2, LEAD, 0)
        allowed = (key > last - WINDOW) & (key <= last) & (key >= floor)
        weights, total = weigh([jnp.where(allowed, scores, masked_low)])
        out = dot(s.values[:, : LEAD + WINDOW], weights) / total
        unpacked = [
            pltpu.roll(out[head * HEAD_DIM : (head + 1) * HEAD_DIM, :], (LEAD - 32 * head) % LEAD, 1) for head in range(heads)
        ]
        s.mixed[carry_at, :] = jnp.concatenate(unpacked, axis=0).T[32 - CARRY : 32, :].astype(jnp.bfloat16)
        carry_copies[0].start()
        carry_copies[1].start()

    part_keys = 3 * chunk_rows if span % (3 * chunk_rows) == 0 else chunk_rows
    row = lax.broadcasted_iota(jnp.int32, (chunk_rows, chunk_rows), 0)
    column = lax.broadcasted_iota(jnp.int32, (chunk_rows, chunk_rows), 1)

    def each_head(allowed, piece):
        return jnp.concatenate(
            [
                jnp.where(allowed, piece[:, head * chunk_rows : (head + 1) * chunk_rows], masked_low)
                for head in range(piece.shape[1] // chunk_rows)
            ],
            axis=1,
        )

    sets = [tuple(range(first, min(first + SET, heads))) for first in range(0, heads, SET)]

    def by_eights(values):
        return values.reshape(values.shape[0] // 8, 8, values.shape[1])

    row_head = lax.broadcasted_iota(jnp.int32, (width, chunk_rows), 0) // HEAD_DIM

    def attend_chunk(chunk):
        begin = chunk * chunk_rows
        floor = jnp.where(place == 0, WINDOW - begin, 0)
        key_at = aligned(LEAD + begin, span, 128)
        query = s.query[:, aligned(LEAD + begin, chunk_rows, chunk_rows)]
        tops, totals = [], []
        for side_heads in sets:
            lanes_of = slice(side_heads[0] * chunk_rows, (side_heads[-1] + 1) * chunk_rows)
            stacked = jnp.concatenate(
                [jnp.where(row_head == head, query, jnp.zeros_like(query)) for head in side_heads], axis=1
            )
            top = None
            for part in range(0, span, part_keys):
                scores = dot(s.keys[aligned(LEAD + begin + part, part_keys, 128), :], stacked)
                for at in range(part, part + part_keys, chunk_rows):
                    piece = scores[at - part : at - part + chunk_rows, :]
                    if at == span - chunk_rows:
                        piece = each_head(row <= column, piece)
                    else:
                        piece = piece + jnp.where(at < floor, masked_low, 0.0)
                        if at == 0:
                            piece = each_head(row > column, piece)
                    s.scores[at : at + chunk_rows, lanes_of] = piece
                    peak = jnp.max(by_eights(piece), axis=0)
                    top = peak if top is None else jnp.maximum(top, peak)
            tops.append(jnp.max(top, axis=0, keepdims=True))
        outs = []
        for which, side_heads in enumerate(sets):
            lanes_of = slice(side_heads[0] * chunk_rows, (side_heads[-1] + 1) * chunk_rows)
            total = jnp.zeros((8, len(side_heads) * chunk_rows), jnp.float32)
            for at in range(0, span, chunk_rows):
                weights = jnp.exp2((s.scores[at : at + chunk_rows, lanes_of] - tops[which]) * EXP2_SCALE)
                total = total + jnp.sum(by_eights(weights), axis=0)
                s.weights[at : at + chunk_rows, lanes_of] = weights.astype(jnp.bfloat16)
            total = jnp.sum(total, axis=0, keepdims=True)
            for index, head in enumerate(side_heads):
                of = slice(head * chunk_rows, (head + 1) * chunk_rows)
                share = dot(s.values[head * HEAD_DIM : (head + 1) * HEAD_DIM, key_at], s.weights[:, of])
                outs.append(share / total[:, index * chunk_rows : (index + 1) * chunk_rows])
        at = mixed_rows(chunk)
        s.mixed[at, :] = jnp.concatenate(outs, axis=0).T.astype(jnp.bfloat16)
        copies = mix_copies(chunk, at)
        copies[0].start()
        copies[1].start()

    def fine_rows(at, start_at):
        merged = dot(s.mixed[at, :], s.cols[:width, :]) + dot(s.others[at, :], s.cols[width:, :])
        value = (s.start[start_at, :].astype(jnp.float32) + merged).astype(jnp.bfloat16).astype(jnp.float32)
        for block in range(lanes):
            s.stream[block, at, :] = value[:, block * 128 : block * 128 + 128]

    peers = (me, sibling, across)
    buffers = (s.send_a, s.recv_a, s.send_b, s.recv_b, s.final)
    short_sum = HeadSum(0, peers, s.part, s.short, buffers, s.sum_send, s.sum_recv)

    def short_rows(chunk):
        return aligned(chunk * group, group, group)

    def relay_chunk(chunk):
        @pl.when(chunk == 0)
        def _():
            carry_copies[0].wait_recv()
            carry_copies[2].start()

        copies = mix_copies(chunk, mixed_rows(chunk))
        copies[0].wait_recv()
        copies[2].start()

    def finish_chunk(chunk):
        @pl.when(chunk == 0)
        def _():
            for copy in column_copies:
                copy.wait_recv()
            loads["cols"].wait()
            loads["ws"].wait()
            carry_copies[1].wait_recv()
            carry_copies[2].wait_recv()
            fine_rows(carry_at, pl.ds(LEAD - CARRY, CARRY))

            @pl.when(place == 0)
            def _():
                s.stream[:, 0:CARRY, :] = jnp.zeros((lanes, CARRY, 128), jnp.float32)

        at = mixed_rows(chunk)
        copies = mix_copies(chunk, at)
        copies[1].wait_recv()
        copies[2].wait_recv()
        fine_rows(at, aligned(LEAD + chunk * chunk_rows, chunk_rows, chunk_rows))
        total = jnp.zeros((group, full), jnp.float32)
        for offset in range(SHORTEN):
            begin = CARRY - (SHORTEN - 1) + offset + chunk * chunk_rows
            member = jnp.concatenate(
                [s.stream[block, pl.ds(begin, group, stride=SHORTEN), :] for block in range(lanes)], axis=1
            )
            total = total + dot(member.astype(jnp.bfloat16), s.ws[offset])
        s.part[short_rows(chunk), :] = total
        short_sum.begin(chunk, short_rows(chunk))

    def pair_rows(chunk, source):
        return aligned((chunk * places + source) * group, group, group)

    def pair_copy(chunk, target):
        at = pair_rows(chunk, place)
        return remote(
            s.pair_out.at[target % 2, short_rows(chunk), :], s.pairs.at[at, :],
            s.pair_send.at[target, chunk], s.pair_recv.at[place, chunk], {"seq": target},
        )

    def pair_arrival(chunk, source):
        at = pair_rows(chunk, source)
        return remote(
            s.pairs.at[at, :], s.pairs.at[at, :], s.pair_send.at[source, chunk], s.pair_recv.at[source, chunk],
            {"seq": cross},
        )

    def query_copy(chunk):
        at = short_rows(chunk)
        return remote(
            s.query_out.at[1 - side, at, :], s.queries.at[aligned(side * rows + chunk * group, group, group), :],
            s.query_send.at[chunk], s.query_recv.at[chunk], {"seq": cross},
        )

    def for_targets(action):
        def one(index, state):
            target = places - 1 - index

            @pl.when(target != place)
            def _():
                action(target)

            return state

        lax.fori_loop(0, places - 2 * level, one, 0)

    def project_chunk(chunk):
        @pl.when(chunk == 0)
        def _():
            for name in ("coarse_gain", "cq", "ck", "cv"):
                loads[name].wait()

        at = short_rows(chunk)
        short_sum.end(chunk, at)
        coarse_in = normed(s.short[at, :].astype(jnp.float32), s.coarse_gain[...])
        cosine, sine = s.coarse_cos[at, :], s.coarse_sin[at, :]
        is_low = lax.broadcasted_iota(jnp.int32, (group, width), 1) % HEAD_DIM < HALF

        def rotated(values):
            other = jnp.where(is_low, pltpu.roll(values, width - HALF, 1), pltpu.roll(values, HALF, 1))
            return (values * cosine + other * sine).astype(jnp.bfloat16)

        key = rotated(dot(coarse_in, s.ck[...]))
        value = dot(coarse_in, s.cv[...]).astype(jnp.bfloat16)
        for half in range(2):
            s.pair_out[half, at, :pair] = key[:, half * pair : half * pair + pair]
            s.pair_out[half, at, pair:] = value[:, half * pair : half * pair + pair]
        for_targets(lambda target: pair_copy(chunk, target).start())
        query = rotated(dot(coarse_in, s.cq[...]))
        for half in range(2):
            s.query_out[half, at, :] = query[:, half * pair : half * pair + pair]
        query_copy(chunk).start()
        s.pairs[pair_rows(chunk, place), :] = s.pair_out[side, at, :]
        s.queries[aligned(side * rows + chunk * group, group, group), :] = s.query_out[side, at, :]

    def lay_out():
        for name in lift_names:
            loads[name].wait()
        part_rows = count // SHORTEN
        for block in range(lanes):
            for begin in range(0, full, part_rows):
                flat = s.raw.at[block, pl.ds(begin, part_rows)].reshape(part_rows * SHORTEN, 128)
                s.spread[block] = flat[...].astype(jnp.float32)
                for member in range(SHORTEN):
                    s.lift[begin : begin + part_rows, member * width + block * 128 : member * width + block * 128 + 128] = (
                        s.spread[block, pl.ds(member, part_rows, stride=SHORTEN), :].astype(jnp.bfloat16)
                    )

    def total_chunk(chunk):
        short_sum.total(chunk, short_rows(chunk))

    def middle_chunk(chunk):
        short_sum.middle(chunk, short_rows(chunk))

    ahead = ((RELAY, relay_chunk), (TOTAL, total_chunk))
    behind = ((PROJECT, project_chunk), (MIDDLE, middle_chunk), (FINISH, finish_chunk))

    def one_step(step, state):
        def run(stages):
            for lag, action in stages:
                @pl.when(step >= lag)
                def _():
                    action(step - lag)

        run(ahead)
        attend_chunk(step)

        @pl.when(step == 0)
        def _():
            attend_carry()

        run(behind)
        return state

    lax.fori_loop(0, chunks, one_step, 0)

    left = {action: max(0, chunks - lag) for lag, action in ahead + behind}

    def rest(action, upto):
        for chunk in range(left[action], upto):
            action(chunk)
        left[action] = max(left[action], upto)

    for action, back in (
        (relay_chunk, 1), (total_chunk, 4), (middle_chunk, 2), (project_chunk, 4), (finish_chunk, 1), (total_chunk, 3),
        (relay_chunk, 0), (middle_chunk, 1), (project_chunk, 3), (finish_chunk, 0), (total_chunk, 2),
        (middle_chunk, 0), (project_chunk, 2), (total_chunk, 1), (project_chunk, 1),
    ):
        rest(action, chunks - back)
    lay_out()
    rest(total_chunk, chunks)
    rest(project_chunk, chunks)

    def wait_chunk(chunk):
        def one(source, state):
            pair_arrival(chunk, source).wait_recv()
            return state

        lax.fori_loop(0, 2 * level, one, 0)

    def wait_queries(chunk, state):
        query_copy(chunk).wait_recv()
        pair_arrival(chunk, cross).wait_recv()
        return state

    lax.fori_loop(0, chunks, wait_queries, 0)

    per_chunk = places * group
    pair_lane = lax.broadcasted_iota(jnp.int32, (2 * rows, pair), 1) // HEAD_DIM
    queries = s.queries[...]
    masked = [jnp.where(pair_lane == head, queries, jnp.zeros_like(queries)) for head in range(pair // HEAD_DIM)]

    def absorb(block, mask, first):
        keys, values = block[:, :pair], block[:, pair:]
        values_t = values.astype(jnp.float32).T.astype(jnp.bfloat16)
        for head in range(pair // HEAD_DIM):
            scores = dot_nt(keys, masked[head])
            pieces = [mask(begin, scores[begin : begin + group, :]) for begin in range(0, scores.shape[0], group)]
            peak = pieces[0]
            for piece in pieces[1:]:
                peak = jnp.maximum(peak, piece)
            fresh = jnp.max(peak, axis=0, keepdims=True)
            if not first:
                fresh = jnp.maximum(s.top[head], fresh)
            weights = [jnp.exp2((piece - fresh) * EXP2_SCALE) for piece in pieces]
            total = weights[0]
            for piece in weights[1:]:
                total = total + piece
            total = jnp.sum(total, axis=0, keepdims=True)
            of = slice(head * HEAD_DIM, (head + 1) * HEAD_DIM)
            rounded = jnp.concatenate([piece.astype(jnp.bfloat16) for piece in weights], axis=0)
            share = dot(values_t[of, :], rounded)
            if not first:
                factor = jnp.exp2((s.top[head] - fresh) * EXP2_SCALE)
                total = total + s.norm[head] * factor
                share = share + s.acc[of, :] * factor
            s.top[head] = fresh
            s.norm[head] = total
            s.acc[of, :] = share

    ahead_of = lax.broadcasted_iota(jnp.int32, (group, 2 * rows), 1) - lax.broadcasted_iota(
        jnp.int32, (group, 2 * rows), 0
    )

    def own_mask(begin, piece):
        index = begin // group
        return jnp.where(ahead_of >= (index % 2) * rows + (index // 2) * group, piece, masked_low)

    own_level = jnp.concatenate(
        [s.pairs[aligned((chunk * places + 2 * level) * group, 2 * group, 2 * group), :] for chunk in range(chunks)], axis=0
    )
    absorb(own_level, own_mask, True)

    def key_step(step, state):
        if per_chunk <= STEP_KEYS:
            for inner in range(STEP_KEYS // per_chunk):
                wait_chunk(step * (STEP_KEYS // per_chunk) + inner)
        else:
            ratio = per_chunk // STEP_KEYS

            @pl.when(step % ratio == 0)
            def _():
                wait_chunk(step // ratio)

        def level_mask(begin, piece):
            source = (step * STEP_KEYS + begin) % per_chunk // group
            return piece + jnp.where(source < 2 * level, 0.0, masked_low)

        absorb(s.pairs[aligned(step * STEP_KEYS, STEP_KEYS, STEP_KEYS), :], level_mask, False)
        return state

    lax.fori_loop(0, places * rows // STEP_KEYS, key_step, 0)

    size = rows // PIECES
    at = [pl.ds(piece * size, size) for piece in range(PIECES)]

    def turn_copy(piece):
        return remote(
            s.turn.at[at[piece], :], s.heads_in.at[at[piece], aligned(side * pair, pair, pair)],
            s.turn_send.at[piece], s.turn_recv.at[piece], {"seq": cross},
        )

    def mixed_of(at):
        shares = [
            s.acc[head * HEAD_DIM : (head + 1) * HEAD_DIM, at] / s.norm[head, :, at] for head in range(pair // HEAD_DIM)
        ]
        return jnp.concatenate(shares, axis=0).T.astype(jnp.bfloat16)

    s.turn[...] = mixed_of(aligned((1 - side) * rows, rows, rows))
    for piece in range(PIECES):
        turn_copy(piece).start()
    s.heads_in[:, aligned(side * pair, pair, pair)] = mixed_of(aligned(side * rows, rows, rows))

    for steps in (1, 2):
        @pl.when(place + steps < places)
        def _():
            id_copy(steps).wait_send()

    for copy in column_copies:
        copy.wait_send()
    for copy in carry_copies:
        copy.wait_send()

    def drain(chunk, state):
        for copy in mix_copies(chunk, mixed_rows(chunk)):
            copy.wait_send()
        short_sum.drain(chunk, short_rows(chunk))
        for_targets(lambda target: pair_copy(chunk, target).wait_send())
        query_copy(chunk).wait_send()
        return state

    lax.fori_loop(0, chunks, drain, 0)
    loads["co"].wait()

    out_sum = HeadSum(1, peers, s.part, s.summed, buffers, s.sum_send, s.sum_recv)
    ffn_sum = HeadSum(2, peers, s.part_b, s.second, buffers, s.sum_send, s.sum_recv)

    for piece in range(PIECES):
        turn_copy(piece).wait_recv()
        s.part[at[piece], :] = dot(s.heads_in[at[piece], :], s.co[...])
        out_sum.begin(piece, at[piece])
    for name in ("ffn_gain", "up", "down"):
        loads[name].wait()
    for piece in range(PIECES):
        out_sum.middle(piece, at[piece])

    def feed(piece):
        out_sum.end(piece, at[piece])
        value = s.short[at[piece], :].astype(jnp.float32) + s.summed[at[piece], :].astype(jnp.float32)
        s.first[at[piece], :] = value
        inner = jax.nn.gelu(dot(normed(value, s.ffn_gain[...]), s.up[...])).astype(jnp.bfloat16)
        s.part_b[at[piece], :] = dot(inner, s.down[...])
        ffn_sum.begin(piece, at[piece])

    def raise_rows(piece):
        ffn_sum.end(piece, at[piece])
        for member in range(SHORTEN):
            lifted = dot(s.second[at[piece], :], s.lift[:, member * width : (member + 1) * width])
            for block in range(lanes):
                s.spread[block, pl.ds(SHORTEN * size * piece + member, size, stride=SHORTEN), :] = lifted[
                    :, block * 128 : block * 128 + 128
                ]
        for block in range(lanes):
            to = slice(SHORTEN * size * piece, SHORTEN * size * (piece + 1))
            base_at = slice(CARRY + SHORTEN * size * piece, CARRY + SHORTEN * size * (piece + 1))
            out_ref[to, block * 128 : block * 128 + 128] = (
                s.stream[block, base_at, :] + s.spread[block, to, :]
            ).astype(jnp.bfloat16)

    for step in range(PIECES + 4):
        if step < PIECES:
            out_sum.total(step, at[step])
        if 0 <= step - 1 < PIECES:
            feed(step - 1)
        if 0 <= step - 2 < PIECES:
            ffn_sum.middle(step - 2, at[step - 2])
        if 0 <= step - 3 < PIECES:
            ffn_sum.total(step - 3, at[step - 3], s.first)
        if 0 <= step - 4 < PIECES:
            raise_rows(step - 4)

    for piece in range(PIECES):
        turn_copy(piece).wait_send()
    for piece in range(PIECES):
        out_sum.drain(piece, at[piece])
        ffn_sum.drain(piece, at[piece])


def local(
    token_ids,
    embedding,
    fine_norm,
    fine_query,
    fine_key,
    fine_value,
    fine_output,
    shorten_weight,
    coarse_norm,
    coarse_query,
    coarse_key,
    coarse_value,
    coarse_output,
    ffn_norm,
    ffn_up,
    ffn_down,
    upsample_weight,
):
    count = token_ids.shape[0]
    width = fine_query.shape[1]
    chunk_rows = min(128, count)
    chunks = count // chunk_rows
    scratch = scratch_list(count, width, chunks, lax.axis_size("seq"))
    names = [name for name, _ in scratch]

    def kernel(*refs):
        block_kernel(names, chunk_rows, *refs)

    return pl.pallas_call(
        kernel,
        out_shape=jax.ShapeDtypeStruct((count, width), jnp.bfloat16),
        in_specs=[HBM_SPEC] * 17,
        out_specs=VMEM_SPEC,
        scratch_shapes=[shape for _, shape in scratch],
        compiler_params=pltpu.CompilerParams(
            collective_id=1, has_side_effects=True, vmem_limit_bytes=46 * 2**20
        ),
        name="block_kernel",
    )(
        *(
            pltpu.with_memory_space_constraint(array, pltpu.HBM)
            for array in (
                token_ids.reshape(1, count), fine_norm.reshape(1, D), coarse_norm.reshape(1, D), ffn_norm.reshape(1, D),
                embedding, fine_query, fine_key, fine_value, fine_output, shorten_weight, coarse_query, coarse_key,
                coarse_value, coarse_output, ffn_up, ffn_down, upsample_weight,
            )
        ),
    )


def solution(mesh):
    return jax.shard_map(
        local,
        mesh=mesh,
        in_specs=(
            P("seq"),
            P(),
            P(),
            P(None, "head"),
            P(None, "head"),
            P(None, "head"),
            P("head", None),
            P(None, "head", None),
            P(),
            P(None, "head"),
            P(None, "head"),
            P(None, "head"),
            P("head", None),
            P(),
            P(None, "head"),
            P("head", None),
            P(None, None, "head"),
        ),
        out_specs=P("seq", "head"),
        check_vma=False,
    )
```

```python
import math

import jax
import jax.numpy as jnp
from jax import lax
from jax.experimental import pallas as pl
from jax.experimental.pallas import tpu as pltpu
from jax.sharding import PartitionSpec as P

D = 1024
HEAD_DIM = 64
HALF = HEAD_DIM // 2
SHORTEN = 4
WINDOW = 1024
LEAD = 128
CARRY = 16

epsilon = 1e-06
masked_low = -1e30
MESH = pl.DeviceIdType.MESH
EXP2_SCALE = HEAD_DIM ** (-0.5) * math.log2(math.e)
VMEM_SPEC = pl.BlockSpec(memory_space=pltpu.VMEM)
HBM_SPEC = pl.BlockSpec(memory_space=pltpu.HBM)

RELAY, FINISH, MIDDLE, TOTAL, PROJECT = (2, 2, 3, 5, 5)
STEP_KEYS = 1024
PIECES = 4
SET = 2


def dot(left, right):
    return jnp.dot(left, right, preferred_element_type=jnp.float32)


def dot_nt(left, right):
    return lax.dot_general(left, right, (((1,), (1,)), ((), ())), preferred_element_type=jnp.float32)


def dot_tn(left, right):
    return lax.dot_general(left, right, (((0,), (0,)), ((), ())), preferred_element_type=jnp.float32)


def normed(data, gain):
    power = jnp.mean(data * data, axis=1, keepdims=True)
    return (data * lax.rsqrt(power + epsilon) * gain).astype(jnp.bfloat16)


def aligned(start, size, unit):
    return pl.ds(pl.multiple_of(start, unit), size)


def periods(column):
    log = 4 + lax.shift_right_logical(column * 14, 5)
    return jnp.left_shift(jnp.ones_like(log), log)


def phase(position, period):
    cycle = jnp.bitwise_and(position, period - 1).astype(jnp.float32)
    return cycle * (2.0 * math.pi / period.astype(jnp.float32))


def remote(source, target, send, receive, device):
    return pltpu.make_async_remote_copy(
        src_ref=source, dst_ref=target, send_sem=send, recv_sem=receive, device_id=device, device_id_type=MESH
    )


class HeadSum:
    def __init__(self, index, peers, part, out, buffers, send_sem, recv_sem):
        self.index = index
        self.me, self.sibling, self.across = peers
        self.part, self.out = part, out
        self.send_a, self.recv_a, self.send_b, self.recv_b, self.final = (buffer.at[index] for buffer in buffers)
        self.send_sem, self.recv_sem = send_sem, recv_sem
        half = part.shape[1] // 2
        self.mine = aligned((self.me % 2) * half, half, half)
        self.theirs = aligned((self.sibling % 2) * half, half, half)

    def copy(self, kind, piece, source, target, device):
        return remote(
            source, target, self.send_sem.at[self.index, kind, piece], self.recv_sem.at[self.index, kind, piece],
            {"head": device},
        )

    def copy_a(self, piece, at):
        return self.copy(0, piece, self.send_a.at[at, :], self.recv_a.at[at, :], self.sibling)

    def copy_b(self, piece, at):
        return self.copy(1, piece, self.send_b.at[at, :], self.recv_b.at[at, :], self.across)

    def copy_c(self, piece, at):
        return self.copy(2, piece, self.final.at[at, :], self.out.at[at, self.mine], self.sibling)

    def begin(self, piece, at):
        self.send_a[at, :] = self.part[at, self.theirs].astype(jnp.bfloat16)
        self.copy_a(piece, at).start()

    def middle(self, piece, at):
        self.copy_a(piece, at).wait_recv()
        summed = self.part[at, self.mine] + self.recv_a[at, :].astype(jnp.float32)
        self.part[at, self.mine] = summed
        self.send_b[at, :] = summed.astype(jnp.bfloat16)
        self.copy_b(piece, at).start()

    def total(self, piece, at, residual=None):
        self.copy_b(piece, at).wait_recv()
        value = self.part[at, self.mine] + self.recv_b[at, :].astype(jnp.float32)
        if residual is not None:
            value = value + residual[at, self.mine]
        value = value.astype(jnp.bfloat16)
        self.final[at, :] = value
        self.copy_c(piece, at).start()
        self.out[at, self.mine] = value

    def end(self, piece, at):
        self.copy_c(piece, at).wait_recv()

    def drain(self, piece, at):
        self.copy_a(piece, at).wait_send()
        self.copy_b(piece, at).wait_send()
        self.copy_c(piece, at).wait_send()


def scratch_list(count, width, chunks, places):
    full = 4 * width
    rows = count // SHORTEN
    frame = LEAD + WINDOW + count
    low = jnp.bfloat16
    wide = jnp.float32
    dma = pltpu.SemaphoreType.DMA
    return [
        ("emb", pltpu.VMEM((256, full), low)),
        ("fq", pltpu.VMEM((full, width), low)),
        ("fk", pltpu.VMEM((full, width), low)),
        ("fv", pltpu.VMEM((full, width), low)),
        ("cols", pltpu.VMEM((full, width), low)),
        ("ws", pltpu.VMEM((SHORTEN, width, full), low)),
        ("cq", pltpu.VMEM((full, width), low)),
        ("ck", pltpu.VMEM((full, width), low)),
        ("cv", pltpu.VMEM((full, width), low)),
        ("co", pltpu.VMEM((width, full), low)),
        ("up", pltpu.VMEM((full, full), low)),
        ("down", pltpu.VMEM((full, full), low)),
        ("lift", pltpu.VMEM((full, SHORTEN * width), low)),
        ("raw", pltpu.VMEM((width // 128, full, SHORTEN, 128), low)),
        ("fine_gain", pltpu.VMEM((1, full), wide)),
        ("coarse_gain", pltpu.VMEM((1, full), wide)),
        ("ffn_gain", pltpu.VMEM((1, full), wide)),
        ("load_sem", dma((17 + width // 128,))),
        ("ids", pltpu.VMEM((1, frame), jnp.int32)),
        ("id_send", dma((2,))),
        ("id_recv", dma((2,))),
        ("col_send", dma((4,))),
        ("col_recv", dma((4,))),
        ("tabs", pltpu.VMEM((6, 256, width), low)),
        ("cos_t", pltpu.VMEM((HALF, frame), wide)),
        ("sin_t", pltpu.VMEM((HALF, frame), wide)),
        ("keys", pltpu.VMEM((frame, width), low)),
        ("values", pltpu.VMEM((width, frame), low)),
        ("query", pltpu.VMEM((width, LEAD + count), low)),
        ("start", pltpu.VMEM((LEAD + count, width), low)),
        ("scores", pltpu.VMEM((WINDOW + count // chunks, 4 * (count // chunks)), wide)),
        ("weights", pltpu.VMEM((WINDOW + count // chunks, 4 * (count // chunks)), low)),
        ("mixed", pltpu.VMEM((CARRY + count, width), low)),
        ("others", pltpu.VMEM((CARRY + count, 3 * width), low)),
        ("mix_send", dma((3, chunks + 1))),
        ("mix_recv", dma((3, chunks + 1))),
        ("stream", pltpu.VMEM((width // 128, CARRY + count, 128), wide)),
        ("part", pltpu.VMEM((rows, full), wide)),
        ("part_b", pltpu.VMEM((rows, full), wide)),
        ("short", pltpu.VMEM((rows, full), low)),
        ("summed", pltpu.VMEM((rows, full), low)),
        ("first", pltpu.VMEM((rows, full), wide)),
        ("second", pltpu.VMEM((rows, full), low)),
        ("send_a", pltpu.VMEM((3, rows, full // 2), low)),
        ("recv_a", pltpu.VMEM((3, rows, full // 2), low)),
        ("send_b", pltpu.VMEM((3, rows, full // 2), low)),
        ("recv_b", pltpu.VMEM((3, rows, full // 2), low)),
        ("final", pltpu.VMEM((3, rows, full // 2), low)),
        ("sum_send", dma((3, 3, chunks))),
        ("sum_recv", dma((3, 3, chunks))),
        ("coarse_cos", pltpu.VMEM((rows, width), wide)),
        ("coarse_sin", pltpu.VMEM((rows, width), wide)),
        ("pair_out", pltpu.VMEM((2, rows, width), low)),
        ("query_out", pltpu.VMEM((2, rows, width // 2), low)),
        ("pairs", pltpu.VMEM((places * rows, width), low)),
        ("queries", pltpu.VMEM((2 * rows, width // 2), low)),
        ("pair_send", dma((places, chunks))),
        ("pair_recv", dma((places, chunks))),
        ("query_send", dma((chunks,))),
        ("query_recv", dma((chunks,))),
        ("top", pltpu.VMEM((2, 1, 2 * rows), wide)),
        ("norm", pltpu.VMEM((2, 1, 2 * rows), wide)),
        ("acc", pltpu.VMEM((width // 2, 2 * rows), wide)),
        ("turn", pltpu.VMEM((rows, width // 2), low)),
        ("heads_in", pltpu.VMEM((rows, width), low)),
        ("turn_send", dma((PIECES,))),
        ("turn_recv", dma((PIECES,))),
        ("spread", pltpu.VMEM((width // 128, count, 128), wide)),
    ]


class Names:
    pass


def block_kernel(names, chunk_rows, *refs):
    (ids_h, fine_gain_h, coarse_gain_h, ffn_gain_h, emb_h, fq_h, fk_h, fv_h, fo_h, ws_h,
     cq_h, ck_h, cv_h, co_h, up_h, down_h, lift_h, out_ref) = refs[:18]
    s = Names()
    for name, ref in zip(names, refs[18:]):
        setattr(s, name, ref)
    count, width = out_ref.shape
    full = 4 * width
    heads = width // HEAD_DIM
    chunks = count // chunk_rows
    group = chunk_rows // SHORTEN
    rows = count // SHORTEN
    frame = LEAD + WINDOW + count
    span = WINDOW + chunk_rows
    lanes = width // 128
    pair = width // 2

    places = lax.axis_size("seq")
    place = lax.axis_index("seq")
    levels = places // 2
    side = place % 2
    level = place // 2
    cross = place + 1 - 2 * side
    me = lax.axis_index("head")
    sibling = me + 1 - 2 * (me % 2)
    across = (me + 2) % 4
    diagonal = (sibling + 2) % 4

    barrier = pltpu.get_barrier_semaphore()
    for device in (sibling, across, diagonal):
        pl.semaphore_signal(barrier, inc=1, device_id={"head": device}, device_id_type=MESH)

    def greet(step, state):
        pl.semaphore_signal(
            barrier, inc=1, device_id={"seq": (place + step) % places}, device_id_type=MESH
        )
        return state

    lax.fori_loop(1, places, greet, 0)

    own_columns = aligned(me * width, width, width)
    own_ids = s.ids.at[:, pl.ds(LEAD + WINDOW, count)]
    loads = {
        name: pltpu.make_async_copy(source, target, s.load_sem.at[index])
        for index, (name, source, target) in enumerate((
            ("ids", ids_h, own_ids), ("emb", emb_h, s.emb), ("fine_gain", fine_gain_h, s.fine_gain),
            ("fk", fk_h, s.fk), ("fv", fv_h, s.fv), ("fq", fq_h, s.fq),
            ("coarse_gain", coarse_gain_h, s.coarse_gain), ("ffn_gain", ffn_gain_h, s.ffn_gain),
            ("cols", fo_h.at[:, own_columns], s.cols.at[pl.ds(0, width), :]),
            ("ws", ws_h, s.ws), ("cq", cq_h, s.cq), ("ck", ck_h, s.ck), ("cv", cv_h, s.cv), ("co", co_h, s.co),
            ("up", up_h, s.up), ("down", down_h, s.down),
            *((f"lift{b}", lift_h.at[:, :, pl.ds(b * 128, 128)], s.raw.at[b]) for b in range(lanes)),
        ))
    }
    lift_names = tuple(f"lift{block}" for block in range(lanes))

    def start_loads(*names):
        for name in names:
            loads[name].start()

    start_loads("ids", "emb", "fine_gain", "fk", "fv", "fq")

    @pl.when(place < 1)
    def _():
        s.ids[:, LEAD : LEAD + WINDOW] = jnp.zeros((1, WINDOW), jnp.int32)

    @pl.when(place < 2)
    def _():
        s.ids[:, :LEAD] = jnp.zeros((1, LEAD), jnp.int32)

    def clear(index, state):
        chunk = index // (places - 2)
        blank = index % (places - 2)

        @pl.when(blank + 2 >= 2 * level + 2)
        def _():
            at = aligned((chunk * places + blank + 2) * group, group, group)
            s.pairs[at, :] = jnp.zeros((group, width), jnp.bfloat16)

        return state

    lax.fori_loop(0, chunks * (places - 2), clear, 0)

    column = lax.broadcasted_iota(jnp.int32, (HALF, 128), 0)
    lane = lax.broadcasted_iota(jnp.int32, (HALF, 128), 1)
    period = periods(column)
    small = phase(lane, period)
    base = (place - 1) * count - LEAD
    large = phase(base + 128 * lane, period)
    cos_b, sin_b, cos_a, sin_a = jnp.cos(small), jnp.sin(small), jnp.cos(large), jnp.sin(large)
    for block in range(frame // 128):
        at = slice(block * 128, block * 128 + 128)
        cos_k, sin_k = cos_a[:, block : block + 1], sin_a[:, block : block + 1]
        s.cos_t[:, at] = cos_b * cos_k - sin_b * sin_k
        s.sin_t[:, at] = sin_b * cos_k + cos_b * sin_k

    lane_f = lax.broadcasted_iota(jnp.int32, (rows, 128), 1) % HEAD_DIM
    period_f = periods(lane_f % HALF)
    angle_f = phase(place * rows + lax.broadcasted_iota(jnp.int32, (rows, 128), 0), period_f)
    cos_f = jnp.cos(angle_f)
    sin_f = jnp.where(lane_f < HALF, -jnp.sin(angle_f), jnp.sin(angle_f))
    for block in range(lanes):
        s.coarse_cos[:, block * 128 : block * 128 + 128] = cos_f
        s.coarse_sin[:, block * 128 : block * 128 + 128] = sin_f

    pl.semaphore_wait(barrier, places + 2)

    def id_copy(steps):
        if steps == 1:
            target = s.ids.at[:, pl.ds(LEAD, WINDOW)]
            source = ids_h
        else:
            target = s.ids.at[:, pl.ds(0, LEAD)]
            source = ids_h.at[:, pl.ds(count - LEAD, LEAD)]
        device = (place + steps) % places
        return remote(source, target, s.id_send.at[steps - 1], s.id_recv.at[steps - 1], {"seq": device})

    for steps in (1, 2):
        @pl.when(place + steps < places)
        def _():
            id_copy(steps).start()

    def column_copy(flip, device):
        return remote(
            fo_h.at[:, aligned(device * width, width, width)], s.cols.at[pl.ds(flip * width, width), :],
            s.col_send.at[flip], s.col_recv.at[flip], {"head": device},
        )

    column_copies = [column_copy(flip, device) for flip, device in ((1, sibling), (2, across), (3, diagonal))]
    for copy in column_copies:
        copy.start()

    loads["emb"].wait()
    loads["fine_gain"].wait()
    level_in = normed(s.emb[...].astype(jnp.float32), s.fine_gain[...])

    def split(values):
        high = values.astype(jnp.bfloat16)
        return high, (values - high.astype(jnp.float32)).astype(jnp.bfloat16)

    loads["fk"].wait()
    s.tabs[0], s.tabs[1] = split(dot(level_in, s.fk[...]).T)
    loads["fv"].wait()
    s.tabs[2] = dot(level_in, s.fv[...]).T.astype(jnp.bfloat16)
    loads["fq"].wait()
    s.tabs[3], s.tabs[4] = split(dot(level_in, s.fq[...]).T)
    s.tabs[5] = s.emb[:, own_columns]
    loads["ids"].wait()
    start_loads("cols", "ws", "coarse_gain", "ffn_gain", "cq", "ck", "cv")

    def turned(joined, at):
        cosine, sine = s.cos_t[:, at], s.sin_t[:, at]
        pieces = []
        for head in range(heads):
            low = joined[head * HEAD_DIM : head * HEAD_DIM + HALF]
            high = joined[head * HEAD_DIM + HALF : (head + 1) * HEAD_DIM]
            pieces += [low * cosine - high * sine, high * cosine + low * sine]
        return jnp.concatenate(pieces, axis=0)

    def hot_rows(at, size):
        levels_at = lax.broadcasted_iota(jnp.int32, (256, size), 0)
        return jnp.where(levels_at == s.ids[:, at], 1.0, 0.0).astype(jnp.bfloat16)

    def key_rows(begin, size):
        at = aligned(begin, size, 128)
        hot = hot_rows(at, size)
        s.keys[at, :] = turned(dot(s.tabs[0], hot) + dot(s.tabs[1], hot), at).T.astype(jnp.bfloat16)
        s.values[:, at] = dot(s.tabs[2], hot).astype(jnp.bfloat16)

    def query_rows(begin, size):
        at = aligned(begin, size, 128)
        to = aligned(begin - WINDOW, size, 128)
        hot = hot_rows(at, size)
        s.query[:, to] = turned(dot(s.tabs[3], hot) + dot(s.tabs[4], hot), at).astype(jnp.bfloat16)
        s.start[to, :] = dot_tn(hot, s.tabs[5]).astype(jnp.bfloat16)

    own_block = min(512, count)

    def own_rows(index, state):
        key_rows(LEAD + WINDOW + index * own_block, own_block)
        query_rows(LEAD + WINDOW + index * own_block, own_block)
        return state

    def prior_rows(index, state):
        key_rows(index * 384, 384)
        return state

    lax.fori_loop(0, count // own_block, own_rows, 0)
    for steps in (1, 2):
        @pl.when(place >= steps)
        def _():
            id_copy(steps).wait_recv()

    lax.fori_loop(0, (LEAD + WINDOW) // 384, prior_rows, 0)
    query_rows(WINDOW, LEAD)

    def weigh(scores):
        top = scores[0]
        for piece in scores[1:]:
            top = jnp.maximum(top, piece)
        top = jnp.max(top, axis=0, keepdims=True)
        weights = [jnp.exp2((piece - top) * EXP2_SCALE) for piece in scores]
        total = weights[0]
        for piece in weights[1:]:
            total = total + piece
        total = jnp.sum(total, axis=0, keepdims=True)
        return jnp.concatenate([piece.astype(jnp.bfloat16) for piece in weights], axis=0), total

    def mixed_rows(chunk):
        return aligned(CARRY + chunk * chunk_rows, chunk_rows, CARRY)

    def mix_copies(chunk, at):
        def slot(which):
            return s.others.at[at, pl.ds((which - 1) * width, width)]

        def copy(kind, source, target, device):
            return remote(source, target, s.mix_send.at[kind, chunk], s.mix_recv.at[kind, chunk], {"head": device})

        return (
            copy(0, s.mixed.at[at, :], slot(2), across),
            copy(1, s.mixed.at[at, :], slot(1), sibling),
            copy(2, slot(2), slot(3), sibling),
        )

    carry_at = pl.ds(0, CARRY)
    carry_copies = mix_copies(chunks, carry_at)

    start_loads("co", "up", "down", *lift_names)

    def attend_carry():
        lane_slot = lax.broadcasted_iota(jnp.int32, (HEAD_DIM, LEAD), 1) // 32
        packed = []
        for head in range(heads):
            rolled = pltpu.roll(s.query[head * HEAD_DIM : (head + 1) * HEAD_DIM, :LEAD].astype(jnp.float32), (32 * head + 32) % LEAD, 1)
            packed.append(jnp.where(lane_slot == head, rolled, 0.0))
        packed = jnp.concatenate(packed, axis=0).astype(jnp.bfloat16)
        scores = dot(s.keys[: LEAD + WINDOW, :], packed)
        key = lax.broadcasted_iota(jnp.int32, scores.shape, 0)
        last = lax.broadcasted_iota(jnp.int32, scores.shape, 1) % 32 + (LEAD + WINDOW - 32)
        floor = jnp.where(place < 2, LEAD, 0)
        allowed = (key > last - WINDOW) & (key <= last) & (key >= floor)
        weights, total = weigh([jnp.where(allowed, scores, masked_low)])
        out = dot(s.values[:, : LEAD + WINDOW], weights) / total
        unpacked = [
            pltpu.roll(out[head * HEAD_DIM : (head + 1) * HEAD_DIM, :], (LEAD - 32 * head) % LEAD, 1) for head in range(heads)
        ]
        s.mixed[carry_at, :] = jnp.concatenate(unpacked, axis=0).T[32 - CARRY : 32, :].astype(jnp.bfloat16)
        carry_copies[0].start()
        carry_copies[1].start()

    part_keys = 3 * chunk_rows if span % (3 * chunk_rows) == 0 else chunk_rows
    row = lax.broadcasted_iota(jnp.int32, (chunk_rows, chunk_rows), 0)
    column = lax.broadcasted_iota(jnp.int32, (chunk_rows, chunk_rows), 1)

    def each_head(allowed, piece):
        return jnp.concatenate(
            [
                jnp.where(allowed, piece[:, head * chunk_rows : (head + 1) * chunk_rows], masked_low)
                for head in range(piece.shape[1] // chunk_rows)
            ],
            axis=1,
        )

    sets = [tuple(range(first, min(first + SET, heads))) for first in range(0, heads, SET)]

    def by_eights(values):
        return values.reshape(values.shape[0] // 8, 8, values.shape[1])

    row_head = lax.broadcasted_iota(jnp.int32, (width, chunk_rows), 0) // HEAD_DIM

    def attend_chunk(chunk):
        begin = chunk * chunk_rows
        floor = jnp.where(place == 0, WINDOW - begin, 0)
        key_at = aligned(LEAD + begin, span, 128)
        query = s.query[:, aligned(LEAD + begin, chunk_rows, chunk_rows)]
        tops, totals = [], []
        for side_heads in sets:
            lanes_of = slice(side_heads[0] * chunk_rows, (side_heads[-1] + 1) * chunk_rows)
            stacked = jnp.concatenate(
                [jnp.where(row_head == head, query, jnp.zeros_like(query)) for head in side_heads], axis=1
            )
            top = None
            for part in range(0, span, part_keys):
                scores = dot(s.keys[aligned(LEAD + begin + part, part_keys, 128), :], stacked)
                for at in range(part, part + part_keys, chunk_rows):
                    piece = scores[at - part : at - part + chunk_rows, :]
                    if at == span - chunk_rows:
                        piece = each_head(row <= column, piece)
                    else:
                        piece = piece + jnp.where(at < floor, masked_low, 0.0)
                        if at == 0:
                            piece = each_head(row > column, piece)
                    s.scores[at : at + chunk_rows, lanes_of] = piece
                    peak = jnp.max(by_eights(piece), axis=0)
                    top = peak if top is None else jnp.maximum(top, peak)
            tops.append(jnp.max(top, axis=0, keepdims=True))
        outs = []
        for which, side_heads in enumerate(sets):
            lanes_of = slice(side_heads[0] * chunk_rows, (side_heads[-1] + 1) * chunk_rows)
            total = jnp.zeros((8, len(side_heads) * chunk_rows), jnp.float32)
            for at in range(0, span, chunk_rows):
                weights = jnp.exp2((s.scores[at : at + chunk_rows, lanes_of] - tops[which]) * EXP2_SCALE)
                total = total + jnp.sum(by_eights(weights), axis=0)
                s.weights[at : at + chunk_rows, lanes_of] = weights.astype(jnp.bfloat16)
            total = jnp.sum(total, axis=0, keepdims=True)
            for index, head in enumerate(side_heads):
                of = slice(head * chunk_rows, (head + 1) * chunk_rows)
                share = dot(s.values[head * HEAD_DIM : (head + 1) * HEAD_DIM, key_at], s.weights[:, of])
                outs.append(share / total[:, index * chunk_rows : (index + 1) * chunk_rows])
        at = mixed_rows(chunk)
        s.mixed[at, :] = jnp.concatenate(outs, axis=0).T.astype(jnp.bfloat16)
        copies = mix_copies(chunk, at)
        copies[0].start()
        copies[1].start()

    def fine_rows(at, start_at):
        merged = dot(s.mixed[at, :], s.cols[:width, :]) + dot(s.others[at, :], s.cols[width:, :])
        value = (s.start[start_at, :].astype(jnp.float32) + merged).astype(jnp.bfloat16).astype(jnp.float32)
        for block in range(lanes):
            s.stream[block, at, :] = value[:, block * 128 : block * 128 + 128]

    peers = (me, sibling, across)
    buffers = (s.send_a, s.recv_a, s.send_b, s.recv_b, s.final)
    short_sum = HeadSum(0, peers, s.part, s.short, buffers, s.sum_send, s.sum_recv)

    def short_rows(chunk):
        return aligned(chunk * group, group, group)

    def relay_chunk(chunk):
        @pl.when(chunk == 0)
        def _():
            carry_copies[0].wait_recv()
            carry_copies[2].start()

        copies = mix_copies(chunk, mixed_rows(chunk))
        copies[0].wait_recv()
        copies[2].start()

    def finish_chunk(chunk):
        @pl.when(chunk == 0)
        def _():
            for copy in column_copies:
                copy.wait_recv()
            loads["cols"].wait()
            loads["ws"].wait()
            carry_copies[1].wait_recv()
            carry_copies[2].wait_recv()
            fine_rows(carry_at, pl.ds(LEAD - CARRY, CARRY))

            @pl.when(place == 0)
            def _():
                s.stream[:, 0:CARRY, :] = jnp.zeros((lanes, CARRY, 128), jnp.float32)

        at = mixed_rows(chunk)
        copies = mix_copies(chunk, at)
        copies[1].wait_recv()
        copies[2].wait_recv()
        fine_rows(at, aligned(LEAD + chunk * chunk_rows, chunk_rows, chunk_rows))
        total = jnp.zeros((group, full), jnp.float32)
        for offset in range(SHORTEN):
            begin = CARRY - (SHORTEN - 1) + offset + chunk * chunk_rows
            member = jnp.concatenate(
                [s.stream[block, pl.ds(begin, group, stride=SHORTEN), :] for block in range(lanes)], axis=1
            )
            total = total + dot(member.astype(jnp.bfloat16), s.ws[offset])
        s.part[short_rows(chunk), :] = total
        short_sum.begin(chunk, short_rows(chunk))

    def pair_rows(chunk, source):
        return aligned((chunk * places + source) * group, group, group)

    def pair_copy(chunk, target):
        at = pair_rows(chunk, place)
        return remote(
            s.pair_out.at[target % 2, short_rows(chunk), :], s.pairs.at[at, :],
            s.pair_send.at[target, chunk], s.pair_recv.at[place, chunk], {"seq": target},
        )

    def pair_arrival(chunk, source):
        at = pair_rows(chunk, source)
        return remote(
            s.pairs.at[at, :], s.pairs.at[at, :], s.pair_send.at[source, chunk], s.pair_recv.at[source, chunk],
            {"seq": cross},
        )

    def query_copy(chunk):
        at = short_rows(chunk)
        return remote(
            s.query_out.at[1 - side, at, :], s.queries.at[aligned(side * rows + chunk * group, group, group), :],
            s.query_send.at[chunk], s.query_recv.at[chunk], {"seq": cross},
        )

    def for_targets(action):
        def one(index, state):
            target = places - 1 - index

            @pl.when(target != place)
            def _():
                action(target)

            return state

        lax.fori_loop(0, places - 2 * level, one, 0)

    def project_chunk(chunk):
        @pl.when(chunk == 0)
        def _():
            for name in ("coarse_gain", "cq", "ck", "cv"):
                loads[name].wait()

        at = short_rows(chunk)
        short_sum.end(chunk, at)
        coarse_in = normed(s.short[at, :].astype(jnp.float32), s.coarse_gain[...])
        cosine, sine = s.coarse_cos[at, :], s.coarse_sin[at, :]
        is_low = lax.broadcasted_iota(jnp.int32, (group, width), 1) % HEAD_DIM < HALF

        def rotated(values):
            other = jnp.where(is_low, pltpu.roll(values, width - HALF, 1), pltpu.roll(values, HALF, 1))
            return (values * cosine + other * sine).astype(jnp.bfloat16)

        key = rotated(dot(coarse_in, s.ck[...]))
        value = dot(coarse_in, s.cv[...]).astype(jnp.bfloat16)
        for half in range(2):
            s.pair_out[half, at, :pair] = key[:, half * pair : half * pair + pair]
            s.pair_out[half, at, pair:] = value[:, half * pair : half * pair + pair]
        for_targets(lambda target: pair_copy(chunk, target).start())
        query = rotated(dot(coarse_in, s.cq[...]))
        for half in range(2):
            s.query_out[half, at, :] = query[:, half * pair : half * pair + pair]
        query_copy(chunk).start()
        s.pairs[pair_rows(chunk, place), :] = s.pair_out[side, at, :]
        s.queries[aligned(side * rows + chunk * group, group, group), :] = s.query_out[side, at, :]

    def total_chunk(chunk):
        short_sum.total(chunk, short_rows(chunk))

    def middle_chunk(chunk):
        short_sum.middle(chunk, short_rows(chunk))

    ahead = ((RELAY, relay_chunk), (TOTAL, total_chunk))
    behind = ((PROJECT, project_chunk), (MIDDLE, middle_chunk), (FINISH, finish_chunk))

    def one_step(step, state):
        def run(stages):
            for lag, action in stages:
                @pl.when(step >= lag)
                def _():
                    action(step - lag)

        run(ahead)
        attend_chunk(step)

        @pl.when(step == 0)
        def _():
            attend_carry()

        run(behind)
        return state

    lax.fori_loop(0, chunks, one_step, 0)

    left = {action: max(0, chunks - lag) for lag, action in ahead + behind}

    def rest(action, upto):
        for chunk in range(left[action], upto):
            action(chunk)
        left[action] = max(left[action], upto)

    for action, back in (
        (relay_chunk, 1), (total_chunk, 4), (middle_chunk, 2), (project_chunk, 4), (finish_chunk, 1), (total_chunk, 3),
        (relay_chunk, 0), (middle_chunk, 1), (project_chunk, 3), (finish_chunk, 0), (total_chunk, 2),
        (middle_chunk, 0), (project_chunk, 2), (total_chunk, 1), (project_chunk, 1),
        (total_chunk, 0), (project_chunk, 0),
    ):
        rest(action, chunks - back)

    def wait_chunk(chunk):
        def one(source, state):
            pair_arrival(chunk, source).wait_recv()
            return state

        lax.fori_loop(0, 2 * level, one, 0)

    def wait_queries(chunk, state):
        query_copy(chunk).wait_recv()
        pair_arrival(chunk, cross).wait_recv()
        return state

    lax.fori_loop(0, chunks, wait_queries, 0)

    per_chunk = places * group
    pair_lane = lax.broadcasted_iota(jnp.int32, (2 * rows, pair), 1) // HEAD_DIM
    queries = s.queries[...]
    masked = [jnp.where(pair_lane == head, queries, jnp.zeros_like(queries)) for head in range(pair // HEAD_DIM)]

    def absorb(block, mask, first):
        keys, values = block[:, :pair], block[:, pair:]
        values_t = values.astype(jnp.float32).T.astype(jnp.bfloat16)
        for head in range(pair // HEAD_DIM):
            scores = dot_nt(keys, masked[head])
            pieces = [mask(begin, scores[begin : begin + group, :]) for begin in range(0, scores.shape[0], group)]
            peak = pieces[0]
            for piece in pieces[1:]:
                peak = jnp.maximum(peak, piece)
            fresh = jnp.max(peak, axis=0, keepdims=True)
            if not first:
                fresh = jnp.maximum(s.top[head], fresh)
            weights = [jnp.exp2((piece - fresh) * EXP2_SCALE) for piece in pieces]
            total = weights[0]
            for piece in weights[1:]:
                total = total + piece
            total = jnp.sum(total, axis=0, keepdims=True)
            of = slice(head * HEAD_DIM, (head + 1) * HEAD_DIM)
            rounded = jnp.concatenate([piece.astype(jnp.bfloat16) for piece in weights], axis=0)
            share = dot(values_t[of, :], rounded)
            if not first:
                factor = jnp.exp2((s.top[head] - fresh) * EXP2_SCALE)
                total = total + s.norm[head] * factor
                share = share + s.acc[of, :] * factor
            s.top[head] = fresh
            s.norm[head] = total
            s.acc[of, :] = share

    ahead_of = lax.broadcasted_iota(jnp.int32, (group, 2 * rows), 1) - lax.broadcasted_iota(
        jnp.int32, (group, 2 * rows), 0
    )

    def own_mask(begin, piece):
        index = begin // group
        return jnp.where(ahead_of >= (index % 2) * rows + (index // 2) * group, piece, masked_low)

    own_level = jnp.concatenate(
        [s.pairs[aligned((chunk * places + 2 * level) * group, 2 * group, 2 * group), :] for chunk in range(chunks)], axis=0
    )
    absorb(own_level, own_mask, True)

    def key_step(step, state):
        if per_chunk <= STEP_KEYS:
            for inner in range(STEP_KEYS // per_chunk):
                wait_chunk(step * (STEP_KEYS // per_chunk) + inner)
        else:
            ratio = per_chunk // STEP_KEYS

            @pl.when(step % ratio == 0)
            def _():
                wait_chunk(step // ratio)

        def level_mask(begin, piece):
            source = (step * STEP_KEYS + begin) % per_chunk // group
            return piece + jnp.where(source < 2 * level, 0.0, masked_low)

        absorb(s.pairs[aligned(step * STEP_KEYS, STEP_KEYS, STEP_KEYS), :], level_mask, False)
        return state

    lax.fori_loop(0, places * rows // STEP_KEYS, key_step, 0)

    size = rows // PIECES
    at = [pl.ds(piece * size, size) for piece in range(PIECES)]

    def turn_copy(piece):
        return remote(
            s.turn.at[at[piece], :], s.heads_in.at[at[piece], aligned(side * pair, pair, pair)],
            s.turn_send.at[piece], s.turn_recv.at[piece], {"seq": cross},
        )

    def mixed_of(at):
        shares = [
            s.acc[head * HEAD_DIM : (head + 1) * HEAD_DIM, at] / s.norm[head, :, at] for head in range(pair // HEAD_DIM)
        ]
        return jnp.concatenate(shares, axis=0).T.astype(jnp.bfloat16)

    s.turn[...] = mixed_of(aligned((1 - side) * rows, rows, rows))
    for piece in range(PIECES):
        turn_copy(piece).start()
    s.heads_in[:, aligned(side * pair, pair, pair)] = mixed_of(aligned(side * rows, rows, rows))

    for name in lift_names:
        loads[name].wait()
    part_rows = count // SHORTEN
    for block in range(lanes):
        for begin in range(0, full, part_rows):
            flat = s.raw.at[block, pl.ds(begin, part_rows)].reshape(part_rows * SHORTEN, 128)
            s.spread[block] = flat[...].astype(jnp.float32)
            for member in range(SHORTEN):
                s.lift[begin : begin + part_rows, member * width + block * 128 : member * width + block * 128 + 128] = (
                    s.spread[block, pl.ds(member, part_rows, stride=SHORTEN), :].astype(jnp.bfloat16)
                )

    loads["co"].wait()

    out_sum = HeadSum(1, peers, s.part, s.summed, buffers, s.sum_send, s.sum_recv)
    ffn_sum = HeadSum(2, peers, s.part_b, s.second, buffers, s.sum_send, s.sum_recv)

    for piece in range(PIECES):
        turn_copy(piece).wait_recv()
        s.part[at[piece], :] = dot(s.heads_in[at[piece], :], s.co[...])
        out_sum.begin(piece, at[piece])
    for name in ("ffn_gain", "up", "down"):
        loads[name].wait()
    for piece in range(PIECES):
        out_sum.middle(piece, at[piece])
    for steps in (1, 2):
        @pl.when(place + steps < places)
        def _():
            id_copy(steps).wait_send()

    for copy in column_copies:
        copy.wait_send()
    for copy in carry_copies:
        copy.wait_send()

    def drain(chunk, state):
        for copy in mix_copies(chunk, mixed_rows(chunk)):
            copy.wait_send()
        short_sum.drain(chunk, short_rows(chunk))
        for_targets(lambda target: pair_copy(chunk, target).wait_send())
        query_copy(chunk).wait_send()
        return state

    lax.fori_loop(0, chunks, drain, 0)

    def feed(piece):
        out_sum.end(piece, at[piece])
        value = s.short[at[piece], :].astype(jnp.float32) + s.summed[at[piece], :].astype(jnp.float32)
        s.first[at[piece], :] = value
        inner = jax.nn.gelu(dot(normed(value, s.ffn_gain[...]), s.up[...])).astype(jnp.bfloat16)
        s.part_b[at[piece], :] = dot(inner, s.down[...])
        ffn_sum.begin(piece, at[piece])

    def raise_rows(piece):
        ffn_sum.end(piece, at[piece])
        for member in range(SHORTEN):
            lifted = dot(s.second[at[piece], :], s.lift[:, member * width : (member + 1) * width])
            for block in range(lanes):
                s.spread[block, pl.ds(SHORTEN * size * piece + member, size, stride=SHORTEN), :] = lifted[
                    :, block * 128 : block * 128 + 128
                ]
        for block in range(lanes):
            to = slice(SHORTEN * size * piece, SHORTEN * size * (piece + 1))
            base_at = slice(CARRY + SHORTEN * size * piece, CARRY + SHORTEN * size * (piece + 1))
            out_ref[to, block * 128 : block * 128 + 128] = (
                s.stream[block, base_at, :] + s.spread[block, to, :]
            ).astype(jnp.bfloat16)

    for step in range(PIECES + 4):
        if step < PIECES:
            out_sum.total(step, at[step])
        if 0 <= step - 1 < PIECES:
            feed(step - 1)
        if 0 <= step - 2 < PIECES:
            ffn_sum.middle(step - 2, at[step - 2])
        if 0 <= step - 3 < PIECES:
            ffn_sum.total(step - 3, at[step - 3], s.first)
        if 0 <= step - 4 < PIECES:
            raise_rows(step - 4)

    for piece in range(PIECES):
        turn_copy(piece).wait_send()
    for piece in range(PIECES):
        out_sum.drain(piece, at[piece])
        ffn_sum.drain(piece, at[piece])


def local(
    token_ids,
    embedding,
    fine_norm,
    fine_query,
    fine_key,
    fine_value,
    fine_output,
    shorten_weight,
    coarse_norm,
    coarse_query,
    coarse_key,
    coarse_value,
    coarse_output,
    ffn_norm,
    ffn_up,
    ffn_down,
    upsample_weight,
):
    count = token_ids.shape[0]
    width = fine_query.shape[1]
    chunk_rows = min(128, count)
    chunks = count // chunk_rows
    scratch = scratch_list(count, width, chunks, lax.axis_size("seq"))
    names = [name for name, _ in scratch]

    def kernel(*refs):
        block_kernel(names, chunk_rows, *refs)

    return pl.pallas_call(
        kernel,
        out_shape=jax.ShapeDtypeStruct((count, width), jnp.bfloat16),
        in_specs=[HBM_SPEC] * 17,
        out_specs=VMEM_SPEC,
        scratch_shapes=[shape for _, shape in scratch],
        compiler_params=pltpu.CompilerParams(
            collective_id=1, has_side_effects=True, vmem_limit_bytes=46 * 2**20
        ),
        name="block_kernel",
    )(
        *(
            pltpu.with_memory_space_constraint(array, pltpu.HBM)
            for array in (
                token_ids.reshape(1, count), fine_norm.reshape(1, D), coarse_norm.reshape(1, D), ffn_norm.reshape(1, D),
                embedding, fine_query, fine_key, fine_value, fine_output, shorten_weight, coarse_query, coarse_key,
                coarse_value, coarse_output, ffn_up, ffn_down, upsample_weight,
            )
        ),
    )


def solution(mesh):
    return jax.shard_map(
        local,
        mesh=mesh,
        in_specs=(
            P("seq"),
            P(),
            P(),
            P(None, "head"),
            P(None, "head"),
            P(None, "head"),
            P("head", None),
            P(None, "head", None),
            P(),
            P(None, "head"),
            P(None, "head"),
            P(None, "head"),
            P("head", None),
            P(),
            P(None, "head"),
            P("head", None),
            P(None, None, "head"),
        ),
        out_specs=P("seq", "head"),
        check_vma=False,
    )
```

```python
import math

import jax
import jax.numpy as jnp
from jax import lax
from jax.experimental import pallas as pl
from jax.experimental.pallas import tpu as pltpu
from jax.sharding import PartitionSpec as P

D = 1024
HEAD_DIM = 64
HALF = HEAD_DIM // 2
SHORTEN = 4
WINDOW = 1024
LEAD = 128
CARRY = 16

epsilon = 1e-06
masked_low = -1e30
MESH = pl.DeviceIdType.MESH
EXP2_SCALE = HEAD_DIM ** (-0.5) * math.log2(math.e)
VMEM_SPEC = pl.BlockSpec(memory_space=pltpu.VMEM)
HBM_SPEC = pl.BlockSpec(memory_space=pltpu.HBM)

RELAY, FINISH, MIDDLE, TOTAL, PROJECT = (2, 2, 3, 5, 5)
STEP_KEYS = 1024
PIECES = 4
SET = 2


def dot(left, right):
    return jnp.dot(left, right, preferred_element_type=jnp.float32)


def dot_nt(left, right):
    return lax.dot_general(left, right, (((1,), (1,)), ((), ())), preferred_element_type=jnp.float32)


def dot_tn(left, right):
    return lax.dot_general(left, right, (((0,), (0,)), ((), ())), preferred_element_type=jnp.float32)


def normed(data, gain):
    power = jnp.mean(data * data, axis=1, keepdims=True)
    return (data * lax.rsqrt(power + epsilon) * gain).astype(jnp.bfloat16)


def aligned(start, size, unit):
    return pl.ds(pl.multiple_of(start, unit), size)


def periods(column):
    log = 4 + lax.shift_right_logical(column * 14, 5)
    return jnp.left_shift(jnp.ones_like(log), log)


def phase(position, period):
    cycle = jnp.bitwise_and(position, period - 1).astype(jnp.float32)
    return cycle * (2.0 * math.pi / period.astype(jnp.float32))


def remote(source, target, send, receive, device):
    return pltpu.make_async_remote_copy(
        src_ref=source, dst_ref=target, send_sem=send, recv_sem=receive, device_id=device, device_id_type=MESH
    )


class HeadSum:
    def __init__(self, index, peers, part, out, buffers, send_sem, recv_sem):
        self.index = index
        self.me, self.sibling, self.across = peers
        self.part, self.out = part, out
        self.send_a, self.recv_a, self.send_b, self.recv_b, self.final = (buffer.at[index] for buffer in buffers)
        self.send_sem, self.recv_sem = send_sem, recv_sem
        half = part.shape[1] // 2
        self.mine = aligned((self.me % 2) * half, half, half)
        self.theirs = aligned((self.sibling % 2) * half, half, half)

    def copy(self, kind, piece, source, target, device):
        return remote(
            source, target, self.send_sem.at[self.index, kind, piece], self.recv_sem.at[self.index, kind, piece],
            {"head": device},
        )

    def copy_a(self, piece, at):
        return self.copy(0, piece, self.send_a.at[at, :], self.recv_a.at[at, :], self.sibling)

    def copy_b(self, piece, at):
        return self.copy(1, piece, self.send_b.at[at, :], self.recv_b.at[at, :], self.across)

    def copy_c(self, piece, at):
        return self.copy(2, piece, self.final.at[at, :], self.out.at[at, self.mine], self.sibling)

    def begin(self, piece, at):
        self.send_a[at, :] = self.part[at, self.theirs].astype(jnp.bfloat16)
        self.copy_a(piece, at).start()

    def middle(self, piece, at):
        self.copy_a(piece, at).wait_recv()
        summed = self.part[at, self.mine] + self.recv_a[at, :].astype(jnp.float32)
        self.part[at, self.mine] = summed
        self.send_b[at, :] = summed.astype(jnp.bfloat16)
        self.copy_b(piece, at).start()

    def total(self, piece, at, residual=None):
        self.copy_b(piece, at).wait_recv()
        value = self.part[at, self.mine] + self.recv_b[at, :].astype(jnp.float32)
        if residual is not None:
            value = value + residual[at, self.mine]
        value = value.astype(jnp.bfloat16)
        self.final[at, :] = value
        self.copy_c(piece, at).start()
        self.out[at, self.mine] = value

    def end(self, piece, at):
        self.copy_c(piece, at).wait_recv()

    def drain(self, piece, at):
        self.copy_a(piece, at).wait_send()
        self.copy_b(piece, at).wait_send()
        self.copy_c(piece, at).wait_send()


def scratch_list(count, width, chunks, places):
    full = 4 * width
    rows = count // SHORTEN
    frame = LEAD + WINDOW + count
    low = jnp.bfloat16
    wide = jnp.float32
    dma = pltpu.SemaphoreType.DMA
    return [
        ("emb", pltpu.VMEM((256, full), low)),
        ("fq", pltpu.VMEM((full, width), low)),
        ("fk", pltpu.VMEM((full, width), low)),
        ("fv", pltpu.VMEM((full, width), low)),
        ("cols", pltpu.VMEM((full, width), low)),
        ("ws", pltpu.VMEM((SHORTEN, width, full), low)),
        ("cq", pltpu.VMEM((full, width), low)),
        ("ck", pltpu.VMEM((full, width), low)),
        ("cv", pltpu.VMEM((full, width), low)),
        ("co", pltpu.VMEM((width, full), low)),
        ("up", pltpu.VMEM((full, full), low)),
        ("down", pltpu.VMEM((full, full), low)),
        ("lift", pltpu.VMEM((full, SHORTEN * width), low)),
        ("raw", pltpu.VMEM((width // 128, full, SHORTEN, 128), low)),
        ("fine_gain", pltpu.VMEM((1, full), wide)),
        ("coarse_gain", pltpu.VMEM((1, full), wide)),
        ("ffn_gain", pltpu.VMEM((1, full), wide)),
        ("load_sem", dma((17 + width // 128,))),
        ("ids", pltpu.VMEM((1, frame), jnp.int32)),
        ("id_send", dma((2,))),
        ("id_recv", dma((2,))),
        ("col_send", dma((4,))),
        ("col_recv", dma((4,))),
        ("tabs", pltpu.VMEM((6, 256, width), low)),
        ("cos_t", pltpu.VMEM((HALF, frame), wide)),
        ("sin_t", pltpu.VMEM((HALF, frame), wide)),
        ("keys", pltpu.VMEM((frame, width), low)),
        ("values", pltpu.VMEM((width, frame), low)),
        ("query", pltpu.VMEM((width, LEAD + count), low)),
        ("start", pltpu.VMEM((LEAD + count, width), low)),
        ("scores", pltpu.VMEM((WINDOW + count // chunks, 4 * (count // chunks)), wide)),
        ("weights", pltpu.VMEM((WINDOW + count // chunks, 4 * (count // chunks)), low)),
        ("mixed", pltpu.VMEM((CARRY + count, width), low)),
        ("others", pltpu.VMEM((CARRY + count, 3 * width), low)),
        ("mix_send", dma((3, chunks + 1))),
        ("mix_recv", dma((3, chunks + 1))),
        ("stream", pltpu.VMEM((width // 128, CARRY + count, 128), wide)),
        ("part", pltpu.VMEM((rows, full), wide)),
        ("part_b", pltpu.VMEM((rows, full), wide)),
        ("short", pltpu.VMEM((rows, full), low)),
        ("summed", pltpu.VMEM((rows, full), low)),
        ("first", pltpu.VMEM((rows, full), wide)),
        ("second", pltpu.VMEM((rows, full), low)),
        ("send_a", pltpu.VMEM((3, rows, full // 2), low)),
        ("recv_a", pltpu.VMEM((3, rows, full // 2), low)),
        ("send_b", pltpu.VMEM((3, rows, full // 2), low)),
        ("recv_b", pltpu.VMEM((3, rows, full // 2), low)),
        ("final", pltpu.VMEM((3, rows, full // 2), low)),
        ("sum_send", dma((3, 3, chunks))),
        ("sum_recv", dma((3, 3, chunks))),
        ("coarse_cos", pltpu.VMEM((rows, width), wide)),
        ("coarse_sin", pltpu.VMEM((rows, width), wide)),
        ("pair_out", pltpu.VMEM((2, rows, width), low)),
        ("query_out", pltpu.VMEM((2, rows, width // 2), low)),
        ("pairs", pltpu.VMEM((places * rows, width), low)),
        ("queries", pltpu.VMEM((2 * rows, width // 2), low)),
        ("pair_send", dma((places, chunks))),
        ("pair_recv", dma((places, chunks))),
        ("query_send", dma((chunks,))),
        ("query_recv", dma((chunks,))),
        ("top", pltpu.VMEM((2, 1, 2 * rows), wide)),
        ("norm", pltpu.VMEM((2, 1, 2 * rows), wide)),
        ("acc", pltpu.VMEM((width // 2, 2 * rows), wide)),
        ("turn", pltpu.VMEM((rows, width // 2), low)),
        ("heads_in", pltpu.VMEM((rows, width), low)),
        ("turn_send", dma((PIECES,))),
        ("turn_recv", dma((PIECES,))),
        ("spread", pltpu.VMEM((width // 128, count, 128), wide)),
    ]


class Names:
    pass


def block_kernel(names, chunk_rows, *refs):
    (ids_h, fine_gain_h, coarse_gain_h, ffn_gain_h, emb_h, fq_h, fk_h, fv_h, fo_h, ws_h,
     cq_h, ck_h, cv_h, co_h, up_h, down_h, lift_h, out_ref) = refs[:18]
    s = Names()
    for name, ref in zip(names, refs[18:]):
        setattr(s, name, ref)
    count, width = out_ref.shape
    full = 4 * width
    heads = width // HEAD_DIM
    chunks = count // chunk_rows
    group = chunk_rows // SHORTEN
    rows = count // SHORTEN
    frame = LEAD + WINDOW + count
    span = WINDOW + chunk_rows
    lanes = width // 128
    pair = width // 2

    places = lax.axis_size("seq")
    place = lax.axis_index("seq")
    levels = places // 2
    side = place % 2
    level = place // 2
    cross = place + 1 - 2 * side
    me = lax.axis_index("head")
    sibling = me + 1 - 2 * (me % 2)
    across = (me + 2) % 4
    diagonal = (sibling + 2) % 4

    barrier = pltpu.get_barrier_semaphore()
    for device in (sibling, across, diagonal):
        pl.semaphore_signal(barrier, inc=1, device_id={"head": device}, device_id_type=MESH)

    def greet(step, state):
        pl.semaphore_signal(
            barrier, inc=1, device_id={"seq": (place + step) % places}, device_id_type=MESH
        )
        return state

    lax.fori_loop(1, places, greet, 0)

    own_columns = aligned(me * width, width, width)
    own_ids = s.ids.at[:, pl.ds(LEAD + WINDOW, count)]
    loads = {
        name: pltpu.make_async_copy(source, target, s.load_sem.at[index])
        for index, (name, source, target) in enumerate((
            ("ids", ids_h, own_ids), ("emb", emb_h, s.emb), ("fine_gain", fine_gain_h, s.fine_gain),
            ("fk", fk_h, s.fk), ("fv", fv_h, s.fv), ("fq", fq_h, s.fq),
            ("coarse_gain", coarse_gain_h, s.coarse_gain), ("ffn_gain", ffn_gain_h, s.ffn_gain),
            ("cols", fo_h.at[:, own_columns], s.cols.at[pl.ds(0, width), :]),
            ("ws", ws_h, s.ws), ("cq", cq_h, s.cq), ("ck", ck_h, s.ck), ("cv", cv_h, s.cv), ("co", co_h, s.co),
            ("up", up_h, s.up), ("down", down_h, s.down),
            *((f"lift{b}", lift_h.at[:, :, pl.ds(b * 128, 128)], s.raw.at[b]) for b in range(lanes)),
        ))
    }
    lift_names = tuple(f"lift{block}" for block in range(lanes))

    def start_loads(*names):
        for name in names:
            loads[name].start()

    start_loads("ids", "emb", "fine_gain", "fk", "fv", "fq")

    @pl.when(place < 1)
    def _():
        s.ids[:, LEAD : LEAD + WINDOW] = jnp.zeros((1, WINDOW), jnp.int32)

    @pl.when(place < 2)
    def _():
        s.ids[:, :LEAD] = jnp.zeros((1, LEAD), jnp.int32)

    def clear(index, state):
        chunk = index // (places - 2)
        blank = index % (places - 2)

        @pl.when(blank + 2 >= 2 * level + 2)
        def _():
            at = aligned((chunk * places + blank + 2) * group, group, group)
            s.pairs[at, :] = jnp.zeros((group, width), jnp.bfloat16)

        return state

    lax.fori_loop(0, chunks * (places - 2), clear, 0)

    column = lax.broadcasted_iota(jnp.int32, (HALF, 128), 0)
    lane = lax.broadcasted_iota(jnp.int32, (HALF, 128), 1)
    period = periods(column)
    small = phase(lane, period)
    base = (place - 1) * count - LEAD
    large = phase(base + 128 * lane, period)
    cos_b, sin_b, cos_a, sin_a = jnp.cos(small), jnp.sin(small), jnp.cos(large), jnp.sin(large)
    for block in range(frame // 128):
        at = slice(block * 128, block * 128 + 128)
        cos_k, sin_k = cos_a[:, block : block + 1], sin_a[:, block : block + 1]
        s.cos_t[:, at] = cos_b * cos_k - sin_b * sin_k
        s.sin_t[:, at] = sin_b * cos_k + cos_b * sin_k

    lane_f = lax.broadcasted_iota(jnp.int32, (rows, 128), 1) % HEAD_DIM
    period_f = periods(lane_f % HALF)
    angle_f = phase(place * rows + lax.broadcasted_iota(jnp.int32, (rows, 128), 0), period_f)
    cos_f = jnp.cos(angle_f)
    sin_f = jnp.where(lane_f < HALF, -jnp.sin(angle_f), jnp.sin(angle_f))
    for block in range(lanes):
        s.coarse_cos[:, block * 128 : block * 128 + 128] = cos_f
        s.coarse_sin[:, block * 128 : block * 128 + 128] = sin_f

    pl.semaphore_wait(barrier, places + 2)

    def id_copy(steps):
        if steps == 1:
            target = s.ids.at[:, pl.ds(LEAD, WINDOW)]
            source = ids_h
        else:
            target = s.ids.at[:, pl.ds(0, LEAD)]
            source = ids_h.at[:, pl.ds(count - LEAD, LEAD)]
        device = (place + steps) % places
        return remote(source, target, s.id_send.at[steps - 1], s.id_recv.at[steps - 1], {"seq": device})

    for steps in (1, 2):
        @pl.when(place + steps < places)
        def _():
            id_copy(steps).start()

    def column_copy(flip, device):
        return remote(
            fo_h.at[:, aligned(device * width, width, width)], s.cols.at[pl.ds(flip * width, width), :],
            s.col_send.at[flip], s.col_recv.at[flip], {"head": device},
        )

    column_copies = [column_copy(flip, device) for flip, device in ((1, sibling), (2, across), (3, diagonal))]
    for copy in column_copies:
        copy.start()

    loads["emb"].wait()
    loads["fine_gain"].wait()
    level_in = normed(s.emb[...].astype(jnp.float32), s.fine_gain[...])

    def split(values):
        high = values.astype(jnp.bfloat16)
        return high, (values - high.astype(jnp.float32)).astype(jnp.bfloat16)

    loads["fk"].wait()
    s.tabs[0], s.tabs[1] = split(dot(level_in, s.fk[...]).T)
    loads["fv"].wait()
    s.tabs[2] = dot(level_in, s.fv[...]).T.astype(jnp.bfloat16)
    loads["fq"].wait()
    s.tabs[3], s.tabs[4] = split(dot(level_in, s.fq[...]).T)
    s.tabs[5] = s.emb[:, own_columns]
    loads["ids"].wait()
    start_loads("cols", "ws", "coarse_gain", "ffn_gain", "cq", "ck", "cv")

    def turned(joined, at):
        cosine, sine = s.cos_t[:, at], s.sin_t[:, at]
        pieces = []
        for head in range(heads):
            low = joined[head * HEAD_DIM : head * HEAD_DIM + HALF]
            high = joined[head * HEAD_DIM + HALF : (head + 1) * HEAD_DIM]
            pieces += [low * cosine - high * sine, high * cosine + low * sine]
        return jnp.concatenate(pieces, axis=0)

    def hot_rows(at, size):
        levels_at = lax.broadcasted_iota(jnp.int32, (256, size), 0)
        return jnp.where(levels_at == s.ids[:, at], 1.0, 0.0).astype(jnp.bfloat16)

    def key_rows(begin, size):
        at = aligned(begin, size, 128)
        hot = hot_rows(at, size)
        s.keys[at, :] = turned(dot(s.tabs[0], hot) + dot(s.tabs[1], hot), at).T.astype(jnp.bfloat16)
        s.values[:, at] = dot(s.tabs[2], hot).astype(jnp.bfloat16)

    def query_rows(begin, size):
        at = aligned(begin, size, 128)
        to = aligned(begin - WINDOW, size, 128)
        hot = hot_rows(at, size)
        s.query[:, to] = turned(dot(s.tabs[3], hot) + dot(s.tabs[4], hot), at).astype(jnp.bfloat16)
        s.start[to, :] = dot_tn(hot, s.tabs[5]).astype(jnp.bfloat16)

    own_block = min(512, count)

    def own_rows(index, state):
        key_rows(LEAD + WINDOW + index * own_block, own_block)
        query_rows(LEAD + WINDOW + index * own_block, own_block)
        return state

    def prior_rows(index, state):
        key_rows(index * 384, 384)
        return state

    lax.fori_loop(0, count // own_block, own_rows, 0)
    for steps in (1, 2):
        @pl.when(place >= steps)
        def _():
            id_copy(steps).wait_recv()

    lax.fori_loop(0, (LEAD + WINDOW) // 384, prior_rows, 0)
    query_rows(WINDOW, LEAD)

    def weigh(scores):
        top = scores[0]
        for piece in scores[1:]:
            top = jnp.maximum(top, piece)
        top = jnp.max(top, axis=0, keepdims=True)
        weights = [jnp.exp2((piece - top) * EXP2_SCALE) for piece in scores]
        total = weights[0]
        for piece in weights[1:]:
            total = total + piece
        total = jnp.sum(total, axis=0, keepdims=True)
        return jnp.concatenate([piece.astype(jnp.bfloat16) for piece in weights], axis=0), total

    def mixed_rows(chunk):
        return aligned(CARRY + chunk * chunk_rows, chunk_rows, CARRY)

    def mix_copies(chunk, at):
        def slot(which):
            return s.others.at[at, pl.ds((which - 1) * width, width)]

        def copy(kind, source, target, device):
            return remote(source, target, s.mix_send.at[kind, chunk], s.mix_recv.at[kind, chunk], {"head": device})

        return (
            copy(0, s.mixed.at[at, :], slot(2), across),
            copy(1, s.mixed.at[at, :], slot(1), sibling),
            copy(2, slot(2), slot(3), sibling),
        )

    carry_at = pl.ds(0, CARRY)
    carry_copies = mix_copies(chunks, carry_at)

    start_loads("co", "up", "down", *lift_names)

    def attend_carry():
        lane_slot = lax.broadcasted_iota(jnp.int32, (HEAD_DIM, LEAD), 1) // 32
        packed = []
        for head in range(heads):
            rolled = pltpu.roll(s.query[head * HEAD_DIM : (head + 1) * HEAD_DIM, :LEAD].astype(jnp.float32), (32 * head + 32) % LEAD, 1)
            packed.append(jnp.where(lane_slot == head, rolled, 0.0))
        packed = jnp.concatenate(packed, axis=0).astype(jnp.bfloat16)
        scores = dot(s.keys[: LEAD + WINDOW, :], packed)
        key = lax.broadcasted_iota(jnp.int32, scores.shape, 0)
        last = lax.broadcasted_iota(jnp.int32, scores.shape, 1) % 32 + (LEAD + WINDOW - 32)
        floor = jnp.where(place < 2, LEAD, 0)
        allowed = (key > last - WINDOW) & (key <= last) & (key >= floor)
        weights, total = weigh([jnp.where(allowed, scores, masked_low)])
        out = dot(s.values[:, : LEAD + WINDOW], weights) / total
        unpacked = [
            pltpu.roll(out[head * HEAD_DIM : (head + 1) * HEAD_DIM, :], (LEAD - 32 * head) % LEAD, 1) for head in range(heads)
        ]
        s.mixed[carry_at, :] = jnp.concatenate(unpacked, axis=0).T[32 - CARRY : 32, :].astype(jnp.bfloat16)
        carry_copies[0].start()
        carry_copies[1].start()

    part_keys = 3 * chunk_rows if span % (3 * chunk_rows) == 0 else chunk_rows
    row = lax.broadcasted_iota(jnp.int32, (chunk_rows, chunk_rows), 0)
    column = lax.broadcasted_iota(jnp.int32, (chunk_rows, chunk_rows), 1)

    def each_head(allowed, piece):
        return jnp.concatenate(
            [
                jnp.where(allowed, piece[:, head * chunk_rows : (head + 1) * chunk_rows], masked_low)
                for head in range(piece.shape[1] // chunk_rows)
            ],
            axis=1,
        )

    sets = [tuple(range(first, min(first + SET, heads))) for first in range(0, heads, SET)]

    def by_eights(values):
        return values.reshape(values.shape[0] // 8, 8, values.shape[1])

    row_head = lax.broadcasted_iota(jnp.int32, (width, chunk_rows), 0) // HEAD_DIM

    def attend_chunk(chunk):
        begin = chunk * chunk_rows
        floor = jnp.where(place == 0, WINDOW - begin, 0)
        key_at = aligned(LEAD + begin, span, 128)
        query = s.query[:, aligned(LEAD + begin, chunk_rows, chunk_rows)]
        tops, totals = [], []
        for side_heads in sets:
            lanes_of = slice(side_heads[0] * chunk_rows, (side_heads[-1] + 1) * chunk_rows)
            stacked = jnp.concatenate(
                [jnp.where(row_head == head, query, jnp.zeros_like(query)) for head in side_heads], axis=1
            )
            top = None
            for part in range(0, span, part_keys):
                scores = dot(s.keys[aligned(LEAD + begin + part, part_keys, 128), :], stacked)
                for at in range(part, part + part_keys, chunk_rows):
                    piece = scores[at - part : at - part + chunk_rows, :]
                    if at == span - chunk_rows:
                        piece = each_head(row <= column, piece)
                    else:
                        piece = piece + jnp.where(at < floor, masked_low, 0.0)
                        if at == 0:
                            piece = each_head(row > column, piece)
                    s.scores[at : at + chunk_rows, lanes_of] = piece
                    peak = jnp.max(by_eights(piece), axis=0)
                    top = peak if top is None else jnp.maximum(top, peak)
            tops.append(jnp.max(top, axis=0, keepdims=True))
        outs = []
        for which, side_heads in enumerate(sets):
            lanes_of = slice(side_heads[0] * chunk_rows, (side_heads[-1] + 1) * chunk_rows)
            total = jnp.zeros((8, len(side_heads) * chunk_rows), jnp.float32)
            for at in range(0, span, chunk_rows):
                weights = jnp.exp2((s.scores[at : at + chunk_rows, lanes_of] - tops[which]) * EXP2_SCALE)
                total = total + jnp.sum(by_eights(weights), axis=0)
                s.weights[at : at + chunk_rows, lanes_of] = weights.astype(jnp.bfloat16)
            total = jnp.sum(total, axis=0, keepdims=True)
            for index, head in enumerate(side_heads):
                of = slice(head * chunk_rows, (head + 1) * chunk_rows)
                share = dot(s.values[head * HEAD_DIM : (head + 1) * HEAD_DIM, key_at], s.weights[:, of])
                outs.append(share / total[:, index * chunk_rows : (index + 1) * chunk_rows])
        at = mixed_rows(chunk)
        s.mixed[at, :] = jnp.concatenate(outs, axis=0).T.astype(jnp.bfloat16)
        copies = mix_copies(chunk, at)
        copies[0].start()
        copies[1].start()

    def fine_rows(at, start_at):
        merged = dot(s.mixed[at, :], s.cols[:width, :]) + dot(s.others[at, :], s.cols[width:, :])
        value = (s.start[start_at, :].astype(jnp.float32) + merged).astype(jnp.bfloat16).astype(jnp.float32)
        for block in range(lanes):
            s.stream[block, at, :] = value[:, block * 128 : block * 128 + 128]

    peers = (me, sibling, across)
    buffers = (s.send_a, s.recv_a, s.send_b, s.recv_b, s.final)
    short_sum = HeadSum(0, peers, s.part, s.short, buffers, s.sum_send, s.sum_recv)

    def short_rows(chunk):
        return aligned(chunk * group, group, group)

    def relay_chunk(chunk):
        @pl.when(chunk == 0)
        def _():
            carry_copies[0].wait_recv()
            carry_copies[2].start()

        copies = mix_copies(chunk, mixed_rows(chunk))
        copies[0].wait_recv()
        copies[2].start()

    def finish_chunk(chunk):
        @pl.when(chunk == 0)
        def _():
            for copy in column_copies:
                copy.wait_recv()
            loads["cols"].wait()
            loads["ws"].wait()
            carry_copies[1].wait_recv()
            carry_copies[2].wait_recv()
            fine_rows(carry_at, pl.ds(LEAD - CARRY, CARRY))

            @pl.when(place == 0)
            def _():
                s.stream[:, 0:CARRY, :] = jnp.zeros((lanes, CARRY, 128), jnp.float32)

        at = mixed_rows(chunk)
        copies = mix_copies(chunk, at)
        copies[1].wait_recv()
        copies[2].wait_recv()
        fine_rows(at, aligned(LEAD + chunk * chunk_rows, chunk_rows, chunk_rows))
        total = jnp.zeros((group, full), jnp.float32)
        for offset in range(SHORTEN):
            begin = CARRY - (SHORTEN - 1) + offset + chunk * chunk_rows
            member = jnp.concatenate(
                [s.stream[block, pl.ds(begin, group, stride=SHORTEN), :] for block in range(lanes)], axis=1
            )
            total = total + dot(member.astype(jnp.bfloat16), s.ws[offset])
        s.part[short_rows(chunk), :] = total
        short_sum.begin(chunk, short_rows(chunk))

    def pair_rows(chunk, source):
        return aligned((chunk * places + source) * group, group, group)

    def pair_copy(chunk, target):
        at = pair_rows(chunk, place)
        return remote(
            s.pair_out.at[target % 2, short_rows(chunk), :], s.pairs.at[at, :],
            s.pair_send.at[target, chunk], s.pair_recv.at[place, chunk], {"seq": target},
        )

    def pair_arrival(chunk, source):
        at = pair_rows(chunk, source)
        return remote(
            s.pairs.at[at, :], s.pairs.at[at, :], s.pair_send.at[source, chunk], s.pair_recv.at[source, chunk],
            {"seq": cross},
        )

    def query_copy(chunk):
        at = short_rows(chunk)
        return remote(
            s.query_out.at[1 - side, at, :], s.queries.at[aligned(side * rows + chunk * group, group, group), :],
            s.query_send.at[chunk], s.query_recv.at[chunk], {"seq": cross},
        )

    def for_targets(action):
        def one(index, state):
            target = places - 1 - index

            @pl.when(target != place)
            def _():
                action(target)

            return state

        lax.fori_loop(0, places - 2 * level, one, 0)

    def project_chunk(chunk):
        @pl.when(chunk == 0)
        def _():
            for name in ("coarse_gain", "cq", "ck", "cv"):
                loads[name].wait()

        at = short_rows(chunk)
        short_sum.end(chunk, at)
        coarse_in = normed(s.short[at, :].astype(jnp.float32), s.coarse_gain[...])
        cosine, sine = s.coarse_cos[at, :], s.coarse_sin[at, :]
        is_low = lax.broadcasted_iota(jnp.int32, (group, width), 1) % HEAD_DIM < HALF

        def rotated(values):
            other = jnp.where(is_low, pltpu.roll(values, width - HALF, 1), pltpu.roll(values, HALF, 1))
            return (values * cosine + other * sine).astype(jnp.bfloat16)

        key = rotated(dot(coarse_in, s.ck[...]))
        value = dot(coarse_in, s.cv[...]).astype(jnp.bfloat16)
        for half in range(2):
            s.pair_out[half, at, :pair] = key[:, half * pair : half * pair + pair]
            s.pair_out[half, at, pair:] = value[:, half * pair : half * pair + pair]
        for_targets(lambda target: pair_copy(chunk, target).start())
        query = rotated(dot(coarse_in, s.cq[...]))
        for half in range(2):
            s.query_out[half, at, :] = query[:, half * pair : half * pair + pair]
        query_copy(chunk).start()
        s.pairs[pair_rows(chunk, place), :] = s.pair_out[side, at, :]
        s.queries[aligned(side * rows + chunk * group, group, group), :] = s.query_out[side, at, :]

    def total_chunk(chunk):
        short_sum.total(chunk, short_rows(chunk))

    def middle_chunk(chunk):
        short_sum.middle(chunk, short_rows(chunk))

    ahead = ((RELAY, relay_chunk), (TOTAL, total_chunk))
    behind = ((PROJECT, project_chunk), (MIDDLE, middle_chunk), (FINISH, finish_chunk))

    def one_step(step, state):
        def run(stages):
            for lag, action in stages:
                @pl.when(step >= lag)
                def _():
                    action(step - lag)

        run(ahead)
        attend_chunk(step)

        @pl.when(step == 0)
        def _():
            attend_carry()

        run(behind)
        return state

    lax.fori_loop(0, chunks, one_step, 0)

    left = {action: max(0, chunks - lag) for lag, action in ahead + behind}

    def rest(action, upto):
        for chunk in range(left[action], upto):
            action(chunk)
        left[action] = max(left[action], upto)

    for action, back in (
        (relay_chunk, 1), (total_chunk, 4), (middle_chunk, 2), (project_chunk, 4), (finish_chunk, 1), (total_chunk, 3),
        (relay_chunk, 0), (middle_chunk, 1), (project_chunk, 3), (finish_chunk, 0), (total_chunk, 2),
        (middle_chunk, 0), (project_chunk, 2), (total_chunk, 1), (project_chunk, 1),
        (total_chunk, 0), (project_chunk, 0),
    ):
        rest(action, chunks - back)

    def wait_chunk(chunk):
        def one(source, state):
            pair_arrival(chunk, source).wait_recv()
            return state

        lax.fori_loop(0, 2 * level, one, 0)

    def wait_queries(chunk, state):
        query_copy(chunk).wait_recv()
        pair_arrival(chunk, cross).wait_recv()
        return state

    lax.fori_loop(0, chunks, wait_queries, 0)

    per_chunk = places * group
    pair_lane = lax.broadcasted_iota(jnp.int32, (2 * rows, pair), 1) // HEAD_DIM
    queries = s.queries[...]
    masked = [jnp.where(pair_lane == head, queries, jnp.zeros_like(queries)) for head in range(pair // HEAD_DIM)]

    def absorb(block, mask, first):
        keys, values = block[:, :pair], block[:, pair:]
        values_t = values.astype(jnp.float32).T.astype(jnp.bfloat16)
        for head in range(pair // HEAD_DIM):
            scores = dot_nt(keys, masked[head])
            pieces = [mask(begin, scores[begin : begin + group, :]) for begin in range(0, scores.shape[0], group)]
            peak = pieces[0]
            for piece in pieces[1:]:
                peak = jnp.maximum(peak, piece)
            fresh = jnp.max(peak, axis=0, keepdims=True)
            if not first:
                fresh = jnp.maximum(s.top[head], fresh)
            weights = [jnp.exp2((piece - fresh) * EXP2_SCALE) for piece in pieces]
            total = weights[0]
            for piece in weights[1:]:
                total = total + piece
            total = jnp.sum(total, axis=0, keepdims=True)
            of = slice(head * HEAD_DIM, (head + 1) * HEAD_DIM)
            rounded = jnp.concatenate([piece.astype(jnp.bfloat16) for piece in weights], axis=0)
            share = dot(values_t[of, :], rounded)
            if not first:
                factor = jnp.exp2((s.top[head] - fresh) * EXP2_SCALE)
                total = total + s.norm[head] * factor
                share = share + s.acc[of, :] * factor
            s.top[head] = fresh
            s.norm[head] = total
            s.acc[of, :] = share

    ahead_of = lax.broadcasted_iota(jnp.int32, (group, 2 * rows), 1) - lax.broadcasted_iota(
        jnp.int32, (group, 2 * rows), 0
    )

    def own_mask(begin, piece):
        index = begin // group
        return jnp.where(ahead_of >= (index % 2) * rows + (index // 2) * group, piece, masked_low)

    own_level = jnp.concatenate(
        [s.pairs[aligned((chunk * places + 2 * level) * group, 2 * group, 2 * group), :] for chunk in range(chunks)], axis=0
    )
    absorb(own_level, own_mask, True)

    def key_step(step, state):
        if per_chunk <= STEP_KEYS:
            for inner in range(STEP_KEYS // per_chunk):
                wait_chunk(step * (STEP_KEYS // per_chunk) + inner)
        else:
            ratio = per_chunk // STEP_KEYS

            @pl.when(step % ratio == 0)
            def _():
                wait_chunk(step // ratio)

        def level_mask(begin, piece):
            source = (step * STEP_KEYS + begin) % per_chunk // group
            return piece + jnp.where(source < 2 * level, 0.0, masked_low)

        absorb(s.pairs[aligned(step * STEP_KEYS, STEP_KEYS, STEP_KEYS), :], level_mask, False)
        return state

    lax.fori_loop(0, places * rows // STEP_KEYS, key_step, 0)

    size = rows // PIECES
    at = [pl.ds(piece * size, size) for piece in range(PIECES)]
    wide = [pl.ds(2 * half * size, 2 * size) for half in range(PIECES // 2)]

    def turn_copy(piece):
        return remote(
            s.turn.at[at[piece], :], s.heads_in.at[at[piece], aligned(side * pair, pair, pair)],
            s.turn_send.at[piece], s.turn_recv.at[piece], {"seq": cross},
        )

    def mixed_of(at):
        shares = [
            s.acc[head * HEAD_DIM : (head + 1) * HEAD_DIM, at] / s.norm[head, :, at] for head in range(pair // HEAD_DIM)
        ]
        return jnp.concatenate(shares, axis=0).T.astype(jnp.bfloat16)

    s.turn[...] = mixed_of(aligned((1 - side) * rows, rows, rows))
    for piece in range(PIECES):
        turn_copy(piece).start()
    s.heads_in[:, aligned(side * pair, pair, pair)] = mixed_of(aligned(side * rows, rows, rows))

    for name in lift_names:
        loads[name].wait()
    part_rows = count // SHORTEN
    for block in range(lanes):
        for begin in range(0, full, part_rows):
            flat = s.raw.at[block, pl.ds(begin, part_rows)].reshape(part_rows * SHORTEN, 128)
            s.spread[block] = flat[...].astype(jnp.float32)
            for member in range(SHORTEN):
                s.lift[begin : begin + part_rows, member * width + block * 128 : member * width + block * 128 + 128] = (
                    s.spread[block, pl.ds(member, part_rows, stride=SHORTEN), :].astype(jnp.bfloat16)
                )

    loads["co"].wait()

    out_sum = HeadSum(1, peers, s.part, s.summed, buffers, s.sum_send, s.sum_recv)
    ffn_sum = HeadSum(2, peers, s.part_b, s.second, buffers, s.sum_send, s.sum_recv)

    for piece in range(PIECES):
        turn_copy(piece).wait_recv()
        s.part[at[piece], :] = dot(s.heads_in[at[piece], :], s.co[...])
        out_sum.begin(piece, at[piece])
    for name in ("ffn_gain", "up", "down"):
        loads[name].wait()
    for piece in range(PIECES):
        out_sum.middle(piece, at[piece])
    for steps in (1, 2):
        @pl.when(place + steps < places)
        def _():
            id_copy(steps).wait_send()

    for copy in column_copies:
        copy.wait_send()
    for copy in carry_copies:
        copy.wait_send()

    def drain(chunk, state):
        for copy in mix_copies(chunk, mixed_rows(chunk)):
            copy.wait_send()
        short_sum.drain(chunk, short_rows(chunk))
        for_targets(lambda target: pair_copy(chunk, target).wait_send())
        query_copy(chunk).wait_send()
        return state

    lax.fori_loop(0, chunks, drain, 0)

    def feed(piece):
        out_sum.end(piece, at[piece])
        out_sum.end(piece + 1, at[piece + 1])
        half = wide[piece // 2]
        value = s.short[half, :].astype(jnp.float32) + s.summed[half, :].astype(jnp.float32)
        s.first[half, :] = value
        inner = jax.nn.gelu(dot(normed(value, s.ffn_gain[...]), s.up[...])).astype(jnp.bfloat16)
        s.part_b[half, :] = dot(inner, s.down[...])
        ffn_sum.begin(piece, at[piece])
        ffn_sum.begin(piece + 1, at[piece + 1])

    def raise_rows(piece):
        ffn_sum.end(piece, at[piece])
        for member in range(SHORTEN):
            lifted = dot(s.second[at[piece], :], s.lift[:, member * width : (member + 1) * width])
            for block in range(lanes):
                s.spread[block, pl.ds(SHORTEN * size * piece + member, size, stride=SHORTEN), :] = lifted[
                    :, block * 128 : block * 128 + 128
                ]
        for block in range(lanes):
            to = slice(SHORTEN * size * piece, SHORTEN * size * (piece + 1))
            base_at = slice(CARRY + SHORTEN * size * piece, CARRY + SHORTEN * size * (piece + 1))
            out_ref[to, block * 128 : block * 128 + 128] = (
                s.stream[block, base_at, :] + s.spread[block, to, :]
            ).astype(jnp.bfloat16)

    def out_total(piece):
        out_sum.total(piece, at[piece])

    def ffn_middle(piece):
        ffn_sum.middle(piece, at[piece])

    def ffn_total(piece):
        ffn_sum.total(piece, at[piece], s.first)

    for action, piece in (
        (out_total, 0), (out_total, 1), (feed, 0), (out_total, 2), (ffn_middle, 0), (out_total, 3), (ffn_middle, 1),
        (feed, 2), (ffn_middle, 2), (ffn_middle, 3), (ffn_total, 0), (ffn_total, 1), (raise_rows, 0), (ffn_total, 2),
        (raise_rows, 1), (ffn_total, 3), (raise_rows, 2), (raise_rows, 3),
    ):
        action(piece)

    for piece in range(PIECES):
        turn_copy(piece).wait_send()
    for piece in range(PIECES):
        out_sum.drain(piece, at[piece])
        ffn_sum.drain(piece, at[piece])


def local(
    token_ids,
    embedding,
    fine_norm,
    fine_query,
    fine_key,
    fine_value,
    fine_output,
    shorten_weight,
    coarse_norm,
    coarse_query,
    coarse_key,
    coarse_value,
    coarse_output,
    ffn_norm,
    ffn_up,
    ffn_down,
    upsample_weight,
):
    count = token_ids.shape[0]
    width = fine_query.shape[1]
    chunk_rows = min(128, count)
    chunks = count // chunk_rows
    scratch = scratch_list(count, width, chunks, lax.axis_size("seq"))
    names = [name for name, _ in scratch]

    def kernel(*refs):
        block_kernel(names, chunk_rows, *refs)

    return pl.pallas_call(
        kernel,
        out_shape=jax.ShapeDtypeStruct((count, width), jnp.bfloat16),
        in_specs=[HBM_SPEC] * 17,
        out_specs=VMEM_SPEC,
        scratch_shapes=[shape for _, shape in scratch],
        compiler_params=pltpu.CompilerParams(
            collective_id=1, has_side_effects=True, vmem_limit_bytes=46 * 2**20
        ),
        name="block_kernel",
    )(
        *(
            pltpu.with_memory_space_constraint(array, pltpu.HBM)
            for array in (
                token_ids.reshape(1, count), fine_norm.reshape(1, D), coarse_norm.reshape(1, D), ffn_norm.reshape(1, D),
                embedding, fine_query, fine_key, fine_value, fine_output, shorten_weight, coarse_query, coarse_key,
                coarse_value, coarse_output, ffn_up, ffn_down, upsample_weight,
            )
        ),
    )


def solution(mesh):
    return jax.shard_map(
        local,
        mesh=mesh,
        in_specs=(
            P("seq"),
            P(),
            P(),
            P(None, "head"),
            P(None, "head"),
            P(None, "head"),
            P("head", None),
            P(None, "head", None),
            P(),
            P(None, "head"),
            P(None, "head"),
            P(None, "head"),
            P("head", None),
            P(),
            P(None, "head"),
            P("head", None),
            P(None, None, "head"),
        ),
        out_specs=P("seq", "head"),
        check_vma=False,
    )
```
